32 devices in a mesh: lat: 8 (over y, x, core), lon: 4 (over z).
Axes of the slice: x: 2, y: 2, z: 4, core: 2. Of those that a mesh axis runs over, the one named last changes fastest.
Arguments:
- noise: float32 [4, 8, 128, 1024], P(None, None, 'lat', 'lon'), may hold values from -6 to 6
- diff_lat: float32 [8, 128, 1024], P(None, 'lat', 'lon'), may hold values from 0.05 to 0.24
- diff_lon: float32 [8, 128, 1024], P(None, 'lat', 'lon'), may hold values from 0.05 to 0.24
- shear: float32 [8, 128, 1024], P(None, 'lat', 'lon'), may hold values from -0.9 to 0.9
- sea_mask: int32 [8, 128, 1024], P(None, 'lat', 'lon'), may hold values from 0 to 1, as said below
Outputs:
- normalized: float32 [4, 8, 128, 1024], P(None, None, 'lat', 'lon')
- mean_var: float32 [], replicated
The draws below stay inside these ranges and needn't reach their ends.
Inputs may be any that keep to these rules, and one draw needn't show every extreme that they name: `sea_mask`: every block of 16 latitude rows by 256 longitude columns has its own chance for each cell to be wet, from a quarter to one; the block of the first rows and first columns is wet at every level.
All inputs are finite; a program needn't handle non-finite values.
Results may differ from the reference program's by a relative error of at most 0.0003.
Values sent between devices are 32-bit elements; how exact they have to be, the bound alone decides.
No kernel may reach another device: no remote copies, remote signals or barrier semaphores. Data moves between devices by JAX's collectives and lax.ppermute only.
A program may use at most 64 MiB of HBM per device.

```python
import jax
import jax.numpy as jnp
from jax import lax

SAMPLES = 4
LEVELS = 8
CX = 16
CY = 256
ITERS = 4
NX = 128
NY = 1024


def draw_sea_mask(key, part):
    tile_key = jax.random.fold_in(key, 11)
    cell_key = jax.random.fold_in(key, 23)
    tile_share = jax.random.randint(tile_key, (NX // CX, NY // CY), 1, 5)
    tile_share = tile_share.at[0, 0].set(4)
    spread_share = jnp.repeat(jnp.repeat(tile_share, CX, axis=0), CY, axis=1)
    cells = jax.random.randint(cell_key, (LEVELS, NX, NY), 0, 4)
    return (cells < spread_share[None, :, :]).astype(jnp.int32)


def shard_levels(rng, shape, split, low, high):
    gain, own = 1.0, jax.random.fold_in(rng, 6)
    for position, shards_of in split:
        heights = jnp.exp(jax.random.uniform(jax.random.fold_in(own, position), (shards_of,), jnp.float32, low / len(split), high / len(split)))
        gain = gain * jnp.repeat(heights, shape[position] // shards_of).reshape([-1 if axis == position else 1 for axis in range(len(shape))])
    return gain


def bell_draw(own_key, dims, scale, bound, cuts=(), kind=jnp.bfloat16):
    drawn = scale * jax.random.normal(own_key, dims, jnp.float32)
    if cuts:
        drawn = drawn * shard_levels(own_key, dims, cuts, -0.22, 0.18)
    return jnp.clip(drawn, -bound, bound).astype(kind)


def setup_inputs(seed: int = 0) -> dict:
    seeds = jax.random.split(jax.random.key(seed), 6)
    return {
        "noise": bell_draw(seeds[0], (SAMPLES, LEVELS, NX, NY), 1.0, 6.0, ((2, 8), (3, 4)), jnp.float32),
        "diff_lat": jnp.clip(0.05 + 0.19 * jax.random.uniform(seeds[1], (LEVELS, NX, NY), jnp.float32) ** shard_levels(seeds[1], (LEVELS, NX, NY), ((1, 8), (2, 4)), -0.2, 0.2), 0.05, 0.24),
        "diff_lon": jnp.clip(0.05 + 0.19 * jax.random.uniform(seeds[2], (LEVELS, NX, NY), jnp.float32) ** shard_levels(seeds[2], (LEVELS, NX, NY), ((1, 8), (2, 4)), -0.2, 0.2), 0.05, 0.24),
        "shear": jnp.clip(jax.random.uniform(seeds[3], (LEVELS, NX, NY), jnp.float32, -0.9, 0.9) * shard_levels(seeds[3], (LEVELS, NX, NY), ((1, 8), (2, 4)), -0.4, 0.0), -0.9, 0.9),
        "sea_mask": draw_sea_mask(jax.random.fold_in(seeds[5], 71), 0),
    }


def offset_weights(diff_lat, diff_lon, shear):
    cross = shear * jnp.sqrt(diff_lat * diff_lon)
    return [((0, 0), 1.0 - 2.0 * (diff_lat + diff_lon)), ((1, 0), diff_lat), ((-1, 0), diff_lat), ((0, 1), diff_lon), ((0, -1), diff_lon), ((1, 1), 0.5 * cross), ((-1, -1), 0.5 * cross), ((1, -1), -0.5 * cross), ((-1, 1), -0.5 * cross)]

def move_rows(field, shift_lat, shift_lon):
    moved = jnp.roll(field, shift_lon, axis=-1)
    zero_row = jnp.zeros_like(moved[:, :1, :])
    if shift_lat == 1:
        moved = jnp.concatenate([zero_row, moved[:, :-1, :]], axis=1)
    elif shift_lat == -1:
        moved = jnp.concatenate([moved[:, 1:, :], zero_row], axis=1)
    return moved

def reference(noise, diff_lat, diff_lon, shear, sea_mask):
    wet = sea_mask.astype(jnp.float32)
    table = offset_weights(diff_lat, diff_lon, shear)

    def diffuse(field):
        for step in range(ITERS):
            masked = wet * field
            total = jnp.zeros_like(field)
            for offset, weight in table:
                total = total + move_rows(weight * masked, offset[0], offset[1])
            field = total
        return field
    diffused = lax.map(diffuse, noise)
    var = lax.optimization_barrier(jnp.sum(diffused * diffused, axis=0)) / SAMPLES
    mean_var = jnp.sum(wet * var) / jnp.sum(wet)
    safe = jnp.where(wet > 0, var, 1.0)
    factor = wet * jnp.sqrt(mean_var / (safe + 1e-06))
    return (diffused * factor, mean_var)
```

```python
import functools

import jax
import jax.numpy as jnp
from jax import lax
from jax.experimental import pallas as pl
from jax.experimental.pallas import tpu as pltpu
from jax.sharding import PartitionSpec as P

ITERS = 4
LANES = 128
SEG = 32
F32 = jnp.float32


def cell_weights(k11, k22, shear, mask):
    m = mask.astype(F32)
    return m * k11, m * k22, m * (0.5 * (shear * jnp.sqrt(k11 * k22)))


def centre_weight(wa, wb):
    return jnp.where(wa > 0, 1.0, 0.0) - 2.0 * (wa + wb)


def roll(x, shift):
    n = x.shape[-1]
    shift = shift % n
    return x if shift == 0 else pltpu.roll(x, shift, x.ndim - 1)


def lane_parts(shape):
    lane = lax.broadcasted_iota(jnp.int32, shape, 1)
    return lane, lane // SEG, lane % SEG


def stencil(rows, get_y, get_w, first, last, put):
    def products(r):
        y = get_y(r)
        w0, wa, wb, wc = get_w(r)
        return w0 * y, wa * y, wb * y, wc * y

    prev, here = products(first - 1), products(first)
    for r in range(first, last):
        after = products(r + 1)
        d, _, b, _ = here
        g = prev[3] - after[3]
        put(r, d + (prev[1] + after[1]) + roll(b + g, 1) + roll(b - g, -1))
        prev, here = here, after


def edge_kernel(n_ref, a_ref, b_ref, s_ref, m_ref, top_ref, bot_ref, n_to, a_to, b_to, s_to, m_to, sem):
    samples, levels, tiles = n_ref.shape[0], top_ref.shape[2], n_to.shape[0]
    rows = n_ref.shape[1] // levels
    copies = []
    for c in range(tiles):
        lanes = pl.ds(c * LANES, LANES)
        for k, (ref, to) in enumerate(((a_ref, a_to), (b_ref, b_to), (s_ref, s_to), (m_ref, m_to))):
            copies.append(pltpu.make_async_copy(ref.at[:, lanes], to.at[c], sem.at[c, k]))
        copies.append(pltpu.make_async_copy(n_ref.at[:, :, lanes], n_to.at[c], sem.at[c, 4]))
    for copy in copies:
        copy.start()
    for copy in copies:
        copy.wait()
    for i in range(ITERS):
        for out, r in ((top_ref, i), (bot_ref, rows - ITERS + i)):
            at = pl.ds(r, levels, stride=rows)
            for c in range(tiles):
                lanes = pl.ds(c * LANES, LANES)
                for s in range(samples):
                    out[i, s, :, lanes] = n_to[c, s, at]
                w = cell_weights(a_to[c, at], b_to[c, at], s_to[c, at], m_to[c, at])
                for k in range(3):
                    out[i, samples + k, :, lanes] = w[k]


def message(get, samples, parts):
    _, seg, l32 = parts
    acc = None
    for s in range(samples):
        v = jnp.where(l32 < SEG // 2, roll(get(s, 1), SEG * s + 4), roll(get(s, 0), SEG * s + 28))
        acc = v if acc is None else jnp.where(seg == s, v, acc)
    w = None
    for k in range(3):
        v = jnp.where(l32 < SEG // 2, roll(get(samples + k, 1), 4 * k + 8), roll(get(samples + k, 0), 24 - 4 * k))
        w = v if w is None else jnp.where((l32 // 4 == k + 1) | (l32 // 4 == 6 - k), v, w)
    w = replicate(w, seg)
    return jnp.where((l32 < 4) | (l32 >= 28), acc, w)


def replicate(v, seg):
    v = jnp.where(seg == 1, roll(v, SEG), v)
    return jnp.where(seg >= 2, roll(v, 2 * SEG), v)


def own_kernel(n_ref, a_ref, b_ref, s_ref, m_ref, y_ref, w_ref, msg_ref):
    rows, samples, levels, cols = y_ref.shape
    parts = lane_parts((levels, LANES))
    tiles = cols // LANES
    for r in range(rows):
        at = pl.ds(r, levels, stride=rows)
        edge = {}
        for c in range(tiles):
            lanes = pl.ds(c * LANES, LANES)
            vals = [n_ref[c, s, at] for s in range(samples)]
            for s in range(samples):
                y_ref[r, s, :, lanes] = vals[s]
            w = cell_weights(a_ref[c, at], b_ref[c, at], s_ref[c, at], m_ref[c, at])
            w_ref[r, 0, :, lanes] = centre_weight(w[0], w[1])
            for k in range(3):
                w_ref[r, 1 + k, :, lanes] = w[k]
            if c == 0:
                edge[0] = vals + list(w)
            if c == tiles - 1:
                edge[1] = vals + list(w)
        msg_ref[r] = message(lambda g, side: edge[side][g], samples, parts)


def join_kernel(own_ref, before_ref, after_ref, msg_ref):
    rows = own_ref.shape[0]
    samples, cols = before_ref.shape[1] - 3, before_ref.shape[3]
    parts = lane_parts(own_ref.shape[1:])
    msg_ref[ITERS : ITERS + rows] = own_ref[...]
    for i in range(ITERS):
        for ref, to in ((before_ref, i), (after_ref, ITERS + rows + i)):
            msg_ref[to] = message(
                lambda g, side: ref[i, g, :, pl.ds(side * (cols - LANES), LANES)], samples, parts
            )


def main_kernel(y_ref, w_ref, before_ref, after_ref, x_ref, sy_ref, sw_ref, wh_ref, p_ref, q_ref):
    rows, samples, levels, cols = y_ref.shape
    high = rows + 2 * ITERS
    _, seg, l32 = lane_parts((levels, LANES))

    def halo(r):
        return (before_ref, r) if r < ITERS else (after_ref, r - ITERS - rows)

    def own(r):
        return ITERS <= r < ITERS + rows

    for r in range(high):
        if not own(r):
            ref, i = halo(r)
            slot = r if r < ITERS else r - rows
            w = [ref[i, samples + k] for k in range(3)]
            wh_ref[slot, 0] = centre_weight(w[0], w[1])
            for k in range(3):
                wh_ref[slot, 1 + k] = w[k]

    def get_w(r):
        if own(r):
            return [w_ref[r - ITERS, k] for k in range(4)]
        return [wh_ref[r if r < ITERS else r - rows, k] for k in range(4)]

    left, right = pl.ds(0, LANES), pl.ds(cols - LANES, LANES)
    for r in range(high):
        acc = None
        for s in range(samples):
            ref, i = (y_ref, r - ITERS) if own(r) else halo(r)
            v = jnp.where(l32 < SEG // 2, roll(ref[i, s, :, left], SEG * s + 4), roll(ref[i, s, :, right], SEG * s + 28))
            acc = v if acc is None else jnp.where(seg == s, v, acc)
        sy_ref[r] = acc
        for k in range(3):
            ref, i, g = (w_ref, r - ITERS, 1 + k) if own(r) else halo(r) + (samples + k,)
            v = jnp.where(l32 < SEG // 2, roll(ref[i, g, :, left], 4), roll(ref[i, g, :, right], 28))
            sw_ref[r, k] = replicate(v, seg)

    def sample(s, carry):
        def first_y(r):
            ref, i = (y_ref, r - ITERS) if own(r) else halo(r)
            return ref[i, s]

        source = first_y
        for step in range(ITERS):
            target = (p_ref, q_ref)[step % 2]

            def put(r, v, target=target, step=step):
                if step == ITERS - 1:
                    x_ref[r - ITERS, s] = v
                else:
                    target[r, s] = v

            stencil(high, source, get_w, step + 1, high - 1 - step, put)
            source = functools.partial(lambda r, target: target[r, s], target=target)
        return carry

    lax.fori_loop(0, samples, sample, 0)


def strip_kernel(x_ref, w_ref, sy_ref, sw_ref, left_ref, right_ref, out_ref, var_ref, sum_ref):
    rows, samples, levels, cols = x_ref.shape
    high = rows + 2 * ITERS
    lane, seg, l32 = lane_parts((levels, LANES))
    from_left, from_right = l32 < 4, l32 >= 28

    def get_w(r):
        w = [
            jnp.where(
                from_left,
                roll(left_ref[r], -4 * (k + 1)),
                jnp.where(from_right, roll(right_ref[r], 4 * (k + 1)), sw_ref[r, k]),
            )
            for k in range(3)
        ]
        return (centre_weight(w[0], w[1]), *w)

    weights = [get_w(r) for r in range(high)]
    field = {
        r: jnp.where(from_left, left_ref[r], jnp.where(from_right, right_ref[r], sy_ref[r]))
        for r in range(high)
    }
    for step in range(ITERS):
        new = {}
        stencil(high, field.__getitem__, weights.__getitem__, step + 1, high - 1 - step, new.__setitem__)
        field = new

    total, count = None, None
    for r in range(rows):
        strip = field[ITERS + r]
        for c in range(0, cols, LANES):
            lanes = pl.ds(c, LANES)
            square = None
            for s in range(samples):
                v = x_ref[r, s, :, lanes]
                if c == 0:
                    v = jnp.where(lane < 4, roll(strip, -(SEG * s + 4)), v)
                if c == cols - LANES:
                    v = jnp.where(lane >= LANES - 4, roll(strip, LANES - SEG * s - 28), v)
                out_ref[r, s, :, lanes] = v
                square = v * v if square is None else square + v * v
            var = square / samples
            var_ref[r, :, lanes] = var
            m = jnp.where(w_ref[r, 1, :, lanes] > 0, 1.0, 0.0)
            total = m * var if total is None else total + m * var
            count = m if count is None else count + m
    sum_ref[0:1] = jnp.sum(total, axis=0, keepdims=True)
    sum_ref[1:2] = jnp.sum(count, axis=0, keepdims=True)


def scale_kernel(x_ref, w_ref, var_ref, all_ref, out_ref, stage, sem):
    rows, samples, levels, cols = x_ref.shape
    sums = jnp.sum(jnp.sum(all_ref[...], axis=0), axis=1, keepdims=True)
    mean = sums[0:1] / sums[1:2]
    copies = []
    for c in range(cols // LANES):
        lanes = pl.ds(c * LANES, LANES)
        for r in range(rows):
            wet = w_ref[r, 1, :, lanes] > 0
            safe = jnp.where(wet, var_ref[r, :, lanes], 1.0)
            factor = jnp.where(wet, jnp.sqrt(mean / (safe + 1e-06)), 0.0)
            for s in range(samples):
                stage[c, s, pl.ds(r, levels, stride=rows)] = x_ref[r, s, :, lanes] * factor
        copies.append(pltpu.make_async_copy(stage.at[c], out_ref.at[:, :, lanes], sem.at[c]))
        copies[-1].start()
    for copy in copies:
        copy.wait()


def call(kernel, out, *args, scratch=(), flops=0, in_space=None, out_space=None):
    out = [o if isinstance(o, jax.ShapeDtypeStruct) else jax.ShapeDtypeStruct(o, F32) for o in out]
    scratch = [pltpu.VMEM(o, F32) if isinstance(o, tuple) else o for o in scratch]
    return pl.pallas_call(
        kernel,
        out_shape=out,
        in_specs=[pl.BlockSpec(memory_space=in_space or pltpu.VMEM)] * len(args),
        out_specs=[pl.BlockSpec(memory_space=out_space or pltpu.VMEM)] * len(out),
        scratch_shapes=scratch,
        cost_estimate=pl.CostEstimate(flops=flops, bytes_accessed=sum(a.size * 4 for a in args), transcendentals=0),
        compiler_params=pltpu.CompilerParams(vmem_limit_bytes=12 << 20),
        name=kernel.__name__,
    )(*args)


def shards(noise, diff_lat, diff_lon, shear, sea_mask):
    samples, levels, rows, cols = noise.shape
    high = rows + 2 * ITERS
    flat = [noise.reshape(samples, levels * rows, cols)] + [
        a.reshape(levels * rows, cols) for a in (diff_lat, diff_lon, shear, sea_mask)
    ]
    n_lat, n_lon = lax.axis_size("lat"), lax.axis_size("lon")
    up = [(i, i + 1) for i in range(n_lat - 1)]
    down = [(j, i) for i, j in up]
    east = [(i, (i + 1) % n_lon) for i in range(n_lon)]
    west = [(j, i) for i, j in east]

    halo = (ITERS, samples + 3, levels, cols)
    tiles = cols // LANES
    plane = (tiles, levels * rows, LANES)
    top, bottom, *staged = call(
        edge_kernel,
        [halo, halo, (tiles, samples, levels * rows, LANES)] + [plane] * 3 + [jax.ShapeDtypeStruct(plane, sea_mask.dtype)],
        *flat,
        scratch=[pltpu.SemaphoreType.DMA((tiles, 5))],
        in_space=pl.ANY,
    )
    after = lax.ppermute(top, "lat", down)
    before = lax.ppermute(bottom, "lat", up)
    y, w, own_msg = call(
        own_kernel,
        [(rows, samples, levels, cols), (rows, 4, levels, cols), (rows, levels, LANES)],
        *staged,
        flops=10**6,
    )
    (msg,) = call(join_kernel, [(high, levels, LANES)], own_msg, before, after)
    left = lax.ppermute(msg, "lon", east)
    right = lax.ppermute(msg, "lon", west)
    buffer = (high, samples, levels, cols)
    x, sy, sw = call(
        main_kernel,
        [y.shape, (high, levels, LANES), (high, 3, levels, LANES)],
        y,
        w,
        before,
        after,
        scratch=[(2 * ITERS, 4, levels, cols), buffer, buffer],
        flops=10**7,
    )
    x, var, part = call(
        strip_kernel, [y.shape, (rows, levels, cols), (2, LANES)], x, w, sy, sw, left, right
    )
    spread = jnp.broadcast_to(part, (n_lat * n_lon, 2, LANES))
    every = lax.all_to_all(spread, ("lat", "lon"), 0, 0, tiled=True)
    (out,) = call(
        scale_kernel,
        [(samples, levels * rows, cols)],
        x,
        w,
        var,
        every,
        scratch=[(tiles, samples, levels * rows, LANES), pltpu.SemaphoreType.DMA((tiles,))],
        out_space=pl.ANY,
    )
    sums = jnp.sum(every, axis=(0, 2))
    return out.reshape(noise.shape), sums[0] / sums[1]


def solution(mesh):
    grid = P(None, "lat", "lon")
    field = P(None, None, "lat", "lon")
    return jax.shard_map(
        shards,
        mesh=mesh,
        in_specs=(field, grid, grid, grid, grid),
        out_specs=(field, P()),
        check_vma=False,
    )
```

```python
import functools

import jax
import jax.numpy as jnp
from jax import lax
from jax.experimental import pallas as pl
from jax.experimental.pallas import tpu as pltpu
from jax.sharding import PartitionSpec as P

ITERS = 4
LANES = 128
SEG = 32
F32 = jnp.float32


def cell_weights(k11, k22, shear, mask):
    m = mask.astype(F32)
    return m * k11, m * k22, m * (0.5 * (shear * jnp.sqrt(k11 * k22)))


def centre_weight(wa, wb):
    return jnp.where(wa > 0, 1.0, 0.0) - 2.0 * (wa + wb)


def roll(x, shift):
    n = x.shape[-1]
    shift = shift % n
    return x if shift == 0 else pltpu.roll(x, shift, x.ndim - 1)


def lane_parts(shape):
    lane = lax.broadcasted_iota(jnp.int32, shape, 1)
    return lane, lane // SEG, lane % SEG


def stencil(rows, get_y, get_w, first, last, put):
    def products(r):
        y = get_y(r)
        w0, wa, wb, wc = get_w(r)
        return w0 * y, wa * y, wb * y, wc * y

    prev, here = products(first - 1), products(first)
    for r in range(first, last):
        after = products(r + 1)
        d, _, b, _ = here
        g = prev[3] - after[3]
        put(r, d + (prev[1] + after[1]) + roll(b + g, 1) + roll(b - g, -1))
        prev, here = here, after


def edge_kernel(n_ref, a_ref, b_ref, s_ref, m_ref, top_ref, bot_ref, n_to, a_to, b_to, s_to, m_to, sem):
    samples, levels, tiles = n_ref.shape[0], top_ref.shape[2], n_to.shape[0]
    rows = n_ref.shape[1] // levels
    copies = []
    for c in range(tiles):
        lanes = pl.ds(c * LANES, LANES)
        for k, (ref, to) in enumerate(((a_ref, a_to), (b_ref, b_to), (s_ref, s_to), (m_ref, m_to))):
            copies.append(pltpu.make_async_copy(ref.at[:, lanes], to.at[c], sem.at[c, k]))
        copies.append(pltpu.make_async_copy(n_ref.at[:, :, lanes], n_to.at[c], sem.at[c, 4]))
    for copy in copies:
        copy.start()
    for copy in copies:
        copy.wait()
    for i in range(ITERS):
        for out, r in ((top_ref, i), (bot_ref, rows - ITERS + i)):
            at = pl.ds(r, levels, stride=rows)
            for c in range(tiles):
                lanes = pl.ds(c * LANES, LANES)
                for s in range(samples):
                    out[i, s, :, lanes] = n_to[c, s, at]
                w = cell_weights(a_to[c, at], b_to[c, at], s_to[c, at], m_to[c, at])
                for k in range(3):
                    out[i, samples + k, :, lanes] = w[k]


BATCH = 4


def replicate(values, seg):
    turned = [roll(v, SEG) for v in values]
    values = [jnp.where(seg == 1, t, v) for t, v in zip(turned, values)]
    turned = [roll(v, 2 * SEG) for v in values]
    return [jnp.where(seg >= 2, t, v) for t, v in zip(turned, values)]


def line_up(gets, samples, parts, low, high):
    _, seg, l32 = parts
    turned = [
        [(roll(get(s, low), SEG * s + 4), roll(get(s, high), SEG * s + 28)) for s in range(samples)] for get in gets
    ]
    lines = []
    for row in turned:
        line = None
        for s, (a, b) in enumerate(row):
            v = jnp.where(l32 < SEG // 2, a, b)
            line = v if line is None else jnp.where(seg == s, v, line)
        lines.append(line)
    return lines


def messages(gets, samples, parts):
    _, seg, l32 = parts
    lines = line_up(gets, samples, parts, 1, 0)
    turned = [
        [(roll(get(samples + k, 1), 4 * k + 8), roll(get(samples + k, 0), 24 - 4 * k)) for k in range(3)] for get in gets
    ]
    packed = []
    for row in turned:
        line = None
        for k, (a, b) in enumerate(row):
            v = jnp.where(l32 < SEG // 2, a, b)
            line = v if line is None else jnp.where((l32 // 4 == k + 1) | (l32 // 4 == 6 - k), v, line)
        packed.append(line)
    packed = replicate(packed, seg)
    return [jnp.where((l32 < 4) | (l32 >= 28), a, b) for a, b in zip(lines, packed)]


def strips(gets, samples, parts):
    _, seg, l32 = parts
    lines = line_up(gets, samples, parts, 0, 1)
    turned = [(roll(get(samples + k, 0), 4), roll(get(samples + k, 1), 28)) for get in gets for k in range(3)]
    weights = replicate([jnp.where(l32 < SEG // 2, a, b) for a, b in turned], seg)
    return lines, [weights[3 * i : 3 * i + 3] for i in range(len(gets))]


def own_kernel(n_ref, a_ref, b_ref, s_ref, m_ref, y_ref, w_ref, msg_ref, sy_ref, sw_ref):
    rows, samples, levels, cols = y_ref.shape
    parts = lane_parts((levels, LANES))
    tiles = cols // LANES

    def read(r):
        at = pl.ds(r, levels, stride=rows)
        return [
            [n_ref[c, s, at] for s in range(samples)]
            + list(cell_weights(a_ref[c, at], b_ref[c, at], s_ref[c, at], m_ref[c, at]))
            for c in range(tiles)
        ]

    for first in range(0, rows, BATCH):
        batch = range(first, first + BATCH)
        data = [read(r) for r in batch]
        gets = [lambda g, side, row=row: row[side * (tiles - 1)][g] for row in data]
        sent = messages(gets, samples, parts)
        lines, weights = strips(gets, samples, parts)
        for i, r in enumerate(batch):
            for c in range(tiles):
                lanes = pl.ds(c * LANES, LANES)
                values = data[i][c]
                for s in range(samples):
                    y_ref[r, s, :, lanes] = values[s]
                w_ref[r, 0, :, lanes] = centre_weight(values[samples], values[samples + 1])
                for k in range(3):
                    w_ref[r, 1 + k, :, lanes] = values[samples + k]
            msg_ref[r] = sent[i]
            sy_ref[r] = lines[i]
            for k in range(3):
                sw_ref[r, k] = weights[i][k]


def halo_gets(ref):
    last = ref.shape[3] - LANES
    return [lambda g, side, i=i: ref[i, g, :, pl.ds(side * last, LANES)] for i in range(ITERS)]


def join_kernel(own_ref, before_ref, after_ref, msg_ref):
    rows = own_ref.shape[0]
    samples = before_ref.shape[1] - 3
    parts = lane_parts(own_ref.shape[1:])
    sent = messages(halo_gets(before_ref) + halo_gets(after_ref), samples, parts)
    msg_ref[ITERS : ITERS + rows] = own_ref[...]
    for i in range(ITERS):
        msg_ref[i] = sent[i]
        msg_ref[ITERS + rows + i] = sent[ITERS + i]


def main_kernel(y_ref, w_ref, before_ref, after_ref, x_ref, hy_ref, hw_ref, wh_ref, p_ref, q_ref):
    rows, samples, levels, cols = y_ref.shape
    high = rows + 2 * ITERS
    parts = lane_parts((levels, LANES))

    def halo(r):
        return (before_ref, r) if r < ITERS else (after_ref, r - ITERS - rows)

    def own(r):
        return ITERS <= r < ITERS + rows

    for r in range(high):
        if not own(r):
            ref, i = halo(r)
            slot = r if r < ITERS else r - rows
            w = [ref[i, samples + k] for k in range(3)]
            wh_ref[slot, 0] = centre_weight(w[0], w[1])
            for k in range(3):
                wh_ref[slot, 1 + k] = w[k]

    def get_w(r):
        if own(r):
            return [w_ref[r - ITERS, k] for k in range(4)]
        return [wh_ref[r if r < ITERS else r - rows, k] for k in range(4)]

    for side, ref in enumerate((before_ref, after_ref)):
        lines, weights = strips(halo_gets(ref), samples, parts)
        for i in range(ITERS):
            hy_ref[side * ITERS + i] = lines[i]
            for k in range(3):
                hw_ref[side * ITERS + i, k] = weights[i][k]

    def sample(s, carry):
        def first_y(r):
            ref, i = (y_ref, r - ITERS) if own(r) else halo(r)
            return ref[i, s]

        source = first_y
        for step in range(ITERS):
            target = (p_ref, q_ref)[step % 2]

            def put(r, v, target=target, step=step):
                if step == ITERS - 1:
                    x_ref[r - ITERS, s] = v
                else:
                    target[r, s] = v

            stencil(high, source, get_w, step + 1, high - 1 - step, put)
            source = functools.partial(lambda r, target: target[r, s], target=target)
        return carry

    lax.fori_loop(0, samples, sample, 0)


def strip_kernel(x_ref, w_ref, sy_ref, sw_ref, hy_ref, hw_ref, left_ref, right_ref, out_ref, var_ref, sum_ref):
    rows, samples, levels, cols = x_ref.shape
    high = rows + 2 * ITERS
    lane, seg, l32 = lane_parts((levels, LANES))
    from_left, from_right = l32 < 4, l32 >= 28

    def strip_at(r):
        if ITERS <= r < ITERS + rows:
            return sy_ref, sw_ref, r - ITERS
        return hy_ref, hw_ref, r if r < ITERS else r - rows

    def get_y(r):
        ref, _, i = strip_at(r)
        return jnp.where(from_left, left_ref[r], jnp.where(from_right, right_ref[r], ref[i]))

    def get_w(r):
        _, ref, i = strip_at(r)
        w = [
            jnp.where(
                from_left,
                roll(left_ref[r], -4 * (k + 1)),
                jnp.where(from_right, roll(right_ref[r], 4 * (k + 1)), ref[i, k]),
            )
            for k in range(3)
        ]
        return (centre_weight(w[0], w[1]), *w)

    weights = [get_w(r) for r in range(high)]
    field = {r: get_y(r) for r in range(high)}
    for step in range(ITERS):
        new = {}
        stencil(high, field.__getitem__, weights.__getitem__, step + 1, high - 1 - step, new.__setitem__)
        field = new

    total, count = None, None
    for r in range(rows):
        strip = field[ITERS + r]
        for c in range(0, cols, LANES):
            lanes = pl.ds(c, LANES)
            square = None
            for s in range(samples):
                v = x_ref[r, s, :, lanes]
                if c == 0:
                    v = jnp.where(lane < 4, roll(strip, -(SEG * s + 4)), v)
                if c == cols - LANES:
                    v = jnp.where(lane >= LANES - 4, roll(strip, LANES - SEG * s - 28), v)
                out_ref[r, s, :, lanes] = v
                square = v * v if square is None else square + v * v
            var = square / samples
            var_ref[r, :, lanes] = var
            m = jnp.where(w_ref[r, 1, :, lanes] > 0, 1.0, 0.0)
            total = m * var if total is None else total + m * var
            count = m if count is None else count + m
    sum_ref[0:1] = jnp.sum(total, axis=0, keepdims=True)
    sum_ref[1:2] = jnp.sum(count, axis=0, keepdims=True)


def scale_kernel(x_ref, w_ref, var_ref, all_ref, out_ref, mean_ref, stage, sem):
    rows, samples, levels, cols = x_ref.shape
    sums = jnp.sum(jnp.sum(all_ref[...], axis=0), axis=1, keepdims=True)
    mean = sums[0:1] / sums[1:2]
    mean_ref[...] = mean
    copies = []
    for c in range(cols // LANES):
        lanes = pl.ds(c * LANES, LANES)
        for r in range(rows):
            wet = w_ref[r, 1, :, lanes] > 0
            safe = jnp.where(wet, var_ref[r, :, lanes], 1.0)
            factor = jnp.where(wet, jnp.sqrt(mean / (safe + 1e-06)), 0.0)
            for s in range(samples):
                stage[c, s, pl.ds(r, levels, stride=rows)] = x_ref[r, s, :, lanes] * factor
        copies.append(pltpu.make_async_copy(stage.at[c], out_ref.at[:, :, lanes], sem.at[c]))
        copies[-1].start()
    for copy in copies:
        copy.wait()


def call(kernel, out, *args, scratch=(), flops=0, in_space=None, out_space=None):
    out = [o if isinstance(o, jax.ShapeDtypeStruct) else jax.ShapeDtypeStruct(o, F32) for o in out]
    scratch = [pltpu.VMEM(o, F32) if isinstance(o, tuple) else o for o in scratch]
    return pl.pallas_call(
        kernel,
        out_shape=out,
        in_specs=[pl.BlockSpec(memory_space=in_space or pltpu.VMEM)] * len(args),
        out_specs=[pl.BlockSpec(memory_space=m) for m in out_space or [pltpu.VMEM] * len(out)],
        scratch_shapes=scratch,
        cost_estimate=pl.CostEstimate(flops=flops, bytes_accessed=sum(a.size * 4 for a in args), transcendentals=0),
        compiler_params=pltpu.CompilerParams(vmem_limit_bytes=12 << 20),
        name=kernel.__name__,
    )(*args)


def shards(noise, diff_lat, diff_lon, shear, sea_mask):
    samples, levels, rows, cols = noise.shape
    high = rows + 2 * ITERS
    flat = [noise.reshape(samples, levels * rows, cols)] + [
        a.reshape(levels * rows, cols) for a in (diff_lat, diff_lon, shear, sea_mask)
    ]
    n_lat, n_lon = lax.axis_size("lat"), lax.axis_size("lon")
    up = [(i, i + 1) for i in range(n_lat - 1)]
    down = [(j, i) for i, j in up]
    east = [(i, (i + 1) % n_lon) for i in range(n_lon)]
    west = [(j, i) for i, j in east]

    halo = (ITERS, samples + 3, levels, cols)
    tiles = cols // LANES
    plane = (tiles, levels * rows, LANES)
    flat = [pltpu.with_memory_space_constraint(a, pltpu.HBM) for a in flat]
    top, bottom, *staged = call(
        edge_kernel,
        [halo, halo, (tiles, samples, levels * rows, LANES)] + [plane] * 3 + [jax.ShapeDtypeStruct(plane, sea_mask.dtype)],
        *flat,
        scratch=[pltpu.SemaphoreType.DMA((tiles, 5))],
        in_space=pltpu.HBM,
    )
    after = lax.ppermute(top, "lat", down)
    before = lax.ppermute(bottom, "lat", up)
    y, w, own_msg, sy, sw = call(
        own_kernel,
        [(rows, samples, levels, cols), (rows, 4, levels, cols), (rows, levels, LANES), (rows, levels, LANES), (rows, 3, levels, LANES)],
        *staged,
        flops=10**6,
    )
    (msg,) = call(join_kernel, [(high, levels, LANES)], own_msg, before, after)
    left = lax.ppermute(msg, "lon", east)
    right = lax.ppermute(msg, "lon", west)
    buffer = (high, samples, levels, cols)
    x, hy, hw = call(
        main_kernel,
        [y.shape, (2 * ITERS, levels, LANES), (2 * ITERS, 3, levels, LANES)],
        y,
        w,
        before,
        after,
        scratch=[(2 * ITERS, 4, levels, cols), buffer, buffer],
        flops=10**7,
    )
    x, var, part = call(
        strip_kernel, [y.shape, (rows, levels, cols), (2, LANES)], x, w, sy, sw, hy, hw, left, right
    )
    spread = jnp.broadcast_to(part, (n_lat * n_lon, 2, LANES))
    every = lax.all_to_all(spread, ("lat", "lon"), 0, 0, tiled=True)
    out, mean = call(
        scale_kernel,
        [(samples, levels * rows, cols), (1, 1)],
        x,
        w,
        var,
        every,
        scratch=[(tiles, samples, levels * rows, LANES), pltpu.SemaphoreType.DMA((tiles,))],
        out_space=[pl.ANY, pltpu.VMEM],
    )
    return out.reshape(noise.shape), mean.reshape(())


def solution(mesh):
    grid = P(None, "lat", "lon")
    field = P(None, None, "lat", "lon")
    return jax.shard_map(
        shards,
        mesh=mesh,
        in_specs=(field, grid, grid, grid, grid),
        out_specs=(field, P()),
        check_vma=False,
    )
```

```python
import functools

import jax
import jax.numpy as jnp
from jax import lax
from jax.experimental import pallas as pl
from jax.experimental.pallas import tpu as pltpu
from jax.sharding import PartitionSpec as P

ITERS = 4
LANES = 128
SEG = 32
F32 = jnp.float32


def cell_weights(k11, k22, shear, mask):
    m = mask.astype(F32)
    return m * k11, m * k22, m * (0.5 * (shear * jnp.sqrt(k11 * k22)))


def centre_weight(wa, wb):
    return jnp.where(wa > 0, 1.0, 0.0) - 2.0 * (wa + wb)


def roll(x, shift):
    n = x.shape[-1]
    shift = shift % n
    return x if shift == 0 else pltpu.roll(x, shift, x.ndim - 1)


def lane_parts(shape):
    lane = lax.broadcasted_iota(jnp.int32, shape, 1)
    return lane, lane // SEG, lane % SEG


def stencil(rows, get_y, get_w, first, last, put):
    def products(r):
        y = get_y(r)
        w0, wa, wb, wc = get_w(r)
        return w0 * y, wa * y, wb * y, wc * y

    prev, here = products(first - 1), products(first)
    for r in range(first, last):
        after = products(r + 1)
        d, _, b, _ = here
        g = prev[3] - after[3]
        put(r, d + (prev[1] + after[1]) + roll(b + g, 1) + roll(b - g, -1))
        prev, here = here, after


def edge_kernel(n_ref, a_ref, b_ref, s_ref, m_ref, top_ref, bot_ref, first_ref, last_ref, n_to, a_to, b_to, s_to, m_to, sem):
    samples, levels, tiles = n_ref.shape[0], top_ref.shape[2], n_to.shape[0]
    rows = n_ref.shape[1] // levels
    copies = []
    for c in range(tiles):
        lanes = pl.ds(c * LANES, LANES)
        for k, (ref, to) in enumerate(((a_ref, a_to), (b_ref, b_to), (s_ref, s_to), (m_ref, m_to))):
            copies.append(pltpu.make_async_copy(ref.at[:, lanes], to.at[c], sem.at[c, k]))
        copies.append(pltpu.make_async_copy(n_ref.at[:, :, lanes], n_to.at[c], sem.at[c, 4]))
    for copy in copies:
        copy.start()
    for copy in copies:
        copy.wait()
    for i in range(ITERS):
        for out, r in ((top_ref, i), (bot_ref, rows - ITERS + i)):
            at = pl.ds(r, levels, stride=rows)
            for c in range(tiles):
                lanes = pl.ds(c * LANES, LANES)
                for s in range(samples):
                    out[i, s, :, lanes] = n_to[c, s, at]
                w = cell_weights(a_to[c, at], b_to[c, at], s_to[c, at], m_to[c, at])
                for k in range(3):
                    out[i, samples + k, :, lanes] = w[k]
    parts = lane_parts((levels, LANES))
    for out, ref in ((first_ref, top_ref), (last_ref, bot_ref)):
        out[0], out[1] = messages(halo_gets(ref), samples, parts)


BATCH = 4


def replicate(values, seg):
    turned = [roll(v, SEG) for v in values]
    values = [jnp.where(seg == 1, t, v) for t, v in zip(turned, values)]
    turned = [roll(v, 2 * SEG) for v in values]
    return [jnp.where(seg >= 2, t, v) for t, v in zip(turned, values)]


def line_up(gets, samples, parts, low, high):
    _, seg, l32 = parts
    turned = [
        [(roll(get(s, low), SEG * s + 4), roll(get(s, high), SEG * s + 28)) for s in range(samples)] for get in gets
    ]
    lines = []
    for row in turned:
        line = None
        for s, (a, b) in enumerate(row):
            v = jnp.where(l32 < SEG // 2, a, b)
            line = v if line is None else jnp.where(seg == s, v, line)
        lines.append(line)
    return lines


def messages(gets, samples, parts):
    lane = parts[0]
    east = west = None
    for j, get in enumerate(gets):
        for g in range(samples + 3):
            last = roll(get(g, 1), SEG * j + 4 * g + 4)
            first = roll(get(g, 0), SEG * j + 28 - 4 * g)
            east = last if east is None else jnp.where(lane // 4 == 8 * j + g, last, east)
            west = first if west is None else jnp.where(lane // 4 == 8 * j + 7 - g, first, west)
    return east, west


def unpack(tile, samples, parts, sign):
    _, seg, _ = parts
    turned = [roll(tile, SEG * q) for q in range(4)]
    rows = []
    for j in range(4):
        every = turned[(0 - j) % 4]
        for q in range(1, 4):
            every = jnp.where(seg == q, turned[(q - j) % 4], every)
        line = every
        for s in range(1, samples):
            line = jnp.where(seg == s, roll(every, -sign * 4 * s), line)
        rows.append((line, [roll(every, -sign * 4 * (samples + k)) for k in range(3)]))
    return rows


def strips(gets, samples, parts):
    _, seg, l32 = parts
    lines = line_up(gets, samples, parts, 0, 1)
    turned = [(roll(get(samples + k, 0), 4), roll(get(samples + k, 1), 28)) for get in gets for k in range(3)]
    weights = replicate([jnp.where(l32 < SEG // 2, a, b) for a, b in turned], seg)
    return lines, [weights[3 * i : 3 * i + 3] for i in range(len(gets))]


def own_kernel(n_ref, a_ref, b_ref, s_ref, m_ref, y_ref, w_ref, msg_ref, sy_ref, sw_ref):
    rows, samples, levels, cols = y_ref.shape
    parts = lane_parts((levels, LANES))
    tiles = cols // LANES

    def read(r):
        at = pl.ds(r, levels, stride=rows)
        return [
            [n_ref[c, s, at] for s in range(samples)]
            + list(cell_weights(a_ref[c, at], b_ref[c, at], s_ref[c, at], m_ref[c, at]))
            for c in range(tiles)
        ]

    for first in range(0, rows, BATCH):
        batch = range(first, first + BATCH)
        data = [read(r) for r in batch]
        gets = [lambda g, side, row=row: row[side * (tiles - 1)][g] for row in data]
        lines, weights = strips(gets, samples, parts)
        if 0 < first < rows - BATCH:
            msg_ref[0, first // BATCH - 1], msg_ref[1, first // BATCH - 1] = messages(gets, samples, parts)
        for i, r in enumerate(batch):
            for c in range(tiles):
                lanes = pl.ds(c * LANES, LANES)
                values = data[i][c]
                for s in range(samples):
                    y_ref[r, s, :, lanes] = values[s]
                w_ref[r, 0, :, lanes] = centre_weight(values[samples], values[samples + 1])
                for k in range(3):
                    w_ref[r, 1 + k, :, lanes] = values[samples + k]
            sy_ref[r] = lines[i]
            for k in range(3):
                sw_ref[r, k] = weights[i][k]


def halo_gets(ref):
    last = ref.shape[3] - LANES
    return [lambda g, side, i=i: ref[i, g, :, pl.ds(side * last, LANES)] for i in range(ITERS)]


def main_kernel(y_ref, w_ref, before_ref, after_ref, x_ref, hy_ref, hw_ref, wh_ref, p_ref, q_ref):
    rows, samples, levels, cols = y_ref.shape
    high = rows + 2 * ITERS
    parts = lane_parts((levels, LANES))

    def halo(r):
        return (before_ref, r) if r < ITERS else (after_ref, r - ITERS - rows)

    def own(r):
        return ITERS <= r < ITERS + rows

    for r in range(high):
        if not own(r):
            ref, i = halo(r)
            slot = r if r < ITERS else r - rows
            w = [ref[i, samples + k] for k in range(3)]
            wh_ref[slot, 0] = centre_weight(w[0], w[1])
            for k in range(3):
                wh_ref[slot, 1 + k] = w[k]

    def get_w(r):
        if own(r):
            return [w_ref[r - ITERS, k] for k in range(4)]
        return [wh_ref[r if r < ITERS else r - rows, k] for k in range(4)]

    for side, ref in enumerate((before_ref, after_ref)):
        lines, weights = strips(halo_gets(ref), samples, parts)
        for i in range(ITERS):
            hy_ref[side * ITERS + i] = lines[i]
            for k in range(3):
                hw_ref[side * ITERS + i, k] = weights[i][k]

    def sample(s, carry):
        def first_y(r):
            ref, i = (y_ref, r - ITERS) if own(r) else halo(r)
            return ref[i, s]

        source = first_y
        for step in range(ITERS):
            target = (p_ref, q_ref)[step % 2]

            def put(r, v, target=target, step=step):
                if step == ITERS - 1:
                    x_ref[r - ITERS, s] = v
                else:
                    target[r, s] = v

            stencil(high, source, get_w, step + 1, high - 1 - step, put)
            source = functools.partial(lambda r, target: target[r, s], target=target)
        return carry

    lax.fori_loop(0, samples, sample, 0)


def strip_kernel(x_ref, w_ref, sy_ref, sw_ref, hy_ref, hw_ref, left_ref, right_ref, out_ref, var_ref, sum_ref):
    rows, samples, levels, cols = x_ref.shape
    high = rows + 2 * ITERS
    parts = lane_parts((levels, LANES))
    lane, _, l32 = parts
    from_left, from_right = l32 < 4, l32 >= 28

    def strip_at(r):
        if ITERS <= r < ITERS + rows:
            return sy_ref, sw_ref, r - ITERS
        return hy_ref, hw_ref, r if r < ITERS else r - rows

    lefts = [row for q in range(high // 4) for row in unpack(left_ref[q], samples, parts, 1)]
    rights = [row for q in range(high // 4) for row in unpack(right_ref[q], samples, parts, -1)]

    def get_y(r):
        ref, _, i = strip_at(r)
        return jnp.where(from_left, lefts[r][0], jnp.where(from_right, rights[r][0], ref[i]))

    def get_w(r):
        _, ref, i = strip_at(r)
        w = [
            jnp.where(from_left, lefts[r][1][k], jnp.where(from_right, rights[r][1][k], ref[i, k])) for k in range(3)
        ]
        return (centre_weight(w[0], w[1]), *w)

    weights = [get_w(r) for r in range(high)]
    field = {r: get_y(r) for r in range(high)}
    for step in range(ITERS):
        new = {}
        stencil(high, field.__getitem__, weights.__getitem__, step + 1, high - 1 - step, new.__setitem__)
        field = new

    total, count = None, None
    for r in range(rows):
        strip = field[ITERS + r]
        for c in range(0, cols, LANES):
            lanes = pl.ds(c, LANES)
            square = None
            for s in range(samples):
                v = x_ref[r, s, :, lanes]
                if c == 0:
                    v = jnp.where(lane < 4, roll(strip, -(SEG * s + 4)), v)
                if c == cols - LANES:
                    v = jnp.where(lane >= LANES - 4, roll(strip, LANES - SEG * s - 28), v)
                out_ref[r, s, :, lanes] = v
                square = v * v if square is None else square + v * v
            var = square / samples
            var_ref[r, :, lanes] = var
            m = jnp.where(w_ref[r, 1, :, lanes] > 0, 1.0, 0.0)
            total = m * var if total is None else total + m * var
            count = m if count is None else count + m
    sum_ref[0:1] = jnp.sum(total, axis=0, keepdims=True)
    sum_ref[1:2] = jnp.sum(count, axis=0, keepdims=True)


def scale_kernel(x_ref, w_ref, var_ref, all_ref, out_ref, mean_ref, stage, sem):
    rows, samples, levels, cols = x_ref.shape
    sums = jnp.sum(jnp.sum(all_ref[...], axis=0), axis=1, keepdims=True)
    mean = sums[0:1] / sums[1:2]
    mean_ref[...] = mean
    copies = []
    for c in range(cols // LANES):
        lanes = pl.ds(c * LANES, LANES)
        for r in range(rows):
            wet = w_ref[r, 1, :, lanes] > 0
            safe = jnp.where(wet, var_ref[r, :, lanes], 1.0)
            factor = jnp.where(wet, jnp.sqrt(mean / (safe + 1e-06)), 0.0)
            for s in range(samples):
                stage[c, s, pl.ds(r, levels, stride=rows)] = x_ref[r, s, :, lanes] * factor
        copies.append(pltpu.make_async_copy(stage.at[c], out_ref.at[:, :, lanes], sem.at[c]))
        copies[-1].start()
    for copy in copies:
        copy.wait()


def call(kernel, out, *args, scratch=(), flops=0, in_space=None, out_space=None):
    out = [o if isinstance(o, jax.ShapeDtypeStruct) else jax.ShapeDtypeStruct(o, F32) for o in out]
    scratch = [pltpu.VMEM(o, F32) if isinstance(o, tuple) else o for o in scratch]
    return pl.pallas_call(
        kernel,
        out_shape=out,
        in_specs=[pl.BlockSpec(memory_space=in_space or pltpu.VMEM)] * len(args),
        out_specs=[pl.BlockSpec(memory_space=m) for m in out_space or [pltpu.VMEM] * len(out)],
        scratch_shapes=scratch,
        cost_estimate=pl.CostEstimate(flops=flops, bytes_accessed=sum(a.size * 4 for a in args), transcendentals=0),
        compiler_params=pltpu.CompilerParams(vmem_limit_bytes=12 << 20),
        name=kernel.__name__,
    )(*args)


def shards(noise, diff_lat, diff_lon, shear, sea_mask):
    samples, levels, rows, cols = noise.shape
    high = rows + 2 * ITERS
    flat = [noise.reshape(samples, levels * rows, cols)] + [
        a.reshape(levels * rows, cols) for a in (diff_lat, diff_lon, shear, sea_mask)
    ]
    n_lat, n_lon = lax.axis_size("lat"), lax.axis_size("lon")
    up = [(i, i + 1) for i in range(n_lat - 1)]
    down = [(j, i) for i, j in up]
    east = [(i, (i + 1) % n_lon) for i in range(n_lon)]
    west = [(j, i) for i, j in east]

    halo = (ITERS, samples + 3, levels, cols)
    tiles = cols // LANES
    plane = (tiles, levels * rows, LANES)
    flat = [pltpu.with_memory_space_constraint(a, pltpu.HBM) for a in flat]
    corner = (2, levels, LANES)
    top, bottom, first, last, *staged = call(
        edge_kernel,
        [halo, halo, corner, corner, (tiles, samples, levels * rows, LANES)]
        + [plane] * 3
        + [jax.ShapeDtypeStruct(plane, sea_mask.dtype)],
        *flat,
        scratch=[pltpu.SemaphoreType.DMA((tiles, 5))],
        in_space=pltpu.HBM,
    )
    last_before = lax.ppermute(last, "lat", up)
    first_after = lax.ppermute(first, "lat", down)
    before = lax.ppermute(bottom, "lat", up)
    after = lax.ppermute(top, "lat", down)
    strip = (rows, levels, LANES)
    y, w, own_msg, sy, sw = call(
        own_kernel,
        [(rows, samples, levels, cols), (rows, 4, levels, cols), (2, rows // 4 - 2, levels, LANES), strip, (rows, 3, levels, LANES)],
        *staged,
        flops=10**6,
    )
    sent = [
        jnp.concatenate([last_before[d : d + 1], first[d : d + 1], own_msg[d], last[d : d + 1], first_after[d : d + 1]])
        for d in range(2)
    ]
    left = lax.ppermute(sent[0], "lon", east)
    right = lax.ppermute(sent[1], "lon", west)
    buffer = (high, samples, levels, cols)
    x, hy, hw = call(
        main_kernel,
        [y.shape, (2 * ITERS, levels, LANES), (2 * ITERS, 3, levels, LANES)],
        y,
        w,
        before,
        after,
        scratch=[(2 * ITERS, 4, levels, cols), buffer, buffer],
        flops=10**7,
    )
    x, var, part = call(
        strip_kernel, [y.shape, (rows, levels, cols), (2, LANES)], x, w, sy, sw, hy, hw, left, right
    )
    spread = jnp.broadcast_to(part, (n_lat * n_lon, 2, LANES))
    every = lax.all_to_all(spread, ("lat", "lon"), 0, 0, tiled=True)
    out, mean = call(
        scale_kernel,
        [(samples, levels * rows, cols), (1, 1)],
        x,
        w,
        var,
        every,
        scratch=[(tiles, samples, levels * rows, LANES), pltpu.SemaphoreType.DMA((tiles,))],
        out_space=[pl.ANY, pltpu.VMEM],
    )
    return out.reshape(noise.shape), mean.reshape(())


def solution(mesh):
    grid = P(None, "lat", "lon")
    field = P(None, None, "lat", "lon")
    return jax.shard_map(
        shards,
        mesh=mesh,
        in_specs=(field, grid, grid, grid, grid),
        out_specs=(field, P()),
        check_vma=False,
    )
```

```python
import functools

import jax
import jax.numpy as jnp
from jax import lax
from jax.experimental import pallas as pl
from jax.experimental.pallas import tpu as pltpu
from jax.sharding import PartitionSpec as P

ITERS = 4
LANES = 128
SEG = 32
F32 = jnp.float32


def cell_weights(k11, k22, shear, mask):
    m = mask.astype(F32)
    return m * k11, m * k22, m * (0.5 * (shear * jnp.sqrt(k11 * k22)))


def centre_weight(wa, wb):
    return jnp.where(wa > 0, 1.0, 0.0) - 2.0 * (wa + wb)


def roll(x, shift):
    n = x.shape[-1]
    shift = shift % n
    return x if shift == 0 else pltpu.roll(x, shift, x.ndim - 1)


def lane_parts(shape):
    lane = lax.broadcasted_iota(jnp.int32, shape, 1)
    return lane, lane // SEG, lane % SEG


def stencil(rows, get_y, get_w, first, last, put):
    def products(r):
        y = get_y(r)
        w0, wa, wb, wc = get_w(r)
        return w0 * y, wa * y, wb * y, wc * y

    prev, here = products(first - 1), products(first)
    for r in range(first, last):
        after = products(r + 1)
        d, _, b, _ = here
        g = prev[3] - after[3]
        put(r, d + (prev[1] + after[1]) + roll(b + g, 1) + roll(b - g, -1))
        prev, here = here, after


def edge_kernel(n_ref, a_ref, b_ref, s_ref, m_ref, top_ref, bot_ref, n_to, a_to, b_to, s_to, m_to, sem):
    samples, levels, tiles = n_ref.shape[0], top_ref.shape[2], n_to.shape[0]
    rows = n_ref.shape[1] // levels
    copies = []
    for c in range(tiles):
        lanes = pl.ds(c * LANES, LANES)
        for k, (ref, to) in enumerate(((a_ref, a_to), (b_ref, b_to), (s_ref, s_to), (m_ref, m_to))):
            copies.append(pltpu.make_async_copy(ref.at[:, lanes], to.at[c], sem.at[c, k]))
        copies.append(pltpu.make_async_copy(n_ref.at[:, :, lanes], n_to.at[c], sem.at[c, 4]))
    for copy in copies:
        copy.start()
    for copy in copies:
        copy.wait()
    for i in range(ITERS):
        for out, r in ((top_ref, i), (bot_ref, rows - ITERS + i)):
            at = pl.ds(r, levels, stride=rows)
            for c in range(tiles):
                lanes = pl.ds(c * LANES, LANES)
                for s in range(samples):
                    out[i, s, :, lanes] = n_to[c, s, at]
                w = cell_weights(a_to[c, at], b_to[c, at], s_to[c, at], m_to[c, at])
                for k in range(3):
                    out[i, samples + k, :, lanes] = w[k]


BATCH = 4


def replicate(values, seg):
    turned = [roll(v, SEG) for v in values]
    values = [jnp.where(seg == 1, t, v) for t, v in zip(turned, values)]
    turned = [roll(v, 2 * SEG) for v in values]
    return [jnp.where(seg >= 2, t, v) for t, v in zip(turned, values)]


def line_up(gets, samples, parts, low, high):
    _, seg, l32 = parts
    turned = [
        [(roll(get(s, low), SEG * s + 4), roll(get(s, high), SEG * s + 28)) for s in range(samples)] for get in gets
    ]
    lines = []
    for row in turned:
        line = None
        for s, (a, b) in enumerate(row):
            v = jnp.where(l32 < SEG // 2, a, b)
            line = v if line is None else jnp.where(seg == s, v, line)
        lines.append(line)
    return lines


def messages(gets, samples, parts):
    _, seg, l32 = parts
    lines = line_up(gets, samples, parts, 1, 0)
    turned = [
        [(roll(get(samples + k, 1), 4 * k + 8), roll(get(samples + k, 0), 24 - 4 * k)) for k in range(3)] for get in gets
    ]
    packed = []
    for row in turned:
        line = None
        for k, (a, b) in enumerate(row):
            v = jnp.where(l32 < SEG // 2, a, b)
            line = v if line is None else jnp.where((l32 // 4 == k + 1) | (l32 // 4 == 6 - k), v, line)
        packed.append(line)
    packed = replicate(packed, seg)
    both = [jnp.where((l32 < 4) | (l32 >= 28), a, b) for a, b in zip(lines, packed)]
    east, west = [], []
    for a, b in zip(both[0::2], both[1::2]):
        east.append(jnp.where(l32 < SEG // 2, a, roll(b, SEG // 2)))
        west.append(jnp.where(l32 < SEG // 2, roll(a, -SEG // 2), b))
    return east, west


def strips(gets, samples, parts):
    _, seg, l32 = parts
    lines = line_up(gets, samples, parts, 0, 1)
    turned = [(roll(get(samples + k, 0), 4), roll(get(samples + k, 1), 28)) for get in gets for k in range(3)]
    weights = replicate([jnp.where(l32 < SEG // 2, a, b) for a, b in turned], seg)
    return lines, [weights[3 * i : 3 * i + 3] for i in range(len(gets))]


def own_kernel(n_ref, a_ref, b_ref, s_ref, m_ref, y_ref, w_ref, msg_ref, sy_ref, sw_ref):
    rows, samples, levels, cols = y_ref.shape
    parts = lane_parts((levels, LANES))
    tiles = cols // LANES

    def read(r):
        at = pl.ds(r, levels, stride=rows)
        return [
            [n_ref[c, s, at] for s in range(samples)]
            + list(cell_weights(a_ref[c, at], b_ref[c, at], s_ref[c, at], m_ref[c, at]))
            for c in range(tiles)
        ]

    for first in range(0, rows, BATCH):
        batch = range(first, first + BATCH)
        data = [read(r) for r in batch]
        gets = [lambda g, side, row=row: row[side * (tiles - 1)][g] for row in data]
        east, west = messages(gets, samples, parts)
        for i in range(BATCH // 2):
            msg_ref[0, first // 2 + i] = east[i]
            msg_ref[1, first // 2 + i] = west[i]
        lines, weights = strips(gets, samples, parts)
        for i, r in enumerate(batch):
            for c in range(tiles):
                lanes = pl.ds(c * LANES, LANES)
                values = data[i][c]
                for s in range(samples):
                    y_ref[r, s, :, lanes] = values[s]
                w_ref[r, 0, :, lanes] = centre_weight(values[samples], values[samples + 1])
                for k in range(3):
                    w_ref[r, 1 + k, :, lanes] = values[samples + k]
            sy_ref[r] = lines[i]
            for k in range(3):
                sw_ref[r, k] = weights[i][k]


def halo_gets(ref):
    last = ref.shape[3] - LANES
    return [lambda g, side, i=i: ref[i, g, :, pl.ds(side * last, LANES)] for i in range(ITERS)]


def join_kernel(own_ref, before_ref, after_ref, east_ref, west_ref):
    pairs, half = own_ref.shape[1], ITERS // 2
    samples = before_ref.shape[1] - 3
    parts = lane_parts(own_ref.shape[2:])
    sent = messages(halo_gets(before_ref) + halo_gets(after_ref), samples, parts)
    for d, ref in enumerate((east_ref, west_ref)):
        ref[half : half + pairs] = own_ref[d]
        for i in range(half):
            ref[i] = sent[d][i]
            ref[half + pairs + i] = sent[d][half + i]


def main_kernel(y_ref, w_ref, before_ref, after_ref, x_ref, hy_ref, hw_ref, wh_ref, p_ref, q_ref):
    rows, samples, levels, cols = y_ref.shape
    high = rows + 2 * ITERS
    parts = lane_parts((levels, LANES))

    def halo(r):
        return (before_ref, r) if r < ITERS else (after_ref, r - ITERS - rows)

    def own(r):
        return ITERS <= r < ITERS + rows

    for r in range(high):
        if not own(r):
            ref, i = halo(r)
            slot = r if r < ITERS else r - rows
            w = [ref[i, samples + k] for k in range(3)]
            wh_ref[slot, 0] = centre_weight(w[0], w[1])
            for k in range(3):
                wh_ref[slot, 1 + k] = w[k]

    def get_w(r):
        if own(r):
            return [w_ref[r - ITERS, k] for k in range(4)]
        return [wh_ref[r if r < ITERS else r - rows, k] for k in range(4)]

    for side, ref in enumerate((before_ref, after_ref)):
        lines, weights = strips(halo_gets(ref), samples, parts)
        for i in range(ITERS):
            hy_ref[side * ITERS + i] = lines[i]
            for k in range(3):
                hw_ref[side * ITERS + i, k] = weights[i][k]

    def sample(s, carry):
        def first_y(r):
            ref, i = (y_ref, r - ITERS) if own(r) else halo(r)
            return ref[i, s]

        source = first_y
        for step in range(ITERS):
            target = (p_ref, q_ref)[step % 2]

            def put(r, v, target=target, step=step):
                if step == ITERS - 1:
                    x_ref[r - ITERS, s] = v
                else:
                    target[r, s] = v

            stencil(high, source, get_w, step + 1, high - 1 - step, put)
            source = functools.partial(lambda r, target: target[r, s], target=target)
        return carry

    lax.fori_loop(0, samples, sample, 0)


def strip_kernel(x_ref, w_ref, sy_ref, sw_ref, hy_ref, hw_ref, left_ref, right_ref, out_ref, var_ref, sum_ref):
    rows, samples, levels, cols = x_ref.shape
    high = rows + 2 * ITERS
    lane, seg, l32 = lane_parts((levels, LANES))
    from_left, from_right = l32 < 4, l32 >= 28

    def strip_at(r):
        if ITERS <= r < ITERS + rows:
            return sy_ref, sw_ref, r - ITERS
        return hy_ref, hw_ref, r if r < ITERS else r - rows

    def get_y(r):
        ref, _, i = strip_at(r)
        a, b = (left_ref[r // 2], roll(right_ref[r // 2], 16)) if r % 2 == 0 else (roll(left_ref[r // 2], -16), right_ref[r // 2])
        return jnp.where(from_left, a, jnp.where(from_right, b, ref[i]))

    def get_w(r):
        _, ref, i = strip_at(r)
        a, b = left_ref[r // 2], right_ref[r // 2]
        skip = (0, 16) if r % 2 == 0 else (16, 0)
        w = [
            jnp.where(
                from_left,
                roll(a, -4 * (k + 1) - skip[0]),
                jnp.where(from_right, roll(b, 4 * (k + 1) + skip[1]), ref[i, k]),
            )
            for k in range(3)
        ]
        return (centre_weight(w[0], w[1]), *w)

    weights = [get_w(r) for r in range(high)]
    field = {r: get_y(r) for r in range(high)}
    for step in range(ITERS):
        new = {}
        stencil(high, field.__getitem__, weights.__getitem__, step + 1, high - 1 - step, new.__setitem__)
        field = new

    total, count = None, None
    for r in range(rows):
        strip = field[ITERS + r]
        for c in range(0, cols, LANES):
            lanes = pl.ds(c, LANES)
            square = None
            for s in range(samples):
                v = x_ref[r, s, :, lanes]
                if c == 0:
                    v = jnp.where(lane < 4, roll(strip, -(SEG * s + 4)), v)
                if c == cols - LANES:
                    v = jnp.where(lane >= LANES - 4, roll(strip, LANES - SEG * s - 28), v)
                out_ref[r, s, :, lanes] = v
                square = v * v if square is None else square + v * v
            var = square / samples
            var_ref[r, :, lanes] = var
            m = jnp.where(w_ref[r, 1, :, lanes] > 0, 1.0, 0.0)
            total = m * var if total is None else total + m * var
            count = m if count is None else count + m
    sum_ref[0:1] = jnp.sum(total, axis=0, keepdims=True)
    sum_ref[1:2] = jnp.sum(count, axis=0, keepdims=True)


def scale_kernel(x_ref, w_ref, var_ref, all_ref, out_ref, mean_ref, stage, sem):
    rows, samples, levels, cols = x_ref.shape
    sums = jnp.sum(jnp.sum(all_ref[...], axis=0), axis=1, keepdims=True)
    mean = sums[0:1] / sums[1:2]
    mean_ref[...] = mean
    copies = []
    for c in range(cols // LANES):
        lanes = pl.ds(c * LANES, LANES)
        factors = []
        for r in range(rows):
            wet = w_ref[r, 1, :, lanes] > 0
            safe = jnp.where(wet, var_ref[r, :, lanes], 1.0)
            factors.append(jnp.where(wet, jnp.sqrt(mean / (safe + 1e-06)), 0.0))
        for s in range(samples):
            for r in range(rows):
                stage[c, s, pl.ds(r, levels, stride=rows)] = x_ref[r, s, :, lanes] * factors[r]
            copies.append(pltpu.make_async_copy(stage.at[c, s], out_ref.at[s, :, lanes], sem.at[c, s]))
            copies[-1].start()
    for copy in copies:
        copy.wait()


def call(kernel, out, *args, scratch=(), flops=0, in_space=None, out_space=None):
    out = [o if isinstance(o, jax.ShapeDtypeStruct) else jax.ShapeDtypeStruct(o, F32) for o in out]
    scratch = [pltpu.VMEM(o, F32) if isinstance(o, tuple) else o for o in scratch]
    return pl.pallas_call(
        kernel,
        out_shape=out,
        in_specs=[pl.BlockSpec(memory_space=in_space or pltpu.VMEM)] * len(args),
        out_specs=[pl.BlockSpec(memory_space=m) for m in out_space or [pltpu.VMEM] * len(out)],
        scratch_shapes=scratch,
        cost_estimate=pl.CostEstimate(flops=flops, bytes_accessed=sum(a.size * 4 for a in args), transcendentals=0),
        compiler_params=pltpu.CompilerParams(vmem_limit_bytes=12 << 20),
        name=kernel.__name__,
    )(*args)


def shards(noise, diff_lat, diff_lon, shear, sea_mask):
    samples, levels, rows, cols = noise.shape
    high = rows + 2 * ITERS
    flat = [noise.reshape(samples, levels * rows, cols)] + [
        a.reshape(levels * rows, cols) for a in (diff_lat, diff_lon, shear, sea_mask)
    ]
    n_lat, n_lon = lax.axis_size("lat"), lax.axis_size("lon")
    up = [(i, i + 1) for i in range(n_lat - 1)]
    down = [(j, i) for i, j in up]
    east = [(i, (i + 1) % n_lon) for i in range(n_lon)]
    west = [(j, i) for i, j in east]

    halo = (ITERS, samples + 3, levels, cols)
    tiles = cols // LANES
    plane = (tiles, levels * rows, LANES)
    flat = [pltpu.with_memory_space_constraint(a, pltpu.HBM) for a in flat]
    top, bottom, *staged = call(
        edge_kernel,
        [halo, halo, (tiles, samples, levels * rows, LANES)] + [plane] * 3 + [jax.ShapeDtypeStruct(plane, sea_mask.dtype)],
        *flat,
        scratch=[pltpu.SemaphoreType.DMA((tiles, 5))],
        in_space=pltpu.HBM,
    )
    after = lax.ppermute(top, "lat", down)
    before = lax.ppermute(bottom, "lat", up)
    y, w, own_msg, sy, sw = call(
        own_kernel,
        [(rows, samples, levels, cols), (rows, 4, levels, cols), (2, rows // 2, levels, LANES), (rows, levels, LANES), (rows, 3, levels, LANES)],
        *staged,
        flops=10**6,
    )
    message = (high // 2, levels, LANES)
    to_east, to_west = call(join_kernel, [message, message], own_msg, before, after)
    left = lax.ppermute(to_east, "lon", east)
    right = lax.ppermute(to_west, "lon", west)
    buffer = (high, samples, levels, cols)
    x, hy, hw = call(
        main_kernel,
        [y.shape, (2 * ITERS, levels, LANES), (2 * ITERS, 3, levels, LANES)],
        y,
        w,
        before,
        after,
        scratch=[(2 * ITERS, 4, levels, cols), buffer, buffer],
        flops=10**7,
    )
    x, var, part = call(
        strip_kernel, [y.shape, (rows, levels, cols), (2, LANES)], x, w, sy, sw, hy, hw, left, right
    )
    spread = jnp.broadcast_to(part, (n_lat * n_lon, 2, LANES))
    every = lax.all_to_all(spread, ("lat", "lon"), 0, 0, tiled=True)
    out, mean = call(
        scale_kernel,
        [(samples, levels * rows, cols), (1, 1)],
        x,
        w,
        var,
        every,
        scratch=[(tiles, samples, levels * rows, LANES), pltpu.SemaphoreType.DMA((tiles, samples))],
        out_space=[pl.ANY, pltpu.VMEM],
    )
    return out.reshape(noise.shape), mean.reshape(())


def solution(mesh):
    grid = P(None, "lat", "lon")
    field = P(None, None, "lat", "lon")
    return jax.shard_map(
        shards,
        mesh=mesh,
        in_specs=(field, grid, grid, grid, grid),
        out_specs=(field, P()),
        check_vma=False,
    )
```

```python
import functools

import jax
import jax.numpy as jnp
from jax import lax
from jax.experimental import pallas as pl
from jax.experimental.pallas import tpu as pltpu
from jax.sharding import PartitionSpec as P

ITERS = 4
LANES = 128
SEG = 32
F32 = jnp.float32


def cell_weights(k11, k22, shear, mask):
    m = mask.astype(F32)
    return m * k11, m * k22, m * (0.5 * (shear * jnp.sqrt(k11 * k22)))


def centre_weight(wa, wb):
    return jnp.where(wa > 0, 1.0, 0.0) - 2.0 * (wa + wb)


def roll(x, shift):
    n = x.shape[-1]
    shift = shift % n
    return x if shift == 0 else pltpu.roll(x, shift, x.ndim - 1)


def lane_parts(shape):
    lane = lax.broadcasted_iota(jnp.int32, shape, 1)
    return lane, lane // SEG, lane % SEG


def stencil(rows, get_y, get_w, first, last, put):
    def products(r):
        y = get_y(r)
        w0, wa, wb, wc = get_w(r)
        return w0 * y, wa * y, wb * y, wc * y

    prev, here = products(first - 1), products(first)
    for r in range(first, last):
        after = products(r + 1)
        d, _, b, _ = here
        g = prev[3] - after[3]
        put(r, d + (prev[1] + after[1]) + roll(b + g, 1) + roll(b - g, -1))
        prev, here = here, after


def odd_row_block():
    return lax.rem(lax.axis_index("lat"), 2)


def halo_slots():
    odd = odd_row_block()
    return (1 - odd) * ITERS, odd * ITERS


def edge_kernel(n_ref, a_ref, b_ref, s_ref, m_ref, near_ref, far_ref, n_to, a_to, b_to, s_to, m_to, sem):
    samples, levels, tiles = n_ref.shape[0], near_ref.shape[2], n_to.shape[0]
    rows = n_ref.shape[1] // levels
    copies = []
    for c in range(tiles):
        lanes = pl.ds(c * LANES, LANES)
        for k, (ref, to) in enumerate(((a_ref, a_to), (b_ref, b_to), (s_ref, s_to), (m_ref, m_to))):
            copies.append(pltpu.make_async_copy(ref.at[:, lanes], to.at[c], sem.at[c, k]))
        copies.append(pltpu.make_async_copy(n_ref.at[:, :, lanes], n_to.at[c], sem.at[c, 4]))
    for copy in copies:
        copy.start()
    for copy in copies:
        copy.wait()
    near_first = (1 - odd_row_block()) * (rows - ITERS)
    for i in range(ITERS):
        for out, r in ((near_ref, near_first + i), (far_ref, rows - ITERS - near_first + i)):
            at = pl.ds(r, levels, stride=rows)
            for c in range(tiles):
                lanes = pl.ds(c * LANES, LANES)
                for s in range(samples):
                    out[i, s, :, lanes] = n_to[c, s, at]
                w = cell_weights(a_to[c, at], b_to[c, at], s_to[c, at], m_to[c, at])
                for k in range(3):
                    out[i, samples + k, :, lanes] = w[k]


BATCH = 4


def replicate(values, seg):
    turned = [roll(v, SEG) for v in values]
    values = [jnp.where(seg == 1, t, v) for t, v in zip(turned, values)]
    turned = [roll(v, 2 * SEG) for v in values]
    return [jnp.where(seg >= 2, t, v) for t, v in zip(turned, values)]


def line_up(gets, samples, parts, low, high):
    _, seg, l32 = parts
    turned = [
        [(roll(get(s, low), SEG * s + 4), roll(get(s, high), SEG * s + 28)) for s in range(samples)] for get in gets
    ]
    lines = []
    for row in turned:
        line = None
        for s, (a, b) in enumerate(row):
            v = jnp.where(l32 < SEG // 2, a, b)
            line = v if line is None else jnp.where(seg == s, v, line)
        lines.append(line)
    return lines


def messages(gets, samples, parts):
    _, seg, l32 = parts
    lines = line_up(gets, samples, parts, 1, 0)
    turned = [
        [(roll(get(samples + k, 1), 4 * k + 8), roll(get(samples + k, 0), 24 - 4 * k)) for k in range(3)] for get in gets
    ]
    packed = []
    for row in turned:
        line = None
        for k, (a, b) in enumerate(row):
            v = jnp.where(l32 < SEG // 2, a, b)
            line = v if line is None else jnp.where((l32 // 4 == k + 1) | (l32 // 4 == 6 - k), v, line)
        packed.append(line)
    packed = replicate(packed, seg)
    both = [jnp.where((l32 < 4) | (l32 >= 28), a, b) for a, b in zip(lines, packed)]
    east, west = [], []
    for a, b in zip(both[0::2], both[1::2]):
        east.append(jnp.where(l32 < SEG // 2, a, roll(b, SEG // 2)))
        west.append(jnp.where(l32 < SEG // 2, roll(a, -SEG // 2), b))
    return east, west


def strips(gets, samples, parts):
    _, seg, l32 = parts
    lines = line_up(gets, samples, parts, 0, 1)
    turned = [(roll(get(samples + k, 0), 4), roll(get(samples + k, 1), 28)) for get in gets for k in range(3)]
    weights = replicate([jnp.where(l32 < SEG // 2, a, b) for a, b in turned], seg)
    return lines, [weights[3 * i : 3 * i + 3] for i in range(len(gets))]


def own_kernel(n_ref, a_ref, b_ref, s_ref, m_ref, y_ref, w_ref, msg_ref, sy_ref, sw_ref):
    rows, samples, levels, cols = y_ref.shape
    parts = lane_parts((levels, LANES))
    tiles = cols // LANES

    def read(r):
        at = pl.ds(r, levels, stride=rows)
        return [
            [n_ref[c, s, at] for s in range(samples)]
            + list(cell_weights(a_ref[c, at], b_ref[c, at], s_ref[c, at], m_ref[c, at]))
            for c in range(tiles)
        ]

    for first in range(0, rows, BATCH):
        batch = range(first, first + BATCH)
        data = [read(r) for r in batch]
        gets = [lambda g, side, row=row: row[side * (tiles - 1)][g] for row in data]
        east, west = messages(gets, samples, parts)
        for i in range(BATCH // 2):
            msg_ref[0, first // 2 + i] = east[i]
            msg_ref[1, first // 2 + i] = west[i]
        lines, weights = strips(gets, samples, parts)
        for i, r in enumerate(batch):
            for c in range(tiles):
                lanes = pl.ds(c * LANES, LANES)
                values = data[i][c]
                for s in range(samples):
                    y_ref[r, s, :, lanes] = values[s]
                w_ref[r, 0, :, lanes] = centre_weight(values[samples], values[samples + 1])
                for k in range(3):
                    w_ref[r, 1 + k, :, lanes] = values[samples + k]
            sy_ref[r] = lines[i]
            for k in range(3):
                sw_ref[r, k] = weights[i][k]


def halo_gets(ref):
    last = ref.shape[3] - LANES
    return [lambda g, side, i=i: ref[i, g, :, pl.ds(side * last, LANES)] for i in range(ITERS)]


def join_kernel(own_ref, near_ref, far_ref, east_ref, west_ref):
    pairs, half = own_ref.shape[1], ITERS // 2
    samples = near_ref.shape[1] - 3
    parts = lane_parts(own_ref.shape[2:])
    sent = messages(halo_gets(near_ref) + halo_gets(far_ref), samples, parts)
    for d, ref in enumerate((east_ref, west_ref)):
        ref[half : half + pairs] = own_ref[d]
        for n, slot in enumerate(halo_slots()):
            at = lax.div(slot, ITERS) * (half + pairs)
            for i in range(half):
                ref[at + i] = sent[d][n * half + i]


def main_kernel(y_ref, w_ref, near_ref, far_ref, x_ref, hy_ref, hw_ref, yh_ref, wh_ref, p_ref, q_ref):
    rows, samples, levels, cols = y_ref.shape
    high = rows + 2 * ITERS
    parts = lane_parts((levels, LANES))

    def own(r):
        return ITERS <= r < ITERS + rows

    def pick(r, own_ref, halo_ref):
        if own(r):
            return own_ref, r - ITERS
        return halo_ref, r if r < ITERS else r - rows

    for ref, slot in zip((near_ref, far_ref), halo_slots()):
        lines, weights = strips(halo_gets(ref), samples, parts)
        for i in range(ITERS):
            hy_ref[slot + i] = lines[i]
            for k in range(3):
                hw_ref[slot + i, k] = weights[i][k]
            for s in range(samples):
                yh_ref[slot + i, s] = ref[i, s]
            w = [ref[i, samples + k] for k in range(3)]
            wh_ref[slot + i, 0] = centre_weight(w[0], w[1])
            for k in range(3):
                wh_ref[slot + i, 1 + k] = w[k]

    def get_w(r):
        ref, i = pick(r, w_ref, wh_ref)
        return [ref[i, k] for k in range(4)]

    def sample(s, carry):
        def first_y(r):
            ref, i = pick(r, y_ref, yh_ref)
            return ref[i, s]

        source = first_y
        for step in range(ITERS):
            target = (p_ref, q_ref)[step % 2]

            def put(r, v, target=target, step=step):
                if step == ITERS - 1:
                    x_ref[r - ITERS, s] = v
                else:
                    target[r, s] = v

            stencil(high, source, get_w, step + 1, high - 1 - step, put)
            source = functools.partial(lambda r, target: target[r, s], target=target)
        return carry

    lax.fori_loop(0, samples, sample, 0)


def strip_kernel(x_ref, w_ref, sy_ref, sw_ref, hy_ref, hw_ref, left_ref, right_ref, out_ref, var_ref, sum_ref):
    rows, samples, levels, cols = x_ref.shape
    high = rows + 2 * ITERS
    lane, seg, l32 = lane_parts((levels, LANES))
    from_left, from_right = l32 < 4, l32 >= 28

    def strip_at(r):
        if ITERS <= r < ITERS + rows:
            return sy_ref, sw_ref, r - ITERS
        return hy_ref, hw_ref, r if r < ITERS else r - rows

    def get_y(r):
        ref, _, i = strip_at(r)
        a, b = (left_ref[r // 2], roll(right_ref[r // 2], 16)) if r % 2 == 0 else (roll(left_ref[r // 2], -16), right_ref[r // 2])
        return jnp.where(from_left, a, jnp.where(from_right, b, ref[i]))

    def get_w(r):
        _, ref, i = strip_at(r)
        a, b = left_ref[r // 2], right_ref[r // 2]
        skip = (0, 16) if r % 2 == 0 else (16, 0)
        w = [
            jnp.where(
                from_left,
                roll(a, -4 * (k + 1) - skip[0]),
                jnp.where(from_right, roll(b, 4 * (k + 1) + skip[1]), ref[i, k]),
            )
            for k in range(3)
        ]
        return (centre_weight(w[0], w[1]), *w)

    weights = [get_w(r) for r in range(high)]
    field = {r: get_y(r) for r in range(high)}
    for step in range(ITERS):
        new = {}
        stencil(high, field.__getitem__, weights.__getitem__, step + 1, high - 1 - step, new.__setitem__)
        field = new

    total, count = None, None
    for r in range(rows):
        strip = field[ITERS + r]
        for c in range(0, cols, LANES):
            lanes = pl.ds(c, LANES)
            square = None
            for s in range(samples):
                v = x_ref[r, s, :, lanes]
                if c == 0:
                    v = jnp.where(lane < 4, roll(strip, -(SEG * s + 4)), v)
                if c == cols - LANES:
                    v = jnp.where(lane >= LANES - 4, roll(strip, LANES - SEG * s - 28), v)
                out_ref[r, s, :, lanes] = v
                square = v * v if square is None else square + v * v
            var = square / samples
            var_ref[r, :, lanes] = var
            m = jnp.where(w_ref[r, 1, :, lanes] > 0, 1.0, 0.0)
            total = m * var if total is None else total + m * var
            count = m if count is None else count + m
    sum_ref[0:1] = jnp.sum(total, axis=0, keepdims=True)
    sum_ref[1:2] = jnp.sum(count, axis=0, keepdims=True)


def scale_kernel(x_ref, w_ref, var_ref, all_ref, out_ref, mean_ref, stage, sem):
    rows, samples, levels, cols = x_ref.shape
    sums = jnp.sum(jnp.sum(all_ref[...], axis=0), axis=1, keepdims=True)
    mean = sums[0:1] / sums[1:2]
    mean_ref[...] = mean
    copies = []
    for c in range(cols // LANES):
        lanes = pl.ds(c * LANES, LANES)
        factors = []
        for r in range(rows):
            wet = w_ref[r, 1, :, lanes] > 0
            safe = jnp.where(wet, var_ref[r, :, lanes], 1.0)
            factors.append(jnp.where(wet, jnp.sqrt(mean / (safe + 1e-06)), 0.0))
        for s in range(samples):
            for r in range(rows):
                stage[c, s, pl.ds(r, levels, stride=rows)] = x_ref[r, s, :, lanes] * factors[r]
            copies.append(pltpu.make_async_copy(stage.at[c, s], out_ref.at[s, :, lanes], sem.at[c, s]))
            copies[-1].start()
    for copy in copies:
        copy.wait()


def call(kernel, out, *args, scratch=(), flops=0, in_space=None, out_space=None):
    out = [o if isinstance(o, jax.ShapeDtypeStruct) else jax.ShapeDtypeStruct(o, F32) for o in out]
    scratch = [pltpu.VMEM(o, F32) if isinstance(o, tuple) else o for o in scratch]
    return pl.pallas_call(
        kernel,
        out_shape=out,
        in_specs=[pl.BlockSpec(memory_space=in_space or pltpu.VMEM)] * len(args),
        out_specs=[pl.BlockSpec(memory_space=m) for m in out_space or [pltpu.VMEM] * len(out)],
        scratch_shapes=scratch,
        cost_estimate=pl.CostEstimate(flops=flops, bytes_accessed=sum(a.size * 4 for a in args), transcendentals=0),
        compiler_params=pltpu.CompilerParams(vmem_limit_bytes=12 << 20),
        name=kernel.__name__,
    )(*args)


def shards(noise, diff_lat, diff_lon, shear, sea_mask):
    samples, levels, rows, cols = noise.shape
    high = rows + 2 * ITERS
    flat = [noise.reshape(samples, levels * rows, cols)] + [
        a.reshape(levels * rows, cols) for a in (diff_lat, diff_lon, shear, sea_mask)
    ]
    n_lat, n_lon = lax.axis_size("lat"), lax.axis_size("lon")
    pair = [(i, i ^ 1) for i in range(n_lat)]
    across = [(i, i - 1 if i % 2 == 0 else i + 1) for i in range(1, n_lat - 1)]
    east = [(i, (i + 1) % n_lon) for i in range(n_lon)]
    west = [(j, i) for i, j in east]

    halo = (ITERS, samples + 3, levels, cols)
    tiles = cols // LANES
    plane = (tiles, levels * rows, LANES)
    flat = [pltpu.with_memory_space_constraint(a, pltpu.HBM) for a in flat]
    to_near, to_far, *staged = call(
        edge_kernel,
        [halo, halo, (tiles, samples, levels * rows, LANES)] + [plane] * 3 + [jax.ShapeDtypeStruct(plane, sea_mask.dtype)],
        *flat,
        scratch=[pltpu.SemaphoreType.DMA((tiles, 5))],
        in_space=pltpu.HBM,
    )
    far = lax.ppermute(to_far, "lat", across)
    near = lax.ppermute(to_near, "lat", pair)
    y, w, own_msg, sy, sw = call(
        own_kernel,
        [(rows, samples, levels, cols), (rows, 4, levels, cols), (2, rows // 2, levels, LANES), (rows, levels, LANES), (rows, 3, levels, LANES)],
        *staged,
        flops=10**6,
    )
    message = (high // 2, levels, LANES)
    to_east, to_west = call(join_kernel, [message, message], own_msg, near, far)
    left = lax.ppermute(to_east, "lon", east)
    right = lax.ppermute(to_west, "lon", west)
    buffer = (high, samples, levels, cols)
    x, hy, hw = call(
        main_kernel,
        [y.shape, (2 * ITERS, levels, LANES), (2 * ITERS, 3, levels, LANES)],
        y,
        w,
        near,
        far,
        scratch=[(2 * ITERS, samples, levels, cols), (2 * ITERS, 4, levels, cols), buffer, buffer],
        flops=10**7,
    )
    x, var, part = call(
        strip_kernel, [y.shape, (rows, levels, cols), (2, LANES)], x, w, sy, sw, hy, hw, left, right
    )
    spread = jnp.broadcast_to(part, (n_lat * n_lon, 2, LANES))
    every = lax.all_to_all(spread, ("lat", "lon"), 0, 0, tiled=True)
    out, mean = call(
        scale_kernel,
        [(samples, levels * rows, cols), (1, 1)],
        x,
        w,
        var,
        every,
        scratch=[(tiles, samples, levels * rows, LANES), pltpu.SemaphoreType.DMA((tiles, samples))],
        out_space=[pl.ANY, pltpu.VMEM],
    )
    return out.reshape(noise.shape), mean.reshape(())


def solution(mesh):
    grid = P(None, "lat", "lon")
    field = P(None, None, "lat", "lon")
    return jax.shard_map(
        shards,
        mesh=mesh,
        in_specs=(field, grid, grid, grid, grid),
        out_specs=(field, P()),
        check_vma=False,
    )
```

```python
import functools

import jax
import jax.numpy as jnp
from jax import lax
from jax.experimental import pallas as pl
from jax.experimental.pallas import tpu as pltpu
from jax.sharding import PartitionSpec as P

ITERS = 4
LANES = 128
SEG = 32
F32 = jnp.float32


def cell_weights(k11, k22, shear, mask):
    m = mask.astype(F32)
    return m * k11, m * k22, m * (0.5 * (shear * jnp.sqrt(k11 * k22)))


def centre_weight(wa, wb):
    return jnp.where(wa > 0, 1.0, 0.0) - 2.0 * (wa + wb)


def roll(x, shift):
    n = x.shape[-1]
    shift = shift % n
    return x if shift == 0 else pltpu.roll(x, shift, x.ndim - 1)


def lane_parts(shape):
    lane = lax.broadcasted_iota(jnp.int32, shape, 1)
    return lane, lane // SEG, lane % SEG


def stencil(get_y, get_w, first, last, put):
    def products(r):
        y = get_y(r)
        w0, wa, wb, wc = get_w(r)
        return w0 * y, wa * y, wb * y, wc * y

    prev, here = products(first - 1), products(first)
    for r in range(first, last):
        after = products(r + 1)
        d, _, b, _ = here
        g = prev[3] - after[3]
        put(r, d + (prev[1] + after[1]) + roll(b + g, 1) + roll(b - g, -1))
        prev, here = here, after


def odd_row_block():
    return lax.rem(lax.axis_index("lat"), 2)


def halo_slots():
    odd = odd_row_block()
    return (1 - odd) * ITERS, odd * ITERS


def edge_kernel(n_ref, a_ref, b_ref, s_ref, m_ref, near_ref, far_ref, corner_ref, n_to, a_to, b_to, s_to, m_to, sem):
    samples, levels, tiles = n_ref.shape[0], near_ref.shape[2], n_to.shape[0]
    rows = n_ref.shape[1] // levels
    copies = []
    for c in range(tiles):
        lanes = pl.ds(c * LANES, LANES)
        for k, (ref, to) in enumerate(((a_ref, a_to), (b_ref, b_to), (s_ref, s_to), (m_ref, m_to))):
            copies.append(pltpu.make_async_copy(ref.at[:, lanes], to.at[c], sem.at[c, k]))
        copies.append(pltpu.make_async_copy(n_ref.at[:, :, lanes], n_to.at[c], sem.at[c, 4]))
    for copy in copies:
        copy.start()
    for copy in copies:
        copy.wait()
    near_first = (1 - odd_row_block()) * (rows - ITERS)
    for i in range(ITERS):
        for out, r in ((near_ref, near_first + i), (far_ref, rows - ITERS - near_first + i)):
            at = pl.ds(r, levels, stride=rows)
            for c in range(tiles):
                lanes = pl.ds(c * LANES, LANES)
                for s in range(samples):
                    out[i, s, :, lanes] = n_to[c, s, at]
                w = cell_weights(a_to[c, at], b_to[c, at], s_to[c, at], m_to[c, at])
                for k in range(3):
                    out[i, samples + k, :, lanes] = w[k]
    sent = messages(halo_gets(far_ref), samples, lane_parts((levels, LANES)))
    for d in range(2):
        for i in range(ITERS // 2):
            corner_ref[d, i] = sent[d][i]


BATCH = 4


def replicate(values, seg):
    turned = [roll(v, SEG) for v in values]
    values = [jnp.where(seg == 1, t, v) for t, v in zip(turned, values)]
    turned = [roll(v, 2 * SEG) for v in values]
    return [jnp.where(seg >= 2, t, v) for t, v in zip(turned, values)]


def line_up(gets, samples, parts, low, high):
    _, seg, l32 = parts
    turned = [
        [(roll(get(s, low), SEG * s + 4), roll(get(s, high), SEG * s + 28)) for s in range(samples)] for get in gets
    ]
    lines = []
    for row in turned:
        line = None
        for s, (a, b) in enumerate(row):
            v = jnp.where(l32 < SEG // 2, a, b)
            line = v if line is None else jnp.where(seg == s, v, line)
        lines.append(line)
    return lines


def messages(gets, samples, parts):
    _, seg, l32 = parts
    lines = line_up(gets, samples, parts, 1, 0)
    turned = [
        [(roll(get(samples + k, 1), 4 * k + 8), roll(get(samples + k, 0), 24 - 4 * k)) for k in range(3)] for get in gets
    ]
    packed = []
    for row in turned:
        line = None
        for k, (a, b) in enumerate(row):
            v = jnp.where(l32 < SEG // 2, a, b)
            line = v if line is None else jnp.where((l32 // 4 == k + 1) | (l32 // 4 == 6 - k), v, line)
        packed.append(line)
    packed = replicate(packed, seg)
    both = [jnp.where((l32 < 4) | (l32 >= 28), a, b) for a, b in zip(lines, packed)]
    east, west = [], []
    for a, b in zip(both[0::2], both[1::2]):
        east.append(jnp.where(l32 < SEG // 2, a, roll(b, SEG // 2)))
        west.append(jnp.where(l32 < SEG // 2, roll(a, -SEG // 2), b))
    return east, west


def strips(gets, samples, parts):
    _, seg, l32 = parts
    lines = line_up(gets, samples, parts, 0, 1)
    turned = [(roll(get(samples + k, 0), 4), roll(get(samples + k, 1), 28)) for get in gets for k in range(3)]
    weights = replicate([jnp.where(l32 < SEG // 2, a, b) for a, b in turned], seg)
    return lines, [weights[3 * i : 3 * i + 3] for i in range(len(gets))]


def own_row(refs, r, rows, levels):
    n_ref, a_ref, b_ref, s_ref, m_ref = refs
    at = pl.ds(r, levels, stride=rows)
    return [
        [n_ref[c, s, at] for s in range(n_ref.shape[1])]
        + list(cell_weights(a_ref[c, at], b_ref[c, at], s_ref[c, at], m_ref[c, at]))
        for c in range(n_ref.shape[0])
    ]


def own_gets(data):
    return [lambda g, side, row=row: row[-side][g] for row in data]


def message_kernel(*refs):
    refs, msg_ref = refs[:-1], refs[-1]
    levels = msg_ref.shape[2]
    rows, samples = refs[0].shape[2] // levels, refs[0].shape[1]
    parts = lane_parts((levels, LANES))
    for first in range(0, rows, BATCH):
        data = [own_row(refs, r, rows, levels) for r in range(first, first + BATCH)]
        sent = messages(own_gets(data), samples, parts)
        for d in range(2):
            for i in range(BATCH // 2):
                msg_ref[d, first // 2 + i] = sent[d][i]


def own_kernel(n_ref, a_ref, b_ref, s_ref, m_ref, y_ref, w_ref, sy_ref, sw_ref):
    rows, samples, levels, _ = y_ref.shape
    parts = lane_parts((levels, LANES))
    for first in range(0, rows, BATCH):
        batch = range(first, first + BATCH)
        data = [own_row((n_ref, a_ref, b_ref, s_ref, m_ref), r, rows, levels) for r in batch]
        lines, weights = strips(own_gets(data), samples, parts)
        for i, r in enumerate(batch):
            for c, values in enumerate(data[i]):
                lanes = pl.ds(c * LANES, LANES)
                for s in range(samples):
                    y_ref[r, s, :, lanes] = values[s]
                w_ref[r, 0, :, lanes] = centre_weight(values[samples], values[samples + 1])
                for k in range(3):
                    w_ref[r, 1 + k, :, lanes] = values[samples + k]
            sy_ref[r] = lines[i]
            for k in range(3):
                sw_ref[r, k] = weights[i][k]


def halo_gets(ref):
    last = ref.shape[3] - LANES
    return [lambda g, side, i=i: ref[i, g, :, pl.ds(side * last, LANES)] for i in range(ITERS)]


def join_kernel(own_ref, near_ref, corner_ref, east_ref, west_ref):
    pairs, half = own_ref.shape[1], ITERS // 2
    sent = messages(halo_gets(near_ref), near_ref.shape[1] - 3, lane_parts(own_ref.shape[2:]))
    near, far = [lax.div(slot, ITERS) * (half + pairs) for slot in halo_slots()]
    for d, ref in enumerate((east_ref, west_ref)):
        ref[half : half + pairs] = own_ref[d]
        for i in range(half):
            ref[near + i] = sent[d][i]
            ref[far + i] = corner_ref[d, i]


def main_kernel(y_ref, w_ref, near_ref, far_ref, x_ref, hy_ref, hw_ref, yh_ref, wh_ref, p_ref, q_ref):
    rows, samples, levels, _ = y_ref.shape
    high = rows + 2 * ITERS
    parts = lane_parts((levels, LANES))

    def own(r):
        return ITERS <= r < ITERS + rows

    def pick(r, own_ref, halo_ref):
        if own(r):
            return own_ref, r - ITERS
        return halo_ref, r if r < ITERS else r - rows

    for ref, slot in zip((near_ref, far_ref), halo_slots()):
        lines, weights = strips(halo_gets(ref), samples, parts)
        for i in range(ITERS):
            hy_ref[slot + i] = lines[i]
            for k in range(3):
                hw_ref[slot + i, k] = weights[i][k]
            for s in range(samples):
                yh_ref[slot + i, s] = ref[i, s]
            w = [ref[i, samples + k] for k in range(3)]
            wh_ref[slot + i, 0] = centre_weight(w[0], w[1])
            for k in range(3):
                wh_ref[slot + i, 1 + k] = w[k]

    def get_w(r):
        ref, i = pick(r, w_ref, wh_ref)
        return [ref[i, k] for k in range(4)]

    def sample(s, carry):
        def first_y(r):
            ref, i = pick(r, y_ref, yh_ref)
            return ref[i, s]

        source = first_y
        for step in range(ITERS):
            target = (p_ref, q_ref)[step % 2]

            def put(r, v, target=target, step=step):
                if step == ITERS - 1:
                    x_ref[r - ITERS, s] = v
                else:
                    target[r, s] = v

            stencil(source, get_w, step + 1, high - 1 - step, put)
            source = functools.partial(lambda r, target: target[r, s], target=target)
        return carry

    lax.fori_loop(0, samples, sample, 0)


def strip_kernel(x_ref, w_ref, sy_ref, sw_ref, hy_ref, hw_ref, left_ref, right_ref, out_ref, var_ref, sum_ref):
    rows, samples, levels, cols = x_ref.shape
    high = rows + 2 * ITERS
    lane, _, l32 = lane_parts((levels, LANES))
    from_left, from_right = l32 < 4, l32 >= 28

    def strip_at(r):
        if ITERS <= r < ITERS + rows:
            return sy_ref, sw_ref, r - ITERS
        return hy_ref, hw_ref, r if r < ITERS else r - rows

    def get_y(r):
        ref, _, i = strip_at(r)
        a, b = (left_ref[r // 2], roll(right_ref[r // 2], 16)) if r % 2 == 0 else (roll(left_ref[r // 2], -16), right_ref[r // 2])
        return jnp.where(from_left, a, jnp.where(from_right, b, ref[i]))

    def get_w(r):
        _, ref, i = strip_at(r)
        a, b = left_ref[r // 2], right_ref[r // 2]
        skip = (0, 16) if r % 2 == 0 else (16, 0)
        w = [
            jnp.where(
                from_left,
                roll(a, -4 * (k + 1) - skip[0]),
                jnp.where(from_right, roll(b, 4 * (k + 1) + skip[1]), ref[i, k]),
            )
            for k in range(3)
        ]
        return (centre_weight(w[0], w[1]), *w)

    weights = [get_w(r) for r in range(high)]
    field = {r: get_y(r) for r in range(high)}
    for step in range(ITERS):
        new = {}
        stencil(field.__getitem__, weights.__getitem__, step + 1, high - 1 - step, new.__setitem__)
        field = new

    total, count = None, None
    for r in range(rows):
        strip = field[ITERS + r]
        for c in range(0, cols, LANES):
            lanes = pl.ds(c, LANES)
            square = None
            for s in range(samples):
                v = x_ref[r, s, :, lanes]
                if c == 0:
                    v = jnp.where(lane < 4, roll(strip, -(SEG * s + 4)), v)
                if c == cols - LANES:
                    v = jnp.where(lane >= LANES - 4, roll(strip, LANES - SEG * s - 28), v)
                out_ref[r, s, :, lanes] = v
                square = v * v if square is None else square + v * v
            var = square / samples
            var_ref[r, :, lanes] = var
            m = jnp.where(w_ref[r, 1, :, lanes] > 0, 1.0, 0.0)
            total = m * var if total is None else total + m * var
            count = m if count is None else count + m
    sum_ref[0:1] = jnp.sum(total, axis=0, keepdims=True)
    sum_ref[1:2] = jnp.sum(count, axis=0, keepdims=True)


def scale_kernel(x_ref, w_ref, var_ref, all_ref, out_ref, mean_ref, stage, sem):
    rows, samples, levels, cols = x_ref.shape
    sums = jnp.sum(jnp.sum(all_ref[...], axis=0), axis=1, keepdims=True)
    mean = sums[0:1] / sums[1:2]
    mean_ref[...] = mean
    copies = []
    for c in range(cols // LANES):
        lanes = pl.ds(c * LANES, LANES)
        factors = []
        for r in range(rows):
            wet = w_ref[r, 1, :, lanes] > 0
            safe = jnp.where(wet, var_ref[r, :, lanes], 1.0)
            factors.append(jnp.where(wet, jnp.sqrt(mean / (safe + 1e-06)), 0.0))
        for s in range(samples):
            for r in range(rows):
                stage[c, s, pl.ds(r, levels, stride=rows)] = x_ref[r, s, :, lanes] * factors[r]
            copies.append(pltpu.make_async_copy(stage.at[c, s], out_ref.at[s, :, lanes], sem.at[c, s]))
            copies[-1].start()
    for copy in copies:
        copy.wait()


def call(kernel, out, *args, scratch=(), flops=0, in_space=None, out_space=None):
    out = [o if isinstance(o, jax.ShapeDtypeStruct) else jax.ShapeDtypeStruct(o, F32) for o in out]
    scratch = [pltpu.VMEM(o, F32) if isinstance(o, tuple) else o for o in scratch]
    return pl.pallas_call(
        kernel,
        out_shape=out,
        in_specs=[pl.BlockSpec(memory_space=in_space or pltpu.VMEM)] * len(args),
        out_specs=[pl.BlockSpec(memory_space=m) for m in out_space or [pltpu.VMEM] * len(out)],
        scratch_shapes=scratch,
        cost_estimate=pl.CostEstimate(flops=flops, bytes_accessed=sum(a.size * 4 for a in args), transcendentals=0),
        compiler_params=pltpu.CompilerParams(vmem_limit_bytes=12 << 20),
    )(*args)


def shards(noise, diff_lat, diff_lon, shear, sea_mask):
    samples, levels, rows, cols = noise.shape
    high = rows + 2 * ITERS
    flat = [noise.reshape(samples, levels * rows, cols)] + [
        a.reshape(levels * rows, cols) for a in (diff_lat, diff_lon, shear, sea_mask)
    ]
    n_lat, n_lon = lax.axis_size("lat"), lax.axis_size("lon")
    pair = [(i, i ^ 1) for i in range(n_lat)]
    across = [(i, i - 1 if i % 2 == 0 else i + 1) for i in range(1, n_lat - 1)]
    east = [(i, (i + 1) % n_lon) for i in range(n_lon)]
    west = [(j, i) for i, j in east]

    halo = (ITERS, samples + 3, levels, cols)
    tiles = cols // LANES
    plane = (tiles, levels * rows, LANES)
    flat = [pltpu.with_memory_space_constraint(a, pltpu.HBM) for a in flat]
    to_near, to_far, to_corner, *staged = call(
        edge_kernel,
        [halo, halo, (2, ITERS // 2, levels, LANES), (tiles, samples, levels * rows, LANES)] + [plane] * 3 + [jax.ShapeDtypeStruct(plane, sea_mask.dtype)],
        *flat,
        scratch=[pltpu.SemaphoreType.DMA((tiles, 5))],
        in_space=pltpu.HBM,
    )
    near = lax.ppermute(to_near, "lat", pair)
    corner = lax.ppermute(to_corner, "lat", across)
    far = lax.ppermute(to_far, "lat", across)
    (own_msg,) = call(message_kernel, [(2, rows // 2, levels, LANES)], *staged, flops=10**6)
    message = (high // 2, levels, LANES)
    to_east, to_west = call(join_kernel, [message, message], own_msg, near, corner)
    left = lax.ppermute(to_east, "lon", east)
    right = lax.ppermute(to_west, "lon", west)
    strip = (rows, levels, LANES)
    y, w, sy, sw = call(
        own_kernel,
        [(rows, samples, levels, cols), (rows, 4, levels, cols), strip, (rows, 3, levels, LANES)],
        *staged,
        flops=10**6,
    )
    buffer = (high, samples, levels, cols)
    x, hy, hw = call(
        main_kernel,
        [y.shape, (2 * ITERS, levels, LANES), (2 * ITERS, 3, levels, LANES)],
        y,
        w,
        near,
        far,
        scratch=[(2 * ITERS, samples, levels, cols), (2 * ITERS, 4, levels, cols), buffer, buffer],
        flops=10**7,
    )
    x, var, part = call(
        strip_kernel, [y.shape, (rows, levels, cols), (2, LANES)], x, w, sy, sw, hy, hw, left, right
    )
    spread = jnp.broadcast_to(part, (n_lat * n_lon, 2, LANES))
    every = lax.all_to_all(spread, ("lat", "lon"), 0, 0, tiled=True)
    out, mean = call(
        scale_kernel,
        [(samples, levels * rows, cols), (1, 1)],
        x,
        w,
        var,
        every,
        scratch=[(tiles, samples, levels * rows, LANES), pltpu.SemaphoreType.DMA((tiles, samples))],
        out_space=[pl.ANY, pltpu.VMEM],
    )
    return out.reshape(noise.shape), mean.reshape(())


def solution(mesh):
    grid = P(None, "lat", "lon")
    field = P(None, None, "lat", "lon")
    return jax.shard_map(
        shards,
        mesh=mesh,
        in_specs=(field, grid, grid, grid, grid),
        out_specs=(field, P()),
        check_vma=False,
    )
```

```python
import functools

import jax
import jax.numpy as jnp
from jax import lax
from jax.experimental import pallas as pl
from jax.experimental.pallas import tpu as pltpu
from jax.sharding import PartitionSpec as P

ITERS = 4
LANES = 128
SEG = 32
F32 = jnp.float32


def cell_weights(k11, k22, shear, mask):
    m = mask.astype(F32)
    return m * k11, m * k22, m * (0.5 * (shear * jnp.sqrt(k11 * k22)))


def centre_weight(wa, wb):
    return jnp.where(wa > 0, 1.0, 0.0) - 2.0 * (wa + wb)


def all_weights(w, sign):
    return centre_weight(w[0], w[1]), w[0], w[1], sign * w[2]


def roll(x, shift):
    n = x.shape[-1]
    shift = shift % n
    return x if shift == 0 else pltpu.roll(x, shift, x.ndim - 1)


def lane_parts(shape):
    lane = lax.broadcasted_iota(jnp.int32, shape, 1)
    return lane, lane // SEG, lane % SEG


def stencil(get_y, get_w, first, last, put):
    def products(r):
        y = get_y(r)
        w0, wa, wb, wc = get_w(r)
        return w0 * y, wa * y, wb * y, wc * y

    prev, here = products(first - 1), products(first)
    for r in range(first, last):
        after = products(r + 1)
        d, _, b, _ = here
        g = prev[3] - after[3]
        put(r, d + (prev[1] + after[1]) + roll(b + g, 1) + roll(b - g, -1))
        prev, here = here, after


def row_order(rows):
    odd = lax.rem(lax.axis_index("lat"), 2)
    step = 2 * odd - 1
    return lambda d: (1 - odd) * (rows - 1) + step * d, step.astype(F32)


def edge_kernel(n_ref, a_ref, b_ref, s_ref, m_ref, near_ref, far_ref, corner_ref, n_to, a_to, b_to, s_to, m_to, sem):
    samples, levels, tiles = n_ref.shape[0], near_ref.shape[2], n_to.shape[0]
    rows = n_ref.shape[1] // levels
    copies = []
    for c in range(tiles):
        lanes = pl.ds(c * LANES, LANES)
        for k, (ref, to) in enumerate(((a_ref, a_to), (b_ref, b_to), (s_ref, s_to), (m_ref, m_to))):
            copies.append(pltpu.make_async_copy(ref.at[:, lanes], to.at[c], sem.at[c, k]))
        copies.append(pltpu.make_async_copy(n_ref.at[:, :, lanes], n_to.at[c], sem.at[c, 4]))
    for copy in copies:
        copy.start()
    for copy in copies:
        copy.wait()
    row_at, _ = row_order(rows)
    for i in range(ITERS):
        for out, d in ((near_ref, ITERS - 1 - i), (far_ref, rows - 1 - i)):
            at = pl.ds(row_at(d), levels, stride=rows)
            for c in range(tiles):
                lanes = pl.ds(c * LANES, LANES)
                for s in range(samples):
                    out[i, s, :, lanes] = n_to[c, s, at]
                w = cell_weights(a_to[c, at], b_to[c, at], s_to[c, at], m_to[c, at])
                for k in range(3):
                    out[i, samples + k, :, lanes] = w[k]
    sent = messages(halo_gets(far_ref), samples, lane_parts((levels, LANES)))
    for d in range(2):
        for i in range(ITERS // 2):
            corner_ref[d, i] = sent[d][i]


BATCH = 4


def replicate(values, seg):
    turned = [roll(v, SEG) for v in values]
    values = [jnp.where(seg == 1, t, v) for t, v in zip(turned, values)]
    turned = [roll(v, 2 * SEG) for v in values]
    return [jnp.where(seg >= 2, t, v) for t, v in zip(turned, values)]


def line_up(gets, samples, parts, low, high):
    _, seg, l32 = parts
    turned = [
        [(roll(get(s, low), SEG * s + 4), roll(get(s, high), SEG * s + 28)) for s in range(samples)] for get in gets
    ]
    lines = []
    for row in turned:
        line = None
        for s, (a, b) in enumerate(row):
            v = jnp.where(l32 < SEG // 2, a, b)
            line = v if line is None else jnp.where(seg == s, v, line)
        lines.append(line)
    return lines


def messages(gets, samples, parts):
    lane, seg, l32 = parts
    left = lane < LANES // 2
    both = [[jnp.where(left, get(g, 0), get(g, 1)) for g in range(samples + 3)] for get in gets]
    lines = [[roll(row[s], SEG * s + 4) for s in range(samples)] for row in both]
    packed = [[roll(row[samples + k], 8 * k + 12) for k in range(3)] for row in both]
    packed = replicate([jnp.where(l32 < 16, a, jnp.where(l32 < 24, b, c)) for a, b, c in packed], seg)
    full = []
    for line, weights in zip(lines, packed):
        v = line[0]
        for s in range(1, samples):
            v = jnp.where(seg == s, line[s], v)
        full.append(jnp.where(l32 < 8, v, weights))
    low = lane % 8 < 4
    pairs = list(zip(full[0::2], full[1::2]))
    east = [jnp.where(low, a, roll(b, 4)) for a, b in pairs]
    west = [jnp.where(low, roll(a, -4), b) for a, b in pairs]
    return east, west


def strips(gets, samples, parts):
    _, seg, l32 = parts
    lines = line_up(gets, samples, parts, 0, 1)
    turned = [(roll(get(samples + k, 0), 4), roll(get(samples + k, 1), 28)) for get in gets for k in range(3)]
    weights = replicate([jnp.where(l32 < SEG // 2, a, b) for a, b in turned], seg)
    return lines, [weights[3 * i : 3 * i + 3] for i in range(len(gets))]


def own_row(refs, r, rows, levels):
    n_ref, a_ref, b_ref, s_ref, m_ref = refs
    at = pl.ds(row_order(rows)[0](r), levels, stride=rows)
    return [
        [n_ref[c, s, at] for s in range(n_ref.shape[1])]
        + list(cell_weights(a_ref[c, at], b_ref[c, at], s_ref[c, at], m_ref[c, at]))
        for c in range(n_ref.shape[0])
    ]


def own_gets(data):
    return [lambda g, side, row=row: row[-side][g] for row in data]


def message_kernel(*refs):
    refs, msg_ref = refs[:-1], refs[-1]
    levels = msg_ref.shape[2]
    rows, samples = refs[0].shape[2] // levels, refs[0].shape[1]
    parts = lane_parts((levels, LANES))
    for first in range(0, rows, BATCH):
        data = [own_row(refs, r, rows, levels) for r in range(first, first + BATCH)]
        sent = messages(own_gets(data), samples, parts)
        for d in range(2):
            for i in range(BATCH // 2):
                msg_ref[d, first // 2 + i] = sent[d][i]


def own_kernel(n_ref, a_ref, b_ref, s_ref, m_ref, y_ref, w_ref, sy_ref, sw_ref):
    rows, samples, levels, _ = y_ref.shape
    parts = lane_parts((levels, LANES))
    _, sign = row_order(rows)
    for first in range(0, rows, BATCH):
        batch = range(first, first + BATCH)
        data = [own_row((n_ref, a_ref, b_ref, s_ref, m_ref), r, rows, levels) for r in batch]
        lines, weights = strips(own_gets(data), samples, parts)
        for i, r in enumerate(batch):
            for c, values in enumerate(data[i]):
                lanes = pl.ds(c * LANES, LANES)
                for s in range(samples):
                    y_ref[r, s, :, lanes] = values[s]
                for k, v in enumerate(all_weights(values[samples:], sign)):
                    w_ref[r, k, :, lanes] = v
            sy_ref[r] = lines[i]
            for k in range(3):
                sw_ref[r, k] = weights[i][k]


def halo_gets(ref):
    last = ref.shape[3] - LANES
    return [lambda g, side, i=i: ref[i, g, :, pl.ds(side * last, LANES)] for i in range(ITERS)]


def join_kernel(own_ref, near_ref, corner_ref, east_ref, west_ref):
    pairs, half = own_ref.shape[1], ITERS // 2
    sent = messages(halo_gets(near_ref), near_ref.shape[1] - 3, lane_parts(own_ref.shape[2:]))
    for d, ref in enumerate((east_ref, west_ref)):
        for i in range(half):
            ref[i] = sent[d][i]
        ref[half : half + pairs] = own_ref[d]
        ref[half + pairs :] = corner_ref[d]


def near_kernel(y_ref, w_ref, near_ref, x_ref, keep_ref, hy_ref, hw_ref, wh_ref, p_ref, q_ref):
    rows, samples, levels, _ = y_ref.shape
    high = rows + ITERS
    _, sign = row_order(rows)
    lines, weights = strips(halo_gets(near_ref), samples, lane_parts((levels, LANES)))
    for i in range(ITERS):
        hy_ref[i] = lines[i]
        for k in range(3):
            hw_ref[i, k] = weights[i][k]
        for k, v in enumerate(all_weights([near_ref[i, samples + k] for k in range(3)], sign)):
            wh_ref[i, k] = v

    def get_w(r):
        ref, i = (wh_ref, r) if r < ITERS else (w_ref, r - ITERS)
        return [ref[i, k] for k in range(4)]

    def sample(s, carry):
        source = lambda r: near_ref[r, s] if r < ITERS else y_ref[r - ITERS, s]
        for step in range(ITERS):
            target = (p_ref, q_ref)[step % 2]

            def put(r, v, target=target, step=step):
                if step == ITERS - 1:
                    x_ref[r - ITERS, s] = v
                    return
                target[r, s] = v
                kept = r - (high - 3 - step)
                if kept >= 0:
                    keep_ref[step, kept, s] = v

            stencil(source, get_w, step + 1, high - 1 - step, put)
            source = functools.partial(lambda r, target: target[r, s], target=target)
        return carry

    lax.fori_loop(0, samples, sample, 0)


def far_rows(y_ref, w_ref, far_ref, keep_ref, wh_ref, s):
    rows = y_ref.shape[0]
    high = rows + ITERS

    def get_w(r):
        ref, i = (wh_ref, r - high) if r >= high else (w_ref, r - ITERS)
        return [ref[i, k] for k in range(4)]

    source = lambda r: far_ref[r - high, s] if r >= high else y_ref[r - ITERS, s]
    for step in range(ITERS):
        new = {}
        stencil(source, get_w, high - 1 - step, high - 1 - step + ITERS, new.__setitem__)
        if step < ITERS - 1:
            new[high - 3 - step], new[high - 2 - step] = keep_ref[step, 0, s], keep_ref[step, 1, s]
        source = new.__getitem__
    return new


def finish_kernel(
    x_ref, y_ref, w_ref, keep_ref, far_ref, sy_ref, sw_ref, hy_ref, hw_ref, left_ref, right_ref,
    out_ref, var_ref, sum_ref, wh_ref,
):
    rows, samples, levels, cols = x_ref.shape
    high = rows + 2 * ITERS
    parts = lane_parts((levels, LANES))
    lane, _, l32 = parts
    from_left, from_right = l32 < 4, l32 >= 28
    _, sign = row_order(rows)

    for i in range(ITERS):
        for k, v in enumerate(all_weights([far_ref[i, samples + k] for k in range(3)], sign)):
            wh_ref[i, k] = v
    far_lines, far_weights = strips(halo_gets(far_ref), samples, parts)

    def strip_at(r):
        if r < ITERS:
            return hy_ref[r], [hw_ref[r, k] for k in range(3)]
        if r < ITERS + rows:
            return sy_ref[r - ITERS], [sw_ref[r - ITERS, k] for k in range(3)]
        return far_lines[r - ITERS - rows], far_weights[r - ITERS - rows]

    field, weights = {}, {}
    for r in range(high):
        skip = 4 * (r % 2)
        values = [
            jnp.where(
                from_left,
                roll(left_ref[r // 2], -8 * g - skip),
                jnp.where(from_right, roll(right_ref[r // 2], 28 - 8 * g - skip), v),
            )
            for g, v in enumerate([strip_at(r)[0], *strip_at(r)[1]])
        ]
        field[r], weights[r] = values[0], all_weights(values[1:], sign)
    for step in range(ITERS):
        new = {}
        stencil(field.__getitem__, weights.__getitem__, step + 1, high - 1 - step, new.__setitem__)
        field = new

    for s in range(samples):
        for r, v in far_rows(y_ref, w_ref, far_ref, keep_ref, wh_ref, s).items():
            out_ref[r - ITERS, s] = v

    total, count = None, None
    for r in range(rows):
        strip = field[ITERS + r]
        for c in range(0, cols, LANES):
            lanes = pl.ds(c, LANES)
            square = None
            for s in range(samples):
                v = (x_ref if r < rows - ITERS else out_ref)[r, s, :, lanes]
                if c == 0:
                    v = jnp.where(lane < 4, roll(strip, -(SEG * s + 4)), v)
                if c == cols - LANES:
                    v = jnp.where(lane >= LANES - 4, roll(strip, LANES - SEG * s - 28), v)
                out_ref[r, s, :, lanes] = v
                square = v * v if square is None else square + v * v
            var = square / samples
            var_ref[r, :, lanes] = var
            m = jnp.where(w_ref[r, 1, :, lanes] > 0, 1.0, 0.0)
            total = m * var if total is None else total + m * var
            count = m if count is None else count + m
    sum_ref[0:1] = jnp.sum(total, axis=0, keepdims=True)
    sum_ref[1:2] = jnp.sum(count, axis=0, keepdims=True)


def scale_kernel(x_ref, w_ref, var_ref, all_ref, out_ref, mean_ref, stage, sem):
    rows, samples, levels, cols = x_ref.shape
    sums = jnp.sum(jnp.sum(all_ref[...], axis=0), axis=1, keepdims=True)
    mean = sums[0:1] / sums[1:2]
    mean_ref[...] = mean
    row_at, _ = row_order(rows)
    copies = []
    for c in range(cols // LANES):
        lanes = pl.ds(c * LANES, LANES)
        factors = []
        for r in range(rows):
            wet = w_ref[r, 1, :, lanes] > 0
            safe = jnp.where(wet, var_ref[r, :, lanes], 1.0)
            factors.append(jnp.where(wet, jnp.sqrt(mean / (safe + 1e-06)), 0.0))
        for s in range(samples):
            for r in range(rows):
                stage[c, s, pl.ds(row_at(r), levels, stride=rows)] = x_ref[r, s, :, lanes] * factors[r]
            copies.append(pltpu.make_async_copy(stage.at[c, s], out_ref.at[s, :, lanes], sem.at[c, s]))
            copies[-1].start()
    for copy in copies:
        copy.wait()


def call(kernel, out, *args, scratch=(), flops=0, in_space=None, out_space=None):
    out = [o if isinstance(o, jax.ShapeDtypeStruct) else jax.ShapeDtypeStruct(o, F32) for o in out]
    scratch = [pltpu.VMEM(o, F32) if isinstance(o, tuple) else o for o in scratch]
    return pl.pallas_call(
        kernel,
        out_shape=out,
        in_specs=[pl.BlockSpec(memory_space=in_space or pltpu.VMEM)] * len(args),
        out_specs=[pl.BlockSpec(memory_space=m) for m in out_space or [pltpu.VMEM] * len(out)],
        scratch_shapes=scratch,
        cost_estimate=pl.CostEstimate(flops=flops, bytes_accessed=sum(a.size * 4 for a in args), transcendentals=0),
        compiler_params=pltpu.CompilerParams(vmem_limit_bytes=12 << 20),
    )(*args)


def shards(noise, diff_lat, diff_lon, shear, sea_mask):
    samples, levels, rows, cols = noise.shape
    high = rows + 2 * ITERS
    flat = [noise.reshape(samples, levels * rows, cols)] + [
        a.reshape(levels * rows, cols) for a in (diff_lat, diff_lon, shear, sea_mask)
    ]
    n_lat, n_lon = lax.axis_size("lat"), lax.axis_size("lon")
    pair = [(i, i ^ 1) for i in range(n_lat)]
    across = [(i, i - 1 if i % 2 == 0 else i + 1) for i in range(1, n_lat - 1)]
    east = [(i, (i + 1) % n_lon) for i in range(n_lon)]
    west = [(j, i) for i, j in east]

    halo = (ITERS, samples + 3, levels, cols)
    tiles = cols // LANES
    plane = (tiles, levels * rows, LANES)
    flat = [pltpu.with_memory_space_constraint(a, pltpu.HBM) for a in flat]
    to_near, to_far, to_corner, *staged = call(
        edge_kernel,
        [halo, halo, (2, ITERS // 2, levels, LANES), (tiles, samples, levels * rows, LANES)] + [plane] * 3 + [jax.ShapeDtypeStruct(plane, sea_mask.dtype)],
        *flat,
        scratch=[pltpu.SemaphoreType.DMA((tiles, 5))],
        in_space=pltpu.HBM,
    )
    near = lax.ppermute(to_near, "lat", pair)
    corner = lax.ppermute(to_corner, "lat", across)
    far = lax.ppermute(to_far, "lat", across)
    (own_msg,) = call(message_kernel, [(2, rows // 2, levels, LANES)], *staged, flops=10**6)
    message = (high // 2, levels, LANES)
    to_east, to_west = call(join_kernel, [message, message], own_msg, near, corner)
    left = lax.ppermute(to_east, "lon", east)
    right = lax.ppermute(to_west, "lon", west)
    strip = (rows, levels, LANES)
    y, w, sy, sw = call(
        own_kernel,
        [(rows, samples, levels, cols), (rows, 4, levels, cols), strip, (rows, 3, levels, LANES)],
        *staged,
        flops=10**6,
    )
    buffer = (rows + ITERS, samples, levels, cols)
    side = [(ITERS, levels, LANES), (ITERS, 3, levels, LANES)]
    x, keep, hy, hw = call(
        near_kernel,
        [y.shape, (ITERS - 1, 2, samples, levels, cols), *side],
        y,
        w,
        near,
        scratch=[(ITERS, 4, levels, cols), buffer, buffer],
        flops=10**7,
    )
    x, var, part = call(
        finish_kernel,
        [y.shape, (rows, levels, cols), (2, LANES)],
        x,
        y,
        w,
        keep,
        far,
        sy,
        sw,
        hy,
        hw,
        left,
        right,
        scratch=[(ITERS, 4, levels, cols)],
    )
    spread = jnp.broadcast_to(part, (n_lat * n_lon, 2, LANES))
    every = lax.all_to_all(spread, ("lat", "lon"), 0, 0, tiled=True)
    out, mean = call(
        scale_kernel,
        [(samples, levels * rows, cols), (1, 1)],
        x,
        w,
        var,
        every,
        scratch=[(tiles, samples, levels * rows, LANES), pltpu.SemaphoreType.DMA((tiles, samples))],
        out_space=[pl.ANY, pltpu.VMEM],
    )
    return out.reshape(noise.shape), mean.reshape(())


def solution(mesh):
    grid = P(None, "lat", "lon")
    field = P(None, None, "lat", "lon")
    return jax.shard_map(
        shards,
        mesh=mesh,
        in_specs=(field, grid, grid, grid, grid),
        out_specs=(field, P()),
        check_vma=False,
    )
```

```python
import functools

import jax
import jax.numpy as jnp
from jax import lax
from jax.experimental import pallas as pl
from jax.experimental.pallas import tpu as pltpu
from jax.sharding import PartitionSpec as P

ITERS = 4
LANES = 128
SEG = 32
F32 = jnp.float32


def cell_weights(k11, k22, shear, mask):
    m = mask.astype(F32)
    return m * k11, m * k22, m * (0.5 * (shear * jnp.sqrt(k11 * k22)))


def centre_weight(wa, wb):
    return jnp.where(wa > 0, 1.0, 0.0) - 2.0 * (wa + wb)


def all_weights(w, sign):
    return centre_weight(w[0], w[1]), w[0], w[1], sign * w[2]


def roll(x, shift):
    n = x.shape[-1]
    shift = shift % n
    return x if shift == 0 else pltpu.roll(x, shift, x.ndim - 1)


def lane_parts(shape):
    lane = lax.broadcasted_iota(jnp.int32, shape, 1)
    return lane, lane // SEG, lane % SEG


def stencil(get_y, get_w, first, last, put):
    def products(r):
        y = get_y(r)
        w0, wa, wb, wc = get_w(r)
        return w0 * y, wa * y, wb * y, wc * y

    prev, here = products(first - 1), products(first)
    for r in range(first, last):
        after = products(r + 1)
        d, _, b, _ = here
        g = prev[3] - after[3]
        put(r, d + (prev[1] + after[1]) + roll(b + g, 1) + roll(b - g, -1))
        prev, here = here, after


def row_order(rows):
    odd = lax.rem(lax.axis_index("lat"), 2)
    step = 2 * odd - 1
    return lambda d: (1 - odd) * (rows - 1) + step * d, step.astype(F32)


def edge_kernel(n_ref, a_ref, b_ref, s_ref, m_ref, near_ref, head_ref, tail_ref, n_to, a_to, b_to, s_to, m_to, sem):
    samples, levels, tiles = n_ref.shape[0], near_ref.shape[2], n_to.shape[0]
    rows = n_ref.shape[1] // levels
    copies = []
    for c in range(tiles):
        lanes = pl.ds(c * LANES, LANES)
        for k, (ref, to) in enumerate(((a_ref, a_to), (b_ref, b_to), (s_ref, s_to), (m_ref, m_to))):
            copies.append(pltpu.make_async_copy(ref.at[:, lanes], to.at[c], sem.at[c, k]))
        copies.append(pltpu.make_async_copy(n_ref.at[:, :, lanes], n_to.at[c], sem.at[c, 4]))
    for copy in copies:
        copy.start()
    for copy in copies:
        copy.wait()
    row_at, _ = row_order(rows)
    parts = lane_parts((levels, LANES))
    edges = []
    for i in range(ITERS):
        for far, d in ((False, ITERS - 1 - i), (True, rows - 1 - i)):
            at = pl.ds(row_at(d), levels, stride=rows)
            data = [
                [n_to[c, s, at] for s in range(samples)]
                + list(cell_weights(a_to[c, at], b_to[c, at], s_to[c, at], m_to[c, at]))
                for c in range(tiles)
            ]
            for c in range(tiles):
                for g, v in enumerate(data[c]):
                    if not far:
                        near_ref[i, g, :, pl.ds(c * LANES, LANES)] = v
                    elif i == 0:
                        head_ref[ITERS + g * tiles + c] = v
                    else:
                        tail_ref[i - 1, g, :, pl.ds(c * LANES, LANES)] = v
            if far:
                edges.append(both_edges(lambda g, side: data[-side][g], samples + 3, parts))
    sent = messages(edges, parts)
    for d in range(2):
        for i in range(ITERS // 2):
            head_ref[d * (ITERS // 2) + i] = sent[d][i]


BATCH = 4


def replicate(values, seg):
    turned = [roll(v, SEG) for v in values]
    values = [jnp.where(seg == 1, t, v) for t, v in zip(turned, values)]
    turned = [roll(v, 2 * SEG) for v in values]
    return [jnp.where(seg >= 2, t, v) for t, v in zip(turned, values)]


def line_up(gets, samples, parts, low, high):
    _, seg, l32 = parts
    turned = [
        [(roll(get(s, low), SEG * s + 4), roll(get(s, high), SEG * s + 28)) for s in range(samples)] for get in gets
    ]
    lines = []
    for row in turned:
        line = None
        for s, (a, b) in enumerate(row):
            v = jnp.where(l32 < SEG // 2, a, b)
            line = v if line is None else jnp.where(seg == s, v, line)
        lines.append(line)
    return lines


def both_edges(get, groups, parts):
    return [jnp.where(parts[0] < LANES // 2, get(g, 0), get(g, 1)) for g in range(groups)]


def messages(both, parts):
    lane, seg, l32 = parts
    samples = len(both[0]) - 3
    lines = [[roll(row[s], SEG * s + 4) for s in range(samples)] for row in both]
    packed = [[roll(row[samples + k], 8 * k + 12) for k in range(3)] for row in both]
    packed = replicate([jnp.where(l32 < 16, a, jnp.where(l32 < 24, b, c)) for a, b, c in packed], seg)
    full = []
    for line, weights in zip(lines, packed):
        v = line[0]
        for s in range(1, samples):
            v = jnp.where(seg == s, line[s], v)
        full.append(jnp.where(l32 < 8, v, weights))
    low = lane % 8 < 4
    pairs = list(zip(full[0::2], full[1::2]))
    east = [jnp.where(low, a, roll(b, 4)) for a, b in pairs]
    west = [jnp.where(low, roll(a, -4), b) for a, b in pairs]
    return east, west


def strips(gets, samples, parts):
    _, seg, l32 = parts
    lines = line_up(gets, samples, parts, 0, 1)
    turned = [(roll(get(samples + k, 0), 4), roll(get(samples + k, 1), 28)) for get in gets for k in range(3)]
    weights = replicate([jnp.where(l32 < SEG // 2, a, b) for a, b in turned], seg)
    return lines, [weights[3 * i : 3 * i + 3] for i in range(len(gets))]


def own_row(refs, r, rows, levels):
    n_ref, a_ref, b_ref, s_ref, m_ref = refs
    at = pl.ds(row_order(rows)[0](r), levels, stride=rows)
    return [
        [n_ref[c, s, at] for s in range(n_ref.shape[1])]
        + list(cell_weights(a_ref[c, at], b_ref[c, at], s_ref[c, at], m_ref[c, at]))
        for c in range(n_ref.shape[0])
    ]


def own_gets(data):
    return [lambda g, side, row=row: row[-side][g] for row in data]


def message_kernel(n_ref, a_ref, b_ref, s_ref, m_ref, msg_ref, n_to, a_to, b_to, s_to, m_to):
    levels = msg_ref.shape[2]
    rows, samples, last = n_ref.shape[2] // levels, n_ref.shape[1], n_ref.shape[0] - 1
    parts = lane_parts((levels, LANES))
    left = lax.broadcasted_iota(jnp.int32, a_to.shape, 1) < LANES // 2
    for ref, to in ((a_ref, a_to), (b_ref, b_to), (s_ref, s_to), (m_ref, m_to)):
        to[...] = jnp.where(left, ref[0], ref[last])
    for s in range(samples):
        n_to[s] = jnp.where(left, n_ref[0, s], n_ref[last, s])
    row_at, _ = row_order(rows)
    for first in range(0, rows, BATCH):
        both = []
        for d in range(first, first + BATCH):
            at = pl.ds(row_at(d), levels, stride=rows)
            both.append([n_to[s, at] for s in range(samples)] + list(cell_weights(a_to[at], b_to[at], s_to[at], m_to[at])))
        sent = messages(both, parts)
        for d in range(2):
            for i in range(BATCH // 2):
                msg_ref[d, first // 2 + i] = sent[d][i]


def own_kernel(n_ref, a_ref, b_ref, s_ref, m_ref, y_ref, w_ref, sy_ref, sw_ref):
    rows, samples, levels, _ = y_ref.shape
    parts = lane_parts((levels, LANES))
    _, sign = row_order(rows)
    for first in range(0, rows, BATCH):
        batch = range(first, first + BATCH)
        data = [own_row((n_ref, a_ref, b_ref, s_ref, m_ref), r, rows, levels) for r in batch]
        lines, weights = strips(own_gets(data), samples, parts)
        for i, r in enumerate(batch):
            for c, values in enumerate(data[i]):
                lanes = pl.ds(c * LANES, LANES)
                for s in range(samples):
                    y_ref[r, s, :, lanes] = values[s]
                for k, v in enumerate(all_weights(values[samples:], sign)):
                    w_ref[r, k, :, lanes] = v
            sy_ref[r] = lines[i]
            for k in range(3):
                sw_ref[r, k] = weights[i][k]


def halo_gets(ref):
    last = ref.shape[3] - LANES
    return [lambda g, side, i=i: ref[i, g, :, pl.ds(side * last, LANES)] for i in range(ITERS)]


def join_kernel(own_ref, near_ref, head_ref, east_ref, west_ref):
    pairs, half = own_ref.shape[1], ITERS // 2
    parts = lane_parts(own_ref.shape[2:])
    sent = messages([both_edges(get, near_ref.shape[1], parts) for get in halo_gets(near_ref)], parts)
    for d, ref in enumerate((east_ref, west_ref)):
        for i in range(half):
            ref[i] = sent[d][i]
            ref[half + pairs + i] = head_ref[d * half + i]
        ref[half : half + pairs] = own_ref[d]


def near_kernel(y_ref, w_ref, near_ref, x_ref, keep_ref, hy_ref, hw_ref, wh_ref, p_ref, q_ref):
    rows, samples, levels, _ = y_ref.shape
    high = rows + ITERS
    _, sign = row_order(rows)
    lines, weights = strips(halo_gets(near_ref), samples, lane_parts((levels, LANES)))
    for i in range(ITERS):
        hy_ref[i] = lines[i]
        for k in range(3):
            hw_ref[i, k] = weights[i][k]
        for k, v in enumerate(all_weights([near_ref[i, samples + k] for k in range(3)], sign)):
            wh_ref[i, k] = v

    def get_w(r):
        ref, i = (wh_ref, r) if r < ITERS else (w_ref, r - ITERS)
        return [ref[i, k] for k in range(4)]

    def sample(s, carry):
        source = lambda r: near_ref[r, s] if r < ITERS else y_ref[r - ITERS, s]
        for step in range(ITERS):
            target = (p_ref, q_ref)[step % 2]

            def put(r, v, target=target, step=step):
                if step == ITERS - 1:
                    x_ref[r - ITERS, s] = v
                    return
                target[r, s] = v
                kept = r - (high - 3 - step)
                if kept >= 0:
                    keep_ref[step, kept, s] = v

            stencil(source, get_w, step + 1, high - 1 - step, put)
            source = functools.partial(lambda r, target: target[r, s], target=target)
        return carry

    lax.fori_loop(0, samples, sample, 0)


def far_kernel(y_ref, w_ref, keep_ref, head_ref, tail_ref, x_ref, hy_ref, hw_ref, wh_ref, yh_ref):
    rows, samples, levels, cols = y_ref.shape
    high = rows + ITERS
    tiles = cols // LANES
    _, sign = row_order(rows)

    def tile(i, g, c):
        return head_ref[ITERS + g * tiles + c] if i == 0 else tail_ref[i - 1, g, :, pl.ds(c * LANES, LANES)]

    for i in range(ITERS):
        for c in range(tiles):
            lanes = pl.ds(c * LANES, LANES)
            for k, v in enumerate(all_weights([tile(i, samples + k, c) for k in range(3)], sign)):
                wh_ref[i, k, :, lanes] = v
    for c in range(tiles):
        for s in range(samples):
            yh_ref[s, :, pl.ds(c * LANES, LANES)] = tile(0, s, c)
    gets = [lambda g, side, i=i: tile(i, g, side * (tiles - 1)) for i in range(ITERS)]
    lines, weights = strips(gets, samples, lane_parts((levels, LANES)))
    for i in range(ITERS):
        hy_ref[i] = lines[i]
        for k in range(3):
            hw_ref[i, k] = weights[i][k]

    def get_w(r):
        ref, i = (wh_ref, r - high) if r >= high else (w_ref, r - ITERS)
        return [ref[i, k] for k in range(4)]

    for s in range(samples):

        def source(r, s=s):
            if r < high:
                return y_ref[r - ITERS, s]
            return yh_ref[s] if r == high else tail_ref[r - high - 1, s]

        for step in range(ITERS):
            new = {}
            stencil(source, get_w, high - 1 - step, high - 1 - step + ITERS, new.__setitem__)
            if step < ITERS - 1:
                new[high - 3 - step], new[high - 2 - step] = keep_ref[step, 0, s], keep_ref[step, 1, s]
            source = new.__getitem__
        for r, v in new.items():
            x_ref[r - rows, s] = v


def finish_kernel(
    x_ref, xf_ref, w_ref, sy_ref, sw_ref, hy_ref, hw_ref, fy_ref, fw_ref, left_ref, right_ref, out_ref, var_ref, sum_ref
):
    rows, samples, levels, cols = x_ref.shape
    high = rows + 2 * ITERS
    parts = lane_parts((levels, LANES))
    lane, _, l32 = parts
    from_left, from_right = l32 < 4, l32 >= 28
    _, sign = row_order(rows)

    def strip_at(r):
        if r < ITERS:
            return hy_ref[r], [hw_ref[r, k] for k in range(3)]
        if r < ITERS + rows:
            return sy_ref[r - ITERS], [sw_ref[r - ITERS, k] for k in range(3)]
        return fy_ref[r - ITERS - rows], [fw_ref[r - ITERS - rows, k] for k in range(3)]

    field, weights = {}, {}
    for r in range(high):
        skip = 4 * (r % 2)
        values = [
            jnp.where(
                from_left,
                roll(left_ref[r // 2], -8 * g - skip),
                jnp.where(from_right, roll(right_ref[r // 2], 28 - 8 * g - skip), v),
            )
            for g, v in enumerate([strip_at(r)[0], *strip_at(r)[1]])
        ]
        field[r], weights[r] = values[0], all_weights(values[1:], sign)
    for step in range(ITERS):
        new = {}
        stencil(field.__getitem__, weights.__getitem__, step + 1, high - 1 - step, new.__setitem__)
        field = new

    total, count = None, None
    for r in range(rows):
        strip = field[ITERS + r]
        for c in range(0, cols, LANES):
            lanes = pl.ds(c, LANES)
            square = None
            for s in range(samples):
                v = x_ref[r, s, :, lanes] if r < rows - ITERS else xf_ref[r - rows + ITERS, s, :, lanes]
                if c == 0:
                    v = jnp.where(lane < 4, roll(strip, -(SEG * s + 4)), v)
                if c == cols - LANES:
                    v = jnp.where(lane >= LANES - 4, roll(strip, LANES - SEG * s - 28), v)
                out_ref[r, s, :, lanes] = v
                square = v * v if square is None else square + v * v
            var = square / samples
            var_ref[r, :, lanes] = var
            m = jnp.where(w_ref[r, 1, :, lanes] > 0, 1.0, 0.0)
            total = m * var if total is None else total + m * var
            count = m if count is None else count + m
    sum_ref[0:1] = jnp.sum(total, axis=0, keepdims=True)
    sum_ref[1:2] = jnp.sum(count, axis=0, keepdims=True)


def scale_kernel(x_ref, w_ref, var_ref, all_ref, out_ref, mean_ref, stage, sem):
    rows, samples, levels, cols = x_ref.shape
    sums = jnp.sum(jnp.sum(all_ref[...], axis=0), axis=1, keepdims=True)
    mean = sums[0:1] / sums[1:2]
    mean_ref[...] = mean
    row_at, _ = row_order(rows)
    copies = []
    for c in range(cols // LANES):
        lanes = pl.ds(c * LANES, LANES)
        factors = []
        for r in range(rows):
            wet = w_ref[r, 1, :, lanes] > 0
            safe = jnp.where(wet, var_ref[r, :, lanes], 1.0)
            factors.append(jnp.where(wet, jnp.sqrt(mean / (safe + 1e-06)), 0.0))
        for s in range(samples):
            for r in range(rows):
                stage[c, s, pl.ds(row_at(r), levels, stride=rows)] = x_ref[r, s, :, lanes] * factors[r]
            copies.append(pltpu.make_async_copy(stage.at[c, s], out_ref.at[s, :, lanes], sem.at[c, s]))
            copies[-1].start()
    for copy in copies:
        copy.wait()


def call(kernel, out, *args, scratch=(), flops=0, in_space=None, out_space=None):
    out = [o if isinstance(o, jax.ShapeDtypeStruct) else jax.ShapeDtypeStruct(o, F32) for o in out]
    scratch = [pltpu.VMEM(o, F32) if isinstance(o, tuple) else o for o in scratch]
    return pl.pallas_call(
        kernel,
        out_shape=out,
        in_specs=[pl.BlockSpec(memory_space=in_space or pltpu.VMEM)] * len(args),
        out_specs=[pl.BlockSpec(memory_space=m) for m in out_space or [pltpu.VMEM] * len(out)],
        scratch_shapes=scratch,
        cost_estimate=pl.CostEstimate(flops=flops, bytes_accessed=sum(a.size * 4 for a in args), transcendentals=0),
        compiler_params=pltpu.CompilerParams(vmem_limit_bytes=12 << 20),
    )(*args)


def shards(noise, diff_lat, diff_lon, shear, sea_mask):
    samples, levels, rows, cols = noise.shape
    high = rows + 2 * ITERS
    flat = [noise.reshape(samples, levels * rows, cols)] + [
        a.reshape(levels * rows, cols) for a in (diff_lat, diff_lon, shear, sea_mask)
    ]
    n_lat, n_lon = lax.axis_size("lat"), lax.axis_size("lon")
    pair = [(i, i ^ 1) for i in range(n_lat)]
    across = [(i, i - 1 if i % 2 == 0 else i + 1) for i in range(1, n_lat - 1)]
    east = [(i, (i + 1) % n_lon) for i in range(n_lon)]
    west = [(j, i) for i, j in east]

    halo = (ITERS, samples + 3, levels, cols)
    tiles = cols // LANES
    plane = (tiles, levels * rows, LANES)
    flat = [pltpu.with_memory_space_constraint(a, pltpu.HBM) for a in flat]
    head = (ITERS + (samples + 3) * tiles, levels, LANES)
    to_near, to_far, to_far_tail, *staged = call(
        edge_kernel,
        [halo, head, (ITERS - 1, *halo[1:]), (tiles, samples, levels * rows, LANES)] + [plane] * 3 + [jax.ShapeDtypeStruct(plane, sea_mask.dtype)],
        *flat,
        scratch=[pltpu.SemaphoreType.DMA((tiles, 5))],
        in_space=pltpu.HBM,
    )
    near = lax.ppermute(to_near, "lat", pair)
    far = lax.ppermute(to_far, "lat", across)
    far_tail = lax.ppermute(to_far_tail, "lat", across)
    flat_plane = plane[1:]
    (own_msg,) = call(
        message_kernel,
        [(2, rows // 2, levels, LANES)],
        *staged,
        scratch=[(samples, *flat_plane)] + [flat_plane] * 3 + [pltpu.VMEM(flat_plane, sea_mask.dtype)],
        flops=10**6,
    )
    message = (high // 2, levels, LANES)
    to_east, to_west = call(join_kernel, [message, message], own_msg, near, far)
    left = lax.ppermute(to_east, "lon", east)
    right = lax.ppermute(to_west, "lon", west)
    strip = (rows, levels, LANES)
    y, w, sy, sw = call(
        own_kernel,
        [(rows, samples, levels, cols), (rows, 4, levels, cols), strip, (rows, 3, levels, LANES)],
        *staged,
        flops=10**6,
    )
    buffer = (rows + ITERS, samples, levels, cols)
    side = [(ITERS, levels, LANES), (ITERS, 3, levels, LANES)]
    x, keep, hy, hw = call(
        near_kernel,
        [y.shape, (ITERS - 1, 2, samples, levels, cols), *side],
        y,
        w,
        near,
        scratch=[(ITERS, 4, levels, cols), buffer, buffer],
        flops=10**7,
    )
    x_far, fy, fw = call(
        far_kernel,
        [(ITERS, samples, levels, cols), *side],
        y,
        w,
        keep,
        far,
        far_tail,
        scratch=[(ITERS, 4, levels, cols), (samples, levels, cols)],
        flops=10**6,
    )
    x, var, part = call(
        finish_kernel,
        [y.shape, (rows, levels, cols), (2, LANES)],
        x,
        x_far,
        w,
        sy,
        sw,
        hy,
        hw,
        fy,
        fw,
        left,
        right,
    )
    spread = jnp.broadcast_to(part, (n_lat * n_lon, 2, LANES))
    every = lax.all_to_all(spread, ("lat", "lon"), 0, 0, tiled=True)
    out, mean = call(
        scale_kernel,
        [(samples, levels * rows, cols), (1, 1)],
        x,
        w,
        var,
        every,
        scratch=[(tiles, samples, levels * rows, LANES), pltpu.SemaphoreType.DMA((tiles, samples))],
        out_space=[pl.ANY, pltpu.VMEM],
    )
    return out.reshape(noise.shape), mean.reshape(())


def solution(mesh):
    grid = P(None, "lat", "lon")
    field = P(None, None, "lat", "lon")
    return jax.shard_map(
        shards,
        mesh=mesh,
        in_specs=(field, grid, grid, grid, grid),
        out_specs=(field, P()),
        check_vma=False,
    )
```

```python
import functools

import jax
import jax.numpy as jnp
from jax import lax
from jax.experimental import pallas as pl
from jax.experimental.pallas import tpu as pltpu
from jax.sharding import PartitionSpec as P

ITERS = 4
LANES = 128
SEG = 32
F32 = jnp.float32


def cell_weights(k11, k22, shear, mask):
    m = mask.astype(F32)
    return m * k11, m * k22, m * (0.5 * (shear * jnp.sqrt(k11 * k22)))


def centre_weight(wa, wb):
    return jnp.where(wa > 0, 1.0, 0.0) - 2.0 * (wa + wb)


def all_weights(w, sign):
    return centre_weight(w[0], w[1]), w[0], w[1], sign * w[2]


def roll(x, shift):
    n = x.shape[-1]
    shift = shift % n
    return x if shift == 0 else pltpu.roll(x, shift, x.ndim - 1)


def lane_parts(shape):
    lane = lax.broadcasted_iota(jnp.int32, shape, 1)
    return lane, lane // SEG, lane % SEG


def shift(x, by):
    tiles = [roll(x[:, c : c + LANES], by) for c in range(0, x.shape[1], LANES)]
    lane = lax.broadcasted_iota(jnp.int32, tiles[0].shape, 1)
    if by > 0:
        joined = tiles[:1] + [jnp.where(lane == 0, a, b) for a, b in zip(tiles, tiles[1:])]
    else:
        joined = [jnp.where(lane == LANES - 1, b, a) for a, b in zip(tiles, tiles[1:])] + tiles[-1:]
    return jnp.concatenate(joined, axis=1) if len(joined) > 1 else joined[0]


def stencil(get_y, get_w, first, last, put):
    def products(r):
        y = get_y(r)
        w0, wa, wb, wc = get_w(r)
        return w0 * y, wa * y, wb * y, wc * y

    prev, here = products(first - 1), products(first)
    for r in range(first, last):
        after = products(r + 1)
        d, _, b, _ = here
        g = prev[3] - after[3]
        put(r, d + (prev[1] + after[1]) + shift(b + g, 1) + shift(b - g, -1))
        prev, here = here, after


def row_order(rows):
    odd = lax.rem(lax.axis_index("lat"), 2)
    step = 2 * odd - 1
    return lambda d: (1 - odd) * (rows - 1) + step * d, step.astype(F32)


def edge_kernel(n_ref, a_ref, b_ref, s_ref, m_ref, near_ref, head_ref, tail_ref, n_to, a_to, b_to, s_to, m_to, sem):
    samples, levels, tiles = n_ref.shape[0], near_ref.shape[2], n_to.shape[0]
    rows = n_ref.shape[1] // levels
    copies = []
    for c in range(tiles):
        lanes = pl.ds(c * LANES, LANES)
        for k, (ref, to) in enumerate(((a_ref, a_to), (b_ref, b_to), (s_ref, s_to), (m_ref, m_to))):
            copies.append(pltpu.make_async_copy(ref.at[:, lanes], to.at[c], sem.at[c, k]))
    for c in range(tiles):
        lanes = pl.ds(c * LANES, LANES)
        copies.append(pltpu.make_async_copy(n_ref.at[:, :, lanes], n_to.at[c], sem.at[c, 4]))
    for copy in copies:
        copy.start()
    row_at, _ = row_order(rows)
    parts = lane_parts((levels, LANES))

    def put(i, far, g, c, v):
        if not far:
            near_ref[i, g, :, pl.ds(c * LANES, LANES)] = v
        elif i == 0:
            head_ref[ITERS + g * tiles + c] = v
        else:
            tail_ref[i - 1, g, :, pl.ds(c * LANES, LANES)] = v

    blocks = [(i, far, row_at(rows - 1 - i if far else ITERS - 1 - i)) for i in range(ITERS) for far in (False, True)]
    data = {}
    for copy in copies[: 4 * tiles]:
        copy.wait()
    for i, far, r in blocks:
        at = pl.ds(r, levels, stride=rows)
        for c in range(tiles):
            for k, v in enumerate(cell_weights(a_to[c, at], b_to[c, at], s_to[c, at], m_to[c, at])):
                put(i, far, samples + k, c, v)
                data[i, far, samples + k, c] = v
    for copy in copies[4 * tiles :]:
        copy.wait()
    for i, far, r in blocks:
        for c in range(tiles):
            for s in range(samples):
                v = n_to[c, s, pl.ds(r, levels, stride=rows)]
                put(i, far, s, c, v)
                data[i, far, s, c] = v
    edges = [
        both_edges(lambda g, side: data[i, True, g, side * (tiles - 1)], samples + 3, parts) for i in range(ITERS)
    ]
    sent = messages(edges, parts)
    for d in range(2):
        for i in range(ITERS // 2):
            head_ref[d * (ITERS // 2) + i] = sent[d][i]


BATCH = 4


def replicate(values, seg):
    turned = [roll(v, SEG) for v in values]
    values = [jnp.where(seg == 1, t, v) for t, v in zip(turned, values)]
    turned = [roll(v, 2 * SEG) for v in values]
    return [jnp.where(seg >= 2, t, v) for t, v in zip(turned, values)]


def line_up(gets, samples, parts, low, high):
    _, seg, l32 = parts
    turned = [
        [(roll(get(s, low), SEG * s + 4), roll(get(s, high), SEG * s + 28)) for s in range(samples)] for get in gets
    ]
    lines = []
    for row in turned:
        line = None
        for s, (a, b) in enumerate(row):
            v = jnp.where(l32 < SEG // 2, a, b)
            line = v if line is None else jnp.where(seg == s, v, line)
        lines.append(line)
    return lines


def both_edges(get, groups, parts):
    return [jnp.where(parts[0] < LANES // 2, get(g, 0), get(g, 1)) for g in range(groups)]


def messages(both, parts):
    lane, seg, l32 = parts
    samples = len(both[0]) - 3
    lines = [[roll(row[s], SEG * s + 4) for s in range(samples)] for row in both]
    packed = [[roll(row[samples + k], 8 * k + 12) for k in range(3)] for row in both]
    packed = replicate([jnp.where(l32 < 16, a, jnp.where(l32 < 24, b, c)) for a, b, c in packed], seg)
    full = []
    for line, weights in zip(lines, packed):
        v = line[0]
        for s in range(1, samples):
            v = jnp.where(seg == s, line[s], v)
        full.append(jnp.where(l32 < 8, v, weights))
    low = lane % 8 < 4
    pairs = list(zip(full[0::2], full[1::2]))
    east = [jnp.where(low, a, roll(b, 4)) for a, b in pairs]
    west = [jnp.where(low, roll(a, -4), b) for a, b in pairs]
    return east, west


def strips(gets, samples, parts):
    _, seg, l32 = parts
    lines = line_up(gets, samples, parts, 0, 1)
    turned = [(roll(get(samples + k, 0), 4), roll(get(samples + k, 1), 28)) for get in gets for k in range(3)]
    weights = replicate([jnp.where(l32 < SEG // 2, a, b) for a, b in turned], seg)
    return lines, [weights[3 * i : 3 * i + 3] for i in range(len(gets))]


def own_row(refs, r, rows, levels):
    n_ref, a_ref, b_ref, s_ref, m_ref = refs
    at = pl.ds(row_order(rows)[0](r), levels, stride=rows)
    return [
        [n_ref[c, s, at] for s in range(n_ref.shape[1])]
        + list(cell_weights(a_ref[c, at], b_ref[c, at], s_ref[c, at], m_ref[c, at]))
        for c in range(n_ref.shape[0])
    ]


def own_gets(data):
    return [lambda g, side, row=row: row[-side][g] for row in data]


def message_kernel(n_ref, a_ref, b_ref, s_ref, m_ref, near_ref, head_ref, east_ref, west_ref, n_to, a_to, b_to, s_to, m_to):
    levels, half = east_ref.shape[1], ITERS // 2
    rows, samples, last = n_ref.shape[2] // levels, n_ref.shape[1], n_ref.shape[0] - 1
    parts = lane_parts((levels, LANES))
    left = lax.broadcasted_iota(jnp.int32, a_to.shape, 1) < LANES // 2
    for ref, to in ((a_ref, a_to), (b_ref, b_to), (s_ref, s_to), (m_ref, m_to)):
        to[...] = jnp.where(left, ref[0], ref[last])
    for s in range(samples):
        n_to[s] = jnp.where(left, n_ref[0, s], n_ref[last, s])
    row_at, _ = row_order(rows)
    for first in range(0, rows, BATCH):
        both = []
        for d in range(first, first + BATCH):
            at = pl.ds(row_at(d), levels, stride=rows)
            both.append([n_to[s, at] for s in range(samples)] + list(cell_weights(a_to[at], b_to[at], s_to[at], m_to[at])))
        for ref, sent in zip((east_ref, west_ref), messages(both, parts)):
            for i in range(BATCH // 2):
                ref[half + first // 2 + i] = sent[i]
    near = [both_edges(get, near_ref.shape[1], parts) for get in halo_gets(near_ref)]
    for d, (ref, sent) in enumerate(zip((east_ref, west_ref), messages(near, parts))):
        for i in range(half):
            ref[i] = sent[i]
            ref[half + rows // 2 + i] = head_ref[d * half + i]


def own_kernel(n_ref, a_ref, b_ref, s_ref, m_ref, y_ref, w_ref, sy_ref, sw_ref):
    rows, samples, levels, _ = y_ref.shape
    parts = lane_parts((levels, LANES))
    _, sign = row_order(rows)
    for first in range(0, rows, BATCH):
        batch = range(first, first + BATCH)
        data = [own_row((n_ref, a_ref, b_ref, s_ref, m_ref), r, rows, levels) for r in batch]
        lines, weights = strips(own_gets(data), samples, parts)
        for i, r in enumerate(batch):
            for c, values in enumerate(data[i]):
                lanes = pl.ds(c * LANES, LANES)
                for s in range(samples):
                    y_ref[r, s, :, lanes] = values[s]
                for k, v in enumerate(all_weights(values[samples:], sign)):
                    w_ref[r, k, :, lanes] = v
            sy_ref[r] = lines[i]
            for k in range(3):
                sw_ref[r, k] = weights[i][k]


def halo_gets(ref):
    last = ref.shape[3] - LANES
    return [lambda g, side, i=i: ref[i, g, :, pl.ds(side * last, LANES)] for i in range(ITERS)]


def near_kernel(y_ref, w_ref, near_ref, x_ref, keep_ref, hy_ref, hw_ref, wh_ref, p_ref, q_ref):
    rows, samples, levels, _ = y_ref.shape
    high = rows + ITERS
    _, sign = row_order(rows)
    lines, weights = strips(halo_gets(near_ref), samples, lane_parts((levels, LANES)))
    for i in range(ITERS):
        hy_ref[i] = lines[i]
        for k in range(3):
            hw_ref[i, k] = weights[i][k]
        for k, v in enumerate(all_weights([near_ref[i, samples + k] for k in range(3)], sign)):
            wh_ref[i, k] = v

    def get_w(r):
        ref, i = (wh_ref, r) if r < ITERS else (w_ref, r - ITERS)
        return [ref[i, k] for k in range(4)]

    def sample(s, carry):
        source = lambda r: near_ref[r, s] if r < ITERS else y_ref[r - ITERS, s]
        for step in range(ITERS):
            target = (p_ref, q_ref)[step % 2]

            def put(r, v, target=target, step=step):
                if step == ITERS - 1:
                    x_ref[r - ITERS, s] = v
                    return
                target[r, s] = v
                kept = r - (high - 3 - step)
                if kept >= 0:
                    keep_ref[step, kept, s] = v

            stencil(source, get_w, step + 1, high - 1 - step, put)
            source = functools.partial(lambda r, target: target[r, s], target=target)
        return carry

    lax.fori_loop(0, samples, sample, 0)


def far_kernel(y_ref, w_ref, keep_ref, head_ref, tail_ref, x_ref, hy_ref, hw_ref, wh_ref, yh_ref):
    rows, samples, levels, cols = y_ref.shape
    high = rows + ITERS
    tiles = cols // LANES
    _, sign = row_order(rows)

    def tile(i, g, c):
        return head_ref[ITERS + g * tiles + c] if i == 0 else tail_ref[i - 1, g, :, pl.ds(c * LANES, LANES)]

    for i in range(ITERS):
        for c in range(tiles):
            lanes = pl.ds(c * LANES, LANES)
            for k, v in enumerate(all_weights([tile(i, samples + k, c) for k in range(3)], sign)):
                wh_ref[i, k, :, lanes] = v
    for c in range(tiles):
        for s in range(samples):
            yh_ref[s, :, pl.ds(c * LANES, LANES)] = tile(0, s, c)
    gets = [lambda g, side, i=i: tile(i, g, side * (tiles - 1)) for i in range(ITERS)]
    lines, weights = strips(gets, samples, lane_parts((levels, LANES)))
    for i in range(ITERS):
        hy_ref[i] = lines[i]
        for k in range(3):
            hw_ref[i, k] = weights[i][k]

    def get_w(r):
        ref, i = (wh_ref, r - high) if r >= high else (w_ref, r - ITERS)
        return [ref[i, k] for k in range(4)]

    for s in range(samples):

        def source(r, s=s):
            if r < high:
                return y_ref[r - ITERS, s]
            return yh_ref[s] if r == high else tail_ref[r - high - 1, s]

        for step in range(ITERS):
            new = {}
            stencil(source, get_w, high - 1 - step, high - 1 - step + ITERS, new.__setitem__)
            if step < ITERS - 1:
                new[high - 3 - step], new[high - 2 - step] = keep_ref[step, 0, s], keep_ref[step, 1, s]
            source = new.__getitem__
        for r, v in new.items():
            x_ref[r - rows, s] = v


def finish_kernel(
    x_ref, xf_ref, w_ref, sy_ref, sw_ref, hy_ref, hw_ref, fy_ref, fw_ref, left_ref, right_ref, out_ref, sum_ref
):
    rows, samples, levels, cols = x_ref.shape
    high = rows + 2 * ITERS
    parts = lane_parts((levels, LANES))
    lane, _, l32 = parts
    from_left, from_right = l32 < 4, l32 >= 28
    _, sign = row_order(rows)

    def strip_at(r):
        if r < ITERS:
            return hy_ref[r], [hw_ref[r, k] for k in range(3)]
        if r < ITERS + rows:
            return sy_ref[r - ITERS], [sw_ref[r - ITERS, k] for k in range(3)]
        return fy_ref[r - ITERS - rows], [fw_ref[r - ITERS - rows, k] for k in range(3)]

    field, weights = {}, {}
    for r in range(high):
        skip = 4 * (r % 2)
        values = [
            jnp.where(
                from_left,
                roll(left_ref[r // 2], -8 * g - skip),
                jnp.where(from_right, roll(right_ref[r // 2], 28 - 8 * g - skip), v),
            )
            for g, v in enumerate([strip_at(r)[0], *strip_at(r)[1]])
        ]
        field[r], weights[r] = values[0], all_weights(values[1:], sign)
    for step in range(ITERS):
        new = {}
        stencil(field.__getitem__, weights.__getitem__, step + 1, high - 1 - step, new.__setitem__)
        field = new

    total, count = None, None
    row_at, _ = row_order(rows)
    for r in range(rows):
        strip = field[ITERS + r]
        for c in range(cols // LANES):
            lanes = pl.ds(c * LANES, LANES)
            values = []
            for s in range(samples):
                v = x_ref[r, s, :, lanes] if r < rows - ITERS else xf_ref[r - rows + ITERS, s, :, lanes]
                if c == 0:
                    v = jnp.where(lane < 4, roll(strip, -(SEG * s + 4)), v)
                if c == cols // LANES - 1:
                    v = jnp.where(lane >= LANES - 4, roll(strip, LANES - SEG * s - 28), v)
                values.append(v)
            var = sum(v * v for v in values[1:]) + values[0] * values[0]
            var = var / samples
            wet = w_ref[r, 1, :, lanes] > 0
            m = jnp.where(wet, 1.0, 0.0)
            total = m * var if total is None else total + m * var
            count = m if count is None else count + m
            factor = m * jnp.sqrt(1.0 / (jnp.where(wet, var, 1.0) + 1e-06))
            for s in range(samples):
                out_ref[c, s, pl.ds(row_at(r), levels, stride=rows)] = values[s] * factor
    sum_ref[0:1] = jnp.sum(total, axis=0, keepdims=True)
    sum_ref[1:2] = jnp.sum(count, axis=0, keepdims=True)


def scale_kernel(x_ref, all_ref, out_ref, mean_ref, stage, sem):
    tiles, samples = x_ref.shape[:2]
    sums = jnp.sum(jnp.sum(all_ref[...], axis=0), axis=1, keepdims=True)
    mean = sums[0:1] / sums[1:2]
    mean_ref[...] = mean
    factor = jnp.sqrt(mean)
    copies = []
    for c in range(tiles):
        for s in range(samples):
            stage[c, s] = x_ref[c, s] * factor
            lanes = pl.ds(c * LANES, LANES)
            copies.append(pltpu.make_async_copy(stage.at[c, s], out_ref.at[s, :, lanes], sem.at[c, s]))
            copies[-1].start()
    for copy in copies:
        copy.wait()


def call(kernel, out, *args, scratch=(), flops=0, in_space=None, out_space=None):
    out = [o if isinstance(o, jax.ShapeDtypeStruct) else jax.ShapeDtypeStruct(o, F32) for o in out]
    scratch = [pltpu.VMEM(o, F32) if isinstance(o, tuple) else o for o in scratch]
    return pl.pallas_call(
        kernel,
        out_shape=out,
        in_specs=[pl.BlockSpec(memory_space=in_space or pltpu.VMEM)] * len(args),
        out_specs=[pl.BlockSpec(memory_space=m) for m in out_space or [pltpu.VMEM] * len(out)],
        scratch_shapes=scratch,
        cost_estimate=pl.CostEstimate(flops=flops, bytes_accessed=sum(a.size * 4 for a in args), transcendentals=0),
        compiler_params=pltpu.CompilerParams(vmem_limit_bytes=12 << 20),
    )(*args)


def shards(noise, diff_lat, diff_lon, shear, sea_mask):
    samples, levels, rows, cols = noise.shape
    high = rows + 2 * ITERS
    flat = [noise.reshape(samples, levels * rows, cols)] + [
        a.reshape(levels * rows, cols) for a in (diff_lat, diff_lon, shear, sea_mask)
    ]
    n_lat, n_lon = lax.axis_size("lat"), lax.axis_size("lon")
    pair = [(i, i ^ 1) for i in range(n_lat)]
    across = [(i, i - 1 if i % 2 == 0 else i + 1) for i in range(1, n_lat - 1)]
    east = [(i, (i + 1) % n_lon) for i in range(n_lon)]
    west = [(j, i) for i, j in east]

    halo = (ITERS, samples + 3, levels, cols)
    tiles = cols // LANES
    plane = (tiles, levels * rows, LANES)
    flat = [pltpu.with_memory_space_constraint(a, pltpu.HBM) for a in flat]
    head = (ITERS + (samples + 3) * tiles, levels, LANES)
    to_near, to_far, to_far_tail, *staged = call(
        edge_kernel,
        [halo, head, (ITERS - 1, *halo[1:]), (tiles, samples, levels * rows, LANES)] + [plane] * 3 + [jax.ShapeDtypeStruct(plane, sea_mask.dtype)],
        *flat,
        scratch=[pltpu.SemaphoreType.DMA((tiles, 5))],
        in_space=pltpu.HBM,
    )
    near = lax.ppermute(to_near, "lat", pair)
    far = lax.ppermute(to_far, "lat", across)
    far_tail = lax.ppermute(to_far_tail, "lat", across)
    flat_plane = plane[1:]
    message = (high // 2, levels, LANES)
    to_east, to_west = call(
        message_kernel,
        [message, message],
        *staged,
        near,
        far,
        scratch=[(samples, *flat_plane)] + [flat_plane] * 3 + [pltpu.VMEM(flat_plane, sea_mask.dtype)],
        flops=10**6,
    )
    left = lax.ppermute(to_east, "lon", east)
    right = lax.ppermute(to_west, "lon", west)
    strip = (rows, levels, LANES)
    y, w, sy, sw = call(
        own_kernel,
        [(rows, samples, levels, cols), (rows, 4, levels, cols), strip, (rows, 3, levels, LANES)],
        *staged,
        flops=10**6,
    )
    buffer = (rows + ITERS, samples, levels, cols)
    side = [(ITERS, levels, LANES), (ITERS, 3, levels, LANES)]
    x, keep, hy, hw = call(
        near_kernel,
        [y.shape, (ITERS - 1, 2, samples, levels, cols), *side],
        y,
        w,
        near,
        scratch=[(ITERS, 4, levels, cols), buffer, buffer],
        flops=10**7,
    )
    x_far, fy, fw = call(
        far_kernel,
        [(ITERS, samples, levels, cols), *side],
        y,
        w,
        keep,
        far,
        far_tail,
        scratch=[(ITERS, 4, levels, cols), (samples, levels, cols)],
        flops=10**6,
    )
    stage = (tiles, samples, levels * rows, LANES)
    x, part = call(
        finish_kernel,
        [stage, (2, LANES)],
        x,
        x_far,
        w,
        sy,
        sw,
        hy,
        hw,
        fy,
        fw,
        left,
        right,
    )
    spread = jnp.broadcast_to(part, (n_lat * n_lon, 2, LANES))
    every = lax.all_to_all(spread, ("lat", "lon"), 0, 0, tiled=True)
    out, mean = call(
        scale_kernel,
        [(samples, levels * rows, cols), (1, 1)],
        x,
        every,
        scratch=[stage, pltpu.SemaphoreType.DMA((tiles, samples))],
        out_space=[pl.ANY, pltpu.VMEM],
    )
    return out.reshape(noise.shape), mean.reshape(())


def solution(mesh):
    grid = P(None, "lat", "lon")
    field = P(None, None, "lat", "lon")
    return jax.shard_map(
        shards,
        mesh=mesh,
        in_specs=(field, grid, grid, grid, grid),
        out_specs=(field, P()),
        check_vma=False,
    )
```

```python
import functools

import jax
import jax.numpy as jnp
from jax import lax
from jax.experimental import pallas as pl
from jax.experimental.pallas import tpu as pltpu
from jax.sharding import PartitionSpec as P

ITERS = 4
LANES = 128
SEG = 32
F32 = jnp.float32


def cell_weights(k11, k22, shear, mask):
    m = mask.astype(F32)
    return m * k11, m * k22, m * (0.5 * (shear * jnp.sqrt(k11 * k22)))


def centre_weight(wa, wb):
    return jnp.where(wa > 0, 1.0, 0.0) - 2.0 * (wa + wb)


def all_weights(w, sign):
    return centre_weight(w[0], w[1]), w[0], w[1], sign * w[2]


def roll(x, shift):
    n = x.shape[-1]
    shift = shift % n
    return x if shift == 0 else pltpu.roll(x, shift, x.ndim - 1)


def lane_parts(shape):
    lane = lax.broadcasted_iota(jnp.int32, shape, 1)
    return lane, lane // SEG, lane % SEG


def stencil(get_y, get_w, first, last, put):
    def products(r):
        y = get_y(r)
        w0, wa, wb, wc = get_w(r)
        return w0 * y, wa * y, wb * y, wc * y

    prev, here = products(first - 1), products(first)
    for r in range(first, last):
        after = products(r + 1)
        d, _, b, _ = here
        g = prev[3] - after[3]
        put(r, d + (prev[1] + after[1]) + roll(b + g, 1) + roll(b - g, -1))
        prev, here = here, after


def row_order(rows):
    odd = lax.rem(lax.axis_index("lat"), 2)
    step = 2 * odd - 1
    return lambda d: (1 - odd) * (rows - 1) + step * d, step.astype(F32)


def edge_kernel(n_ref, a_ref, b_ref, s_ref, m_ref, near_ref, head_ref, tail_ref, n_to, a_to, b_to, s_to, m_to, sem):
    samples, levels, tiles = n_ref.shape[0], near_ref.shape[2], n_to.shape[0]
    rows = n_ref.shape[1] // levels
    copies = []
    for c in range(tiles):
        lanes = pl.ds(c * LANES, LANES)
        for k, (ref, to) in enumerate(((a_ref, a_to), (b_ref, b_to), (s_ref, s_to), (m_ref, m_to))):
            copies.append(pltpu.make_async_copy(ref.at[:, lanes], to.at[c], sem.at[c, k]))
    for c in range(tiles):
        lanes = pl.ds(c * LANES, LANES)
        copies.append(pltpu.make_async_copy(n_ref.at[:, :, lanes], n_to.at[c], sem.at[c, 4]))
    for copy in copies:
        copy.start()
    row_at, _ = row_order(rows)
    parts = lane_parts((levels, LANES))

    def put(i, far, g, c, v):
        if not far:
            near_ref[i, g, :, pl.ds(c * LANES, LANES)] = v
        elif i == 0:
            head_ref[ITERS + g * tiles + c] = v
        else:
            tail_ref[i - 1, g, :, pl.ds(c * LANES, LANES)] = v

    blocks = [(i, far, row_at(rows - 1 - i if far else ITERS - 1 - i)) for i in range(ITERS) for far in (False, True)]
    data = {}
    for copy in copies[: 4 * tiles]:
        copy.wait()
    for i, far, r in blocks:
        at = pl.ds(r, levels, stride=rows)
        for c in range(tiles):
            for k, v in enumerate(cell_weights(a_to[c, at], b_to[c, at], s_to[c, at], m_to[c, at])):
                put(i, far, samples + k, c, v)
                data[i, far, samples + k, c] = v
    for copy in copies[4 * tiles :]:
        copy.wait()
    for i, far, r in blocks:
        for c in range(tiles):
            for s in range(samples):
                v = n_to[c, s, pl.ds(r, levels, stride=rows)]
                put(i, far, s, c, v)
                data[i, far, s, c] = v
    edges = [
        both_edges(lambda g, side: data[i, True, g, side * (tiles - 1)], samples + 3, parts) for i in range(ITERS)
    ]
    sent = messages(edges, parts)
    for d in range(2):
        for i in range(ITERS // 2):
            head_ref[d * (ITERS // 2) + i] = sent[d][i]


BATCH = 4


def replicate(values, seg):
    turned = [roll(v, SEG) for v in values]
    values = [jnp.where(seg == 1, t, v) for t, v in zip(turned, values)]
    turned = [roll(v, 2 * SEG) for v in values]
    return [jnp.where(seg >= 2, t, v) for t, v in zip(turned, values)]


def line_up(gets, samples, parts, low, high):
    _, seg, l32 = parts
    turned = [
        [(roll(get(s, low), SEG * s + 4), roll(get(s, high), SEG * s + 28)) for s in range(samples)] for get in gets
    ]
    lines = []
    for row in turned:
        line = None
        for s, (a, b) in enumerate(row):
            v = jnp.where(l32 < SEG // 2, a, b)
            line = v if line is None else jnp.where(seg == s, v, line)
        lines.append(line)
    return lines


def both_edges(get, groups, parts):
    return [jnp.where(parts[0] < LANES // 2, get(g, 0), get(g, 1)) for g in range(groups)]


def messages(both, parts):
    lane, seg, l32 = parts
    samples = len(both[0]) - 3
    lines = [[roll(row[s], SEG * s + 4) for s in range(samples)] for row in both]
    packed = [[roll(row[samples + k], 8 * k + 12) for k in range(3)] for row in both]
    packed = replicate([jnp.where(l32 < 16, a, jnp.where(l32 < 24, b, c)) for a, b, c in packed], seg)
    full = []
    for line, weights in zip(lines, packed):
        v = line[0]
        for s in range(1, samples):
            v = jnp.where(seg == s, line[s], v)
        full.append(jnp.where(l32 < 8, v, weights))
    low = lane % 8 < 4
    pairs = list(zip(full[0::2], full[1::2]))
    east = [jnp.where(low, a, roll(b, 4)) for a, b in pairs]
    west = [jnp.where(low, roll(a, -4), b) for a, b in pairs]
    return east, west


def strips(gets, samples, parts):
    _, seg, l32 = parts
    lines = line_up(gets, samples, parts, 0, 1)
    turned = [(roll(get(samples + k, 0), 4), roll(get(samples + k, 1), 28)) for get in gets for k in range(3)]
    weights = replicate([jnp.where(l32 < SEG // 2, a, b) for a, b in turned], seg)
    return lines, [weights[3 * i : 3 * i + 3] for i in range(len(gets))]


def own_row(refs, r, rows, levels):
    n_ref, a_ref, b_ref, s_ref, m_ref = refs
    at = pl.ds(row_order(rows)[0](r), levels, stride=rows)
    return [
        [n_ref[c, s, at] for s in range(n_ref.shape[1])]
        + list(cell_weights(a_ref[c, at], b_ref[c, at], s_ref[c, at], m_ref[c, at]))
        for c in range(n_ref.shape[0])
    ]


def own_gets(data):
    return [lambda g, side, row=row: row[-side][g] for row in data]


def message_kernel(n_ref, a_ref, b_ref, s_ref, m_ref, msg_ref, n_to, a_to, b_to, s_to, m_to):
    levels = msg_ref.shape[2]
    rows, samples, last = n_ref.shape[2] // levels, n_ref.shape[1], n_ref.shape[0] - 1
    parts = lane_parts((levels, LANES))
    left = lax.broadcasted_iota(jnp.int32, a_to.shape, 1) < LANES // 2
    for ref, to in ((a_ref, a_to), (b_ref, b_to), (s_ref, s_to), (m_ref, m_to)):
        to[...] = jnp.where(left, ref[0], ref[last])
    for s in range(samples):
        n_to[s] = jnp.where(left, n_ref[0, s], n_ref[last, s])
    row_at, _ = row_order(rows)
    for first in range(0, rows, BATCH):
        both = []
        for d in range(first, first + BATCH):
            at = pl.ds(row_at(d), levels, stride=rows)
            both.append([n_to[s, at] for s in range(samples)] + list(cell_weights(a_to[at], b_to[at], s_to[at], m_to[at])))
        sent = messages(both, parts)
        for d in range(2):
            for i in range(BATCH // 2):
                msg_ref[d, first // 2 + i] = sent[d][i]


def own_kernel(n_ref, a_ref, b_ref, s_ref, m_ref, y_ref, w_ref, sy_ref, sw_ref):
    rows, samples, levels, _ = y_ref.shape
    parts = lane_parts((levels, LANES))
    _, sign = row_order(rows)
    for first in range(0, rows, BATCH):
        batch = range(first, first + BATCH)
        data = [own_row((n_ref, a_ref, b_ref, s_ref, m_ref), r, rows, levels) for r in batch]
        lines, weights = strips(own_gets(data), samples, parts)
        for i, r in enumerate(batch):
            for c, values in enumerate(data[i]):
                lanes = pl.ds(c * LANES, LANES)
                for s in range(samples):
                    y_ref[r, s, :, lanes] = values[s]
                for k, v in enumerate(all_weights(values[samples:], sign)):
                    w_ref[r, k, :, lanes] = v
            sy_ref[r] = lines[i]
            for k in range(3):
                sw_ref[r, k] = weights[i][k]


def halo_gets(ref):
    last = ref.shape[3] - LANES
    return [lambda g, side, i=i: ref[i, g, :, pl.ds(side * last, LANES)] for i in range(ITERS)]


def join_kernel(own_ref, near_ref, head_ref, east_ref, west_ref):
    pairs, half = own_ref.shape[1], ITERS // 2
    parts = lane_parts(own_ref.shape[2:])
    sent = messages([both_edges(get, near_ref.shape[1], parts) for get in halo_gets(near_ref)], parts)
    for d, ref in enumerate((east_ref, west_ref)):
        for i in range(half):
            ref[i] = sent[d][i]
            ref[half + pairs + i] = head_ref[d * half + i]
        ref[half : half + pairs] = own_ref[d]


def near_kernel(y_ref, w_ref, near_ref, x_ref, keep_ref, hy_ref, hw_ref, wh_ref, p_ref, q_ref):
    rows, samples, levels, _ = y_ref.shape
    high = rows + ITERS
    _, sign = row_order(rows)
    lines, weights = strips(halo_gets(near_ref), samples, lane_parts((levels, LANES)))
    for i in range(ITERS):
        hy_ref[i] = lines[i]
        for k in range(3):
            hw_ref[i, k] = weights[i][k]
        for k, v in enumerate(all_weights([near_ref[i, samples + k] for k in range(3)], sign)):
            wh_ref[i, k] = v

    def get_w(r):
        ref, i = (wh_ref, r) if r < ITERS else (w_ref, r - ITERS)
        return [ref[i, k] for k in range(4)]

    def sample(s, carry):
        source = lambda r: near_ref[r, s] if r < ITERS else y_ref[r - ITERS, s]
        for step in range(ITERS):
            target = (p_ref, q_ref)[step % 2]

            def put(r, v, target=target, step=step):
                if step == ITERS - 1:
                    x_ref[r - ITERS, s] = v
                    return
                target[r, s] = v
                kept = r - (high - 3 - step)
                if kept >= 0:
                    keep_ref[step, kept, s] = v

            stencil(source, get_w, step + 1, high - 1 - step, put)
            source = functools.partial(lambda r, target: target[r, s], target=target)
        return carry

    lax.fori_loop(0, samples, sample, 0)


def far_kernel(y_ref, w_ref, keep_ref, head_ref, tail_ref, x_ref, hy_ref, hw_ref, wh_ref, yh_ref):
    rows, samples, levels, cols = y_ref.shape
    high = rows + ITERS
    tiles = cols // LANES
    _, sign = row_order(rows)

    def tile(i, g, c):
        return head_ref[ITERS + g * tiles + c] if i == 0 else tail_ref[i - 1, g, :, pl.ds(c * LANES, LANES)]

    for i in range(ITERS):
        for c in range(tiles):
            lanes = pl.ds(c * LANES, LANES)
            for k, v in enumerate(all_weights([tile(i, samples + k, c) for k in range(3)], sign)):
                wh_ref[i, k, :, lanes] = v
    for c in range(tiles):
        for s in range(samples):
            yh_ref[s, :, pl.ds(c * LANES, LANES)] = tile(0, s, c)
    gets = [lambda g, side, i=i: tile(i, g, side * (tiles - 1)) for i in range(ITERS)]
    lines, weights = strips(gets, samples, lane_parts((levels, LANES)))
    for i in range(ITERS):
        hy_ref[i] = lines[i]
        for k in range(3):
            hw_ref[i, k] = weights[i][k]

    def get_w(r):
        ref, i = (wh_ref, r - high) if r >= high else (w_ref, r - ITERS)
        return [ref[i, k] for k in range(4)]

    for s in range(samples):

        def source(r, s=s):
            if r < high:
                return y_ref[r - ITERS, s]
            return yh_ref[s] if r == high else tail_ref[r - high - 1, s]

        for step in range(ITERS):
            new = {}
            stencil(source, get_w, high - 1 - step, high - 1 - step + ITERS, new.__setitem__)
            if step < ITERS - 1:
                new[high - 3 - step], new[high - 2 - step] = keep_ref[step, 0, s], keep_ref[step, 1, s]
            source = new.__getitem__
        for r, v in new.items():
            x_ref[r - rows, s] = v


def finish_kernel(
    x_ref, xf_ref, w_ref, sy_ref, sw_ref, hy_ref, hw_ref, fy_ref, fw_ref, left_ref, right_ref, out_ref, var_ref, sum_ref
):
    rows, samples, levels, cols = x_ref.shape
    high = rows + 2 * ITERS
    parts = lane_parts((levels, LANES))
    lane, _, l32 = parts
    from_left, from_right = l32 < 4, l32 >= 28
    _, sign = row_order(rows)

    def strip_at(r):
        if r < ITERS:
            return hy_ref[r], [hw_ref[r, k] for k in range(3)]
        if r < ITERS + rows:
            return sy_ref[r - ITERS], [sw_ref[r - ITERS, k] for k in range(3)]
        return fy_ref[r - ITERS - rows], [fw_ref[r - ITERS - rows, k] for k in range(3)]

    field, weights = {}, {}
    for r in range(high):
        skip = 4 * (r % 2)
        values = [
            jnp.where(
                from_left,
                roll(left_ref[r // 2], -8 * g - skip),
                jnp.where(from_right, roll(right_ref[r // 2], 28 - 8 * g - skip), v),
            )
            for g, v in enumerate([strip_at(r)[0], *strip_at(r)[1]])
        ]
        field[r], weights[r] = values[0], all_weights(values[1:], sign)
    for step in range(ITERS):
        new = {}
        stencil(field.__getitem__, weights.__getitem__, step + 1, high - 1 - step, new.__setitem__)
        field = new

    total, count = None, None
    for r in range(rows):
        strip = field[ITERS + r]
        for c in range(0, cols, LANES):
            lanes = pl.ds(c, LANES)
            square = None
            for s in range(samples):
                v = x_ref[r, s, :, lanes] if r < rows - ITERS else xf_ref[r - rows + ITERS, s, :, lanes]
                if c == 0:
                    v = jnp.where(lane < 4, roll(strip, -(SEG * s + 4)), v)
                if c == cols - LANES:
                    v = jnp.where(lane >= LANES - 4, roll(strip, LANES - SEG * s - 28), v)
                out_ref[r, s, :, lanes] = v
                square = v * v if square is None else square + v * v
            var = square / samples
            var_ref[r, :, lanes] = var
            m = jnp.where(w_ref[r, 1, :, lanes] > 0, 1.0, 0.0)
            total = m * var if total is None else total + m * var
            count = m if count is None else count + m
    sum_ref[0:1] = jnp.sum(total, axis=0, keepdims=True)
    sum_ref[1:2] = jnp.sum(count, axis=0, keepdims=True)


def scale_kernel(x_ref, w_ref, var_ref, all_ref, out_ref, mean_ref, stage, mean_to, sem, mean_sem):
    rows, samples, levels, cols = x_ref.shape
    sums = jnp.sum(jnp.sum(all_ref[...], axis=0), axis=1, keepdims=True)
    mean = sums[0:1] / sums[1:2]
    mean_to[...] = mean
    copies = [pltpu.make_async_copy(mean_to, mean_ref, mean_sem)]
    copies[0].start()
    row_at, _ = row_order(rows)
    for c in range(cols // LANES):
        lanes = pl.ds(c * LANES, LANES)
        factors = []
        for r in range(rows):
            wet = w_ref[r, 1, :, lanes] > 0
            safe = jnp.where(wet, var_ref[r, :, lanes], 1.0)
            factors.append(jnp.where(wet, jnp.sqrt(mean / (safe + 1e-06)), 0.0))
        for s in range(samples):
            for r in range(rows):
                stage[c, s, pl.ds(row_at(r), levels, stride=rows)] = x_ref[r, s, :, lanes] * factors[r]
            copies.append(pltpu.make_async_copy(stage.at[c, s], out_ref.at[s, :, lanes], sem.at[c, s]))
            copies[-1].start()
    for copy in copies:
        copy.wait()


def call(kernel, out, *args, scratch=(), flops=0, in_space=None, out_space=None):
    out = [o if isinstance(o, jax.ShapeDtypeStruct) else jax.ShapeDtypeStruct(o, F32) for o in out]
    scratch = [pltpu.VMEM(o, F32) if isinstance(o, tuple) else o for o in scratch]
    return pl.pallas_call(
        kernel,
        out_shape=out,
        in_specs=[pl.BlockSpec(memory_space=in_space or pltpu.VMEM)] * len(args),
        out_specs=[pl.BlockSpec(memory_space=m) for m in out_space or [pltpu.VMEM] * len(out)],
        scratch_shapes=scratch,
        cost_estimate=pl.CostEstimate(flops=flops, bytes_accessed=sum(a.size * 4 for a in args), transcendentals=0),
        compiler_params=pltpu.CompilerParams(vmem_limit_bytes=12 << 20),
    )(*args)


def shards(noise, diff_lat, diff_lon, shear, sea_mask):
    samples, levels, rows, cols = noise.shape
    high = rows + 2 * ITERS
    flat = [noise.reshape(samples, levels * rows, cols)] + [
        a.reshape(levels * rows, cols) for a in (diff_lat, diff_lon, shear, sea_mask)
    ]
    n_lat, n_lon = lax.axis_size("lat"), lax.axis_size("lon")
    pair = [(i, i ^ 1) for i in range(n_lat)]
    across = [(i, i - 1 if i % 2 == 0 else i + 1) for i in range(1, n_lat - 1)]
    east = [(i, (i + 1) % n_lon) for i in range(n_lon)]
    west = [(j, i) for i, j in east]

    halo = (ITERS, samples + 3, levels, cols)
    tiles = cols // LANES
    plane = (tiles, levels * rows, LANES)
    flat = [pltpu.with_memory_space_constraint(a, pltpu.HBM) for a in flat]
    head = (ITERS + (samples + 3) * tiles, levels, LANES)
    to_near, to_far, to_far_tail, *staged = call(
        edge_kernel,
        [halo, head, (ITERS - 1, *halo[1:]), (tiles, samples, levels * rows, LANES)] + [plane] * 3 + [jax.ShapeDtypeStruct(plane, sea_mask.dtype)],
        *flat,
        scratch=[pltpu.SemaphoreType.DMA((tiles, 5))],
        in_space=pltpu.HBM,
    )
    near = lax.ppermute(to_near, "lat", pair)
    far = lax.ppermute(to_far, "lat", across)
    far_tail = lax.ppermute(to_far_tail, "lat", across)
    flat_plane = plane[1:]
    (own_msg,) = call(
        message_kernel,
        [(2, rows // 2, levels, LANES)],
        *staged,
        scratch=[(samples, *flat_plane)] + [flat_plane] * 3 + [pltpu.VMEM(flat_plane, sea_mask.dtype)],
        flops=10**6,
    )
    message = (high // 2, levels, LANES)
    to_east, to_west = call(join_kernel, [message, message], own_msg, near, far)
    left = lax.ppermute(to_east, "lon", east)
    right = lax.ppermute(to_west, "lon", west)
    strip = (rows, levels, LANES)
    y, w, sy, sw = call(
        own_kernel,
        [(rows, samples, levels, cols), (rows, 4, levels, cols), strip, (rows, 3, levels, LANES)],
        *staged,
        flops=10**6,
    )
    buffer = (rows + ITERS, samples, levels, cols)
    side = [(ITERS, levels, LANES), (ITERS, 3, levels, LANES)]
    x, keep, hy, hw = call(
        near_kernel,
        [y.shape, (ITERS - 1, 2, samples, levels, cols), *side],
        y,
        w,
        near,
        scratch=[(ITERS, 4, levels, cols), buffer, buffer],
        flops=10**7,
    )
    x_far, fy, fw = call(
        far_kernel,
        [(ITERS, samples, levels, cols), *side],
        y,
        w,
        keep,
        far,
        far_tail,
        scratch=[(ITERS, 4, levels, cols), (samples, levels, cols)],
        flops=10**6,
    )
    x, var, part = call(
        finish_kernel,
        [y.shape, (rows, levels, cols), (2, LANES)],
        x,
        x_far,
        w,
        sy,
        sw,
        hy,
        hw,
        fy,
        fw,
        left,
        right,
    )
    spread = jnp.broadcast_to(part, (n_lat * n_lon, 2, LANES))
    every = lax.all_to_all(spread, ("lat", "lon"), 0, 0, tiled=True)
    out, mean = call(
        scale_kernel,
        [(samples, levels * rows, cols), (1, 1)],
        x,
        w,
        var,
        every,
        scratch=[
            (tiles, samples, levels * rows, LANES),
            (1, 1),
            pltpu.SemaphoreType.DMA((tiles, samples)),
            pltpu.SemaphoreType.DMA,
        ],
        out_space=[pl.ANY, pl.ANY],
    )
    return out.reshape(noise.shape), mean.reshape(())


def solution(mesh):
    grid = P(None, "lat", "lon")
    field = P(None, None, "lat", "lon")
    return jax.shard_map(
        shards,
        mesh=mesh,
        in_specs=(field, grid, grid, grid, grid),
        out_specs=(field, P()),
        check_vma=False,
    )
```

```python
import functools

import jax
import jax.numpy as jnp
from jax import lax
from jax.experimental import pallas as pl
from jax.experimental.pallas import tpu as pltpu
from jax.sharding import PartitionSpec as P

ITERS = 4
LANES = 128
SEG = 32
F32 = jnp.float32


def cell_weights(k11, k22, shear, mask):
    m = mask.astype(F32)
    return m * k11, m * k22, m * (0.5 * (shear * jnp.sqrt(k11 * k22)))


def centre_weight(wa, wb):
    return jnp.where(wa > 0, 1.0, 0.0) - 2.0 * (wa + wb)


def all_weights(w, sign):
    return centre_weight(w[0], w[1]), w[0], w[1], sign * w[2]


def roll(x, shift):
    n = x.shape[-1]
    shift = shift % n
    return x if shift == 0 else pltpu.roll(x, shift, x.ndim - 1)


def lane_parts(shape):
    lane = lax.broadcasted_iota(jnp.int32, shape, 1)
    return lane, lane // SEG, lane % SEG


def stencil(get_y, get_w, first, last, put):
    def products(r):
        y = get_y(r)
        w0, wa, wb, wc = get_w(r)
        return w0 * y, wa * y, wb * y, wc * y

    prev, here = products(first - 1), products(first)
    for r in range(first, last):
        after = products(r + 1)
        d, _, b, _ = here
        g = prev[3] - after[3]
        put(r, d + (prev[1] + after[1]) + roll(b + g, 1) + roll(b - g, -1))
        prev, here = here, after


def row_order(rows):
    odd = lax.rem(lax.axis_index("lat"), 2)
    step = 2 * odd - 1
    return lambda d: (1 - odd) * (rows - 1) + step * d, step.astype(F32)


def edge_kernel(n_ref, a_ref, b_ref, s_ref, m_ref, near_ref, head_ref, tail_ref, n_to, a_to, b_to, s_to, m_to, sem):
    samples, levels, tiles = n_ref.shape[0], near_ref.shape[2], n_to.shape[0]
    rows = n_ref.shape[1] // levels
    copies = []
    for c in range(tiles):
        lanes = pl.ds(c * LANES, LANES)
        for k, (ref, to) in enumerate(((a_ref, a_to), (b_ref, b_to), (s_ref, s_to), (m_ref, m_to))):
            copies.append(pltpu.make_async_copy(ref.at[:, lanes], to.at[c], sem.at[c, k]))
    for c in range(tiles):
        lanes = pl.ds(c * LANES, LANES)
        copies.append(pltpu.make_async_copy(n_ref.at[:, :, lanes], n_to.at[c], sem.at[c, 4]))
    for copy in copies:
        copy.start()
    row_at, _ = row_order(rows)
    parts = lane_parts((levels, LANES))

    def put(i, far, g, c, v):
        if not far:
            near_ref[i, g, :, pl.ds(c * LANES, LANES)] = v
        elif i == 0:
            head_ref[ITERS + g * tiles + c] = v
        else:
            tail_ref[i - 1, g, :, pl.ds(c * LANES, LANES)] = v

    blocks = [(i, far, row_at(rows - 1 - i if far else ITERS - 1 - i)) for i in range(ITERS) for far in (False, True)]
    data = {}
    for copy in copies[: 4 * tiles]:
        copy.wait()
    for i, far, r in blocks:
        at = pl.ds(r, levels, stride=rows)
        for c in range(tiles):
            for k, v in enumerate(cell_weights(a_to[c, at], b_to[c, at], s_to[c, at], m_to[c, at])):
                put(i, far, samples + k, c, v)
                data[i, far, samples + k, c] = v
    for copy in copies[4 * tiles :]:
        copy.wait()
    for i, far, r in blocks:
        for c in range(tiles):
            for s in range(samples):
                v = n_to[c, s, pl.ds(r, levels, stride=rows)]
                put(i, far, s, c, v)
                data[i, far, s, c] = v
    edges = [
        both_edges(lambda g, side: data[i, True, g, side * (tiles - 1)], samples + 3, parts) for i in range(ITERS)
    ]
    sent = messages(edges, parts)
    for d in range(2):
        for i in range(ITERS // 2):
            head_ref[d * (ITERS // 2) + i] = sent[d][i]


BATCH = 4


def replicate(values, seg):
    turned = [roll(v, SEG) for v in values]
    values = [jnp.where(seg == 1, t, v) for t, v in zip(turned, values)]
    turned = [roll(v, 2 * SEG) for v in values]
    return [jnp.where(seg >= 2, t, v) for t, v in zip(turned, values)]


def line_up(gets, samples, parts, low, high):
    _, seg, l32 = parts
    turned = [
        [(roll(get(s, low), SEG * s + 4), roll(get(s, high), SEG * s + 28)) for s in range(samples)] for get in gets
    ]
    lines = []
    for row in turned:
        line = None
        for s, (a, b) in enumerate(row):
            v = jnp.where(l32 < SEG // 2, a, b)
            line = v if line is None else jnp.where(seg == s, v, line)
        lines.append(line)
    return lines


def both_edges(get, groups, parts):
    return [jnp.where(parts[0] < LANES // 2, get(g, 0), get(g, 1)) for g in range(groups)]


def messages(both, parts):
    lane, seg, l32 = parts
    samples = len(both[0]) - 3
    lines = [[roll(row[s], SEG * s + 4) for s in range(samples)] for row in both]
    packed = [[roll(row[samples + k], 8 * k + 12) for k in range(3)] for row in both]
    packed = replicate([jnp.where(l32 < 16, a, jnp.where(l32 < 24, b, c)) for a, b, c in packed], seg)
    full = []
    for line, weights in zip(lines, packed):
        v = line[0]
        for s in range(1, samples):
            v = jnp.where(seg == s, line[s], v)
        full.append(jnp.where(l32 < 8, v, weights))
    low = lane % 8 < 4
    pairs = list(zip(full[0::2], full[1::2]))
    east = [jnp.where(low, a, roll(b, 4)) for a, b in pairs]
    west = [jnp.where(low, roll(a, -4), b) for a, b in pairs]
    return east, west


def strips(gets, samples, parts):
    _, seg, l32 = parts
    lines = line_up(gets, samples, parts, 0, 1)
    turned = [(roll(get(samples + k, 0), 4), roll(get(samples + k, 1), 28)) for get in gets for k in range(3)]
    weights = replicate([jnp.where(l32 < SEG // 2, a, b) for a, b in turned], seg)
    return lines, [weights[3 * i : 3 * i + 3] for i in range(len(gets))]


def own_row(refs, r, rows, levels):
    n_ref, a_ref, b_ref, s_ref, m_ref = refs
    at = pl.ds(row_order(rows)[0](r), levels, stride=rows)
    return [
        [n_ref[c, s, at] for s in range(n_ref.shape[1])]
        + list(cell_weights(a_ref[c, at], b_ref[c, at], s_ref[c, at], m_ref[c, at]))
        for c in range(n_ref.shape[0])
    ]


def own_gets(data):
    return [lambda g, side, row=row: row[-side][g] for row in data]


def message_kernel(n_ref, a_ref, b_ref, s_ref, m_ref, msg_ref, n_to, a_to, b_to, s_to, m_to):
    levels = msg_ref.shape[2]
    rows, samples, last = n_ref.shape[2] // levels, n_ref.shape[1], n_ref.shape[0] - 1
    parts = lane_parts((levels, LANES))
    left = lax.broadcasted_iota(jnp.int32, a_to.shape, 1) < LANES // 2
    for ref, to in ((a_ref, a_to), (b_ref, b_to), (s_ref, s_to), (m_ref, m_to)):
        to[...] = jnp.where(left, ref[0], ref[last])
    for s in range(samples):
        n_to[s] = jnp.where(left, n_ref[0, s], n_ref[last, s])
    row_at, _ = row_order(rows)
    for first in range(0, rows, BATCH):
        both = []
        for d in range(first, first + BATCH):
            at = pl.ds(row_at(d), levels, stride=rows)
            both.append([n_to[s, at] for s in range(samples)] + list(cell_weights(a_to[at], b_to[at], s_to[at], m_to[at])))
        sent = messages(both, parts)
        for d in range(2):
            for i in range(BATCH // 2):
                msg_ref[d, first // 2 + i] = sent[d][i]


def own_kernel(n_ref, a_ref, b_ref, s_ref, m_ref, y_ref, w_ref, sy_ref, sw_ref):
    rows, samples, levels, _ = y_ref.shape
    parts = lane_parts((levels, LANES))
    _, sign = row_order(rows)
    for first in range(0, rows, BATCH):
        batch = range(first, first + BATCH)
        data = [own_row((n_ref, a_ref, b_ref, s_ref, m_ref), r, rows, levels) for r in batch]
        lines, weights = strips(own_gets(data), samples, parts)
        for i, r in enumerate(batch):
            for c, values in enumerate(data[i]):
                lanes = pl.ds(c * LANES, LANES)
                for s in range(samples):
                    y_ref[r, s, :, lanes] = values[s]
                for k, v in enumerate(all_weights(values[samples:], sign)):
                    w_ref[r, k, :, lanes] = v
            sy_ref[r] = lines[i]
            for k in range(3):
                sw_ref[r, k] = weights[i][k]


def halo_gets(ref):
    last = ref.shape[3] - LANES
    return [lambda g, side, i=i: ref[i, g, :, pl.ds(side * last, LANES)] for i in range(ITERS)]


def join_kernel(own_ref, near_ref, head_ref, east_ref, west_ref):
    pairs, half = own_ref.shape[1], ITERS // 2
    parts = lane_parts(own_ref.shape[2:])
    sent = messages([both_edges(get, near_ref.shape[1], parts) for get in halo_gets(near_ref)], parts)
    for d, ref in enumerate((east_ref, west_ref)):
        for i in range(half):
            ref[i] = sent[d][i]
            ref[half + pairs + i] = head_ref[d * half + i]
        ref[half : half + pairs] = own_ref[d]


def near_kernel(y_ref, w_ref, near_ref, x_ref, keep_ref, hy_ref, hw_ref, wh_ref, p_ref, q_ref):
    rows, samples, levels, _ = y_ref.shape
    high = rows + ITERS
    _, sign = row_order(rows)
    lines, weights = strips(halo_gets(near_ref), samples, lane_parts((levels, LANES)))
    for i in range(ITERS):
        hy_ref[i] = lines[i]
        for k in range(3):
            hw_ref[i, k] = weights[i][k]
        for k, v in enumerate(all_weights([near_ref[i, samples + k] for k in range(3)], sign)):
            wh_ref[i, k] = v

    def get_w(r):
        ref, i = (wh_ref, r) if r < ITERS else (w_ref, r - ITERS)
        return [ref[i, k] for k in range(4)]

    def sample(s, carry):
        source = lambda r: near_ref[r, s] if r < ITERS else y_ref[r - ITERS, s]
        for step in range(ITERS):
            target = (p_ref, q_ref)[step % 2]

            def put(r, v, target=target, step=step):
                if step == ITERS - 1:
                    x_ref[r - ITERS, s] = v
                    return
                target[r, s] = v
                kept = r - (high - 3 - step)
                if kept >= 0:
                    keep_ref[step, kept, s] = v

            stencil(source, get_w, step + 1, high - 1 - step, put)
            source = functools.partial(lambda r, target: target[r, s], target=target)
        return carry

    lax.fori_loop(0, samples, sample, 0)


def far_kernel(y_ref, w_ref, keep_ref, head_ref, tail_ref, x_ref, hy_ref, hw_ref, wh_ref, yh_ref):
    rows, samples, levels, cols = y_ref.shape
    high = rows + ITERS
    tiles = cols // LANES
    _, sign = row_order(rows)

    def tile(i, g, c):
        return head_ref[ITERS + g * tiles + c] if i == 0 else tail_ref[i - 1, g, :, pl.ds(c * LANES, LANES)]

    for i in range(ITERS):
        for c in range(tiles):
            lanes = pl.ds(c * LANES, LANES)
            for k, v in enumerate(all_weights([tile(i, samples + k, c) for k in range(3)], sign)):
                wh_ref[i, k, :, lanes] = v
    for c in range(tiles):
        for s in range(samples):
            yh_ref[s, :, pl.ds(c * LANES, LANES)] = tile(0, s, c)
    gets = [lambda g, side, i=i: tile(i, g, side * (tiles - 1)) for i in range(ITERS)]
    lines, weights = strips(gets, samples, lane_parts((levels, LANES)))
    for i in range(ITERS):
        hy_ref[i] = lines[i]
        for k in range(3):
            hw_ref[i, k] = weights[i][k]

    def get_w(r):
        ref, i = (wh_ref, r - high) if r >= high else (w_ref, r - ITERS)
        return [ref[i, k] for k in range(4)]

    for s in range(samples):

        def source(r, s=s):
            if r < high:
                return y_ref[r - ITERS, s]
            return yh_ref[s] if r == high else tail_ref[r - high - 1, s]

        for step in range(ITERS):
            new = {}
            stencil(source, get_w, high - 1 - step, high - 1 - step + ITERS, new.__setitem__)
            if step < ITERS - 1:
                new[high - 3 - step], new[high - 2 - step] = keep_ref[step, 0, s], keep_ref[step, 1, s]
            source = new.__getitem__
        for r, v in new.items():
            x_ref[r - rows, s] = v


def finish_kernel(
    x_ref, xf_ref, w_ref, sy_ref, sw_ref, hy_ref, hw_ref, fy_ref, fw_ref, left_ref, right_ref, out_ref, var_ref, sum_ref
):
    rows, samples, levels, cols = x_ref.shape
    high = rows + 2 * ITERS
    parts = lane_parts((levels, LANES))
    lane, _, l32 = parts
    from_left, from_right = l32 < 4, l32 >= 28
    _, sign = row_order(rows)

    def strip_at(r):
        if r < ITERS:
            return hy_ref[r], [hw_ref[r, k] for k in range(3)]
        if r < ITERS + rows:
            return sy_ref[r - ITERS], [sw_ref[r - ITERS, k] for k in range(3)]
        return fy_ref[r - ITERS - rows], [fw_ref[r - ITERS - rows, k] for k in range(3)]

    field, weights = {}, {}
    for r in range(high):
        skip = 4 * (r % 2)
        values = [
            jnp.where(
                from_left,
                roll(left_ref[r // 2], -8 * g - skip),
                jnp.where(from_right, roll(right_ref[r // 2], 28 - 8 * g - skip), v),
            )
            for g, v in enumerate([strip_at(r)[0], *strip_at(r)[1]])
        ]
        field[r], weights[r] = values[0], all_weights(values[1:], sign)
    for step in range(ITERS):
        new = {}
        stencil(field.__getitem__, weights.__getitem__, step + 1, high - 1 - step, new.__setitem__)
        field = new

    total, count = None, None
    for r in range(rows):
        strip = field[ITERS + r]
        for c in range(0, cols, LANES):
            lanes = pl.ds(c, LANES)
            square = None
            for s in range(samples):
                v = x_ref[r, s, :, lanes] if r < rows - ITERS else xf_ref[r - rows + ITERS, s, :, lanes]
                if c == 0:
                    v = jnp.where(lane < 4, roll(strip, -(SEG * s + 4)), v)
                if c == cols - LANES:
                    v = jnp.where(lane >= LANES - 4, roll(strip, LANES - SEG * s - 28), v)
                out_ref[r, s, :, lanes] = v
                square = v * v if square is None else square + v * v
            var = square / samples
            var_ref[r, :, lanes] = var
            m = jnp.where(w_ref[r, 1, :, lanes] > 0, 1.0, 0.0)
            total = m * var if total is None else total + m * var
            count = m if count is None else count + m
    total, count = [jnp.sum(v, axis=0, keepdims=True) for v in (total, count)]
    low = lax.broadcasted_iota(jnp.int32, total.shape, 1) < LANES // 2
    sum_ref[...] = jnp.where(low, total + roll(total, LANES // 2), count + roll(count, LANES // 2))


def scale_kernel(x_ref, w_ref, var_ref, all_ref, out_ref, mean_ref, stage, mean_to, sem, mean_sem):
    rows, samples, levels, cols = x_ref.shape
    sums = jnp.sum(all_ref[...], axis=0)
    low = lax.broadcasted_iota(jnp.int32, sums.shape, 1) < LANES // 2
    total, count = [jnp.sum(jnp.where(m, sums, 0.0), axis=1, keepdims=True) for m in (low, ~low)]
    mean = total / count
    mean_to[...] = mean
    copies = [pltpu.make_async_copy(mean_to, mean_ref, mean_sem)]
    copies[0].start()
    row_at, _ = row_order(rows)
    for c in range(cols // LANES):
        lanes = pl.ds(c * LANES, LANES)
        factors = []
        for r in range(rows):
            wet = w_ref[r, 1, :, lanes] > 0
            safe = jnp.where(wet, var_ref[r, :, lanes], 1.0)
            factors.append(jnp.where(wet, jnp.sqrt(mean / (safe + 1e-06)), 0.0))
        for s in range(samples):
            for r in range(rows):
                stage[c, s, pl.ds(row_at(r), levels, stride=rows)] = x_ref[r, s, :, lanes] * factors[r]
            copies.append(pltpu.make_async_copy(stage.at[c, s], out_ref.at[s, :, lanes], sem.at[c, s]))
            copies[-1].start()
    for copy in copies:
        copy.wait()


def call(kernel, out, *args, scratch=(), flops=0, in_space=None, out_space=None):
    out = [o if isinstance(o, jax.ShapeDtypeStruct) else jax.ShapeDtypeStruct(o, F32) for o in out]
    scratch = [pltpu.VMEM(o, F32) if isinstance(o, tuple) else o for o in scratch]
    return pl.pallas_call(
        kernel,
        out_shape=out,
        in_specs=[pl.BlockSpec(memory_space=in_space or pltpu.VMEM)] * len(args),
        out_specs=[pl.BlockSpec(memory_space=m) for m in out_space or [pltpu.VMEM] * len(out)],
        scratch_shapes=scratch,
        cost_estimate=pl.CostEstimate(flops=flops, bytes_accessed=sum(a.size * 4 for a in args), transcendentals=0),
        compiler_params=pltpu.CompilerParams(vmem_limit_bytes=12 << 20),
    )(*args)


def shards(noise, diff_lat, diff_lon, shear, sea_mask):
    samples, levels, rows, cols = noise.shape
    high = rows + 2 * ITERS
    flat = [noise.reshape(samples, levels * rows, cols)] + [
        a.reshape(levels * rows, cols) for a in (diff_lat, diff_lon, shear, sea_mask)
    ]
    n_lat, n_lon = lax.axis_size("lat"), lax.axis_size("lon")
    pair = [(i, i ^ 1) for i in range(n_lat)]
    across = [(i, i - 1 if i % 2 == 0 else i + 1) for i in range(1, n_lat - 1)]
    east = [(i, (i + 1) % n_lon) for i in range(n_lon)]
    west = [(j, i) for i, j in east]

    halo = (ITERS, samples + 3, levels, cols)
    tiles = cols // LANES
    plane = (tiles, levels * rows, LANES)
    flat = [pltpu.with_memory_space_constraint(a, pltpu.HBM) for a in flat]
    head = (ITERS + (samples + 3) * tiles, levels, LANES)
    to_near, to_far, to_far_tail, *staged = call(
        edge_kernel,
        [halo, head, (ITERS - 1, *halo[1:]), (tiles, samples, levels * rows, LANES)] + [plane] * 3 + [jax.ShapeDtypeStruct(plane, sea_mask.dtype)],
        *flat,
        scratch=[pltpu.SemaphoreType.DMA((tiles, 5))],
        in_space=pltpu.HBM,
    )
    near = lax.ppermute(to_near, "lat", pair)
    far = lax.ppermute(to_far, "lat", across)
    far_tail = lax.ppermute(to_far_tail, "lat", across)
    flat_plane = plane[1:]
    (own_msg,) = call(
        message_kernel,
        [(2, rows // 2, levels, LANES)],
        *staged,
        scratch=[(samples, *flat_plane)] + [flat_plane] * 3 + [pltpu.VMEM(flat_plane, sea_mask.dtype)],
        flops=10**6,
    )
    message = (high // 2, levels, LANES)
    to_east, to_west = call(join_kernel, [message, message], own_msg, near, far)
    left = lax.ppermute(to_east, "lon", east)
    right = lax.ppermute(to_west, "lon", west)
    strip = (rows, levels, LANES)
    y, w, sy, sw = call(
        own_kernel,
        [(rows, samples, levels, cols), (rows, 4, levels, cols), strip, (rows, 3, levels, LANES)],
        *staged,
        flops=10**6,
    )
    buffer = (rows + ITERS, samples, levels, cols)
    side = [(ITERS, levels, LANES), (ITERS, 3, levels, LANES)]
    x, keep, hy, hw = call(
        near_kernel,
        [y.shape, (ITERS - 1, 2, samples, levels, cols), *side],
        y,
        w,
        near,
        scratch=[(ITERS, 4, levels, cols), buffer, buffer],
        flops=10**7,
    )
    x_far, fy, fw = call(
        far_kernel,
        [(ITERS, samples, levels, cols), *side],
        y,
        w,
        keep,
        far,
        far_tail,
        scratch=[(ITERS, 4, levels, cols), (samples, levels, cols)],
        flops=10**6,
    )
    x, var, part = call(
        finish_kernel,
        [y.shape, (rows, levels, cols), (1, LANES)],
        x,
        x_far,
        w,
        sy,
        sw,
        hy,
        hw,
        fy,
        fw,
        left,
        right,
    )
    spread = jnp.broadcast_to(part, (n_lat * n_lon, 1, LANES))
    every = lax.all_to_all(spread, ("lat", "lon"), 0, 0, tiled=True)
    out, mean = call(
        scale_kernel,
        [(samples, levels * rows, cols), (1, 1)],
        x,
        w,
        var,
        every,
        scratch=[
            (tiles, samples, levels * rows, LANES),
            (1, 1),
            pltpu.SemaphoreType.DMA((tiles, samples)),
            pltpu.SemaphoreType.DMA,
        ],
        out_space=[pl.ANY, pl.ANY],
    )
    return out.reshape(noise.shape), mean.reshape(())


def solution(mesh):
    grid = P(None, "lat", "lon")
    field = P(None, None, "lat", "lon")
    return jax.shard_map(
        shards,
        mesh=mesh,
        in_specs=(field, grid, grid, grid, grid),
        out_specs=(field, P()),
        check_vma=False,
    )
```

```python
import functools

import jax
import jax.numpy as jnp
from jax import lax
from jax.experimental import pallas as pl
from jax.experimental.pallas import tpu as pltpu
from jax.sharding import PartitionSpec as P

ITERS = 4
LANES = 128
SEG = 32
F32 = jnp.float32


def cell_weights(k11, k22, shear, mask):
    m = mask.astype(F32)
    return m * k11, m * k22, m * (0.5 * (shear * jnp.sqrt(k11 * k22)))


def centre_weight(wa, wb):
    return jnp.where(wa > 0, 1.0, 0.0) - 2.0 * (wa + wb)


def all_weights(w, sign):
    return centre_weight(w[0], w[1]), w[0], w[1], sign * w[2]


def roll(x, shift):
    n = x.shape[-1]
    shift = shift % n
    return x if shift == 0 else pltpu.roll(x, shift, x.ndim - 1)


def lane_parts(shape):
    lane = lax.broadcasted_iota(jnp.int32, shape, 1)
    return lane, lane // SEG, lane % SEG


def stencil(get_y, get_w, first, last, put):
    def products(r):
        y = get_y(r)
        w0, wa, wb, wc = get_w(r)
        return w0 * y, wa * y, wb * y, wc * y

    prev, here = products(first - 1), products(first)
    for r in range(first, last):
        after = products(r + 1)
        d, _, b, _ = here
        g = prev[3] - after[3]
        put(r, d + (prev[1] + after[1]) + roll(b + g, 1) + roll(b - g, -1))
        prev, here = here, after


def row_order(rows):
    odd = lax.rem(lax.axis_index("lat"), 2)
    step = 2 * odd - 1
    return lambda d: (1 - odd) * (rows - 1) + step * d, step.astype(F32)


def edge_kernel(n_ref, a_ref, b_ref, s_ref, m_ref, near_ref, head_ref, tail_ref, n_to, a_to, b_to, s_to, m_to, sem):
    samples, levels, tiles = n_ref.shape[0], near_ref.shape[2], n_to.shape[0]
    rows = n_ref.shape[1] // levels
    copies = []
    for c in range(tiles):
        lanes = pl.ds(c * LANES, LANES)
        for k, (ref, to) in enumerate(((a_ref, a_to), (b_ref, b_to), (s_ref, s_to), (m_ref, m_to))):
            copies.append(pltpu.make_async_copy(ref.at[:, lanes], to.at[c], sem.at[c, k]))
    for c in range(tiles):
        lanes = pl.ds(c * LANES, LANES)
        copies.append(pltpu.make_async_copy(n_ref.at[:, :, lanes], n_to.at[c], sem.at[c, 4]))
    for copy in copies:
        copy.start()
    row_at, _ = row_order(rows)
    parts = lane_parts((levels, LANES))

    def put(i, far, g, c, v):
        if not far:
            near_ref[i, g, :, pl.ds(c * LANES, LANES)] = v
        elif i == 0:
            head_ref[2 + g * tiles + c] = v
        else:
            tail_ref[i - 1, g, :, pl.ds(c * LANES, LANES)] = v

    blocks = [(i, far, row_at(rows - 1 - i if far else ITERS - 1 - i)) for i in range(ITERS) for far in (False, True)]
    data = {}
    for copy in copies[: 4 * tiles]:
        copy.wait()
    for i, far, r in blocks:
        at = pl.ds(r, levels, stride=rows)
        for c in range(tiles):
            for k, v in enumerate(cell_weights(a_to[c, at], b_to[c, at], s_to[c, at], m_to[c, at])):
                put(i, far, samples + k, c, v)
                data[i, far, samples + k, c] = v
    for copy in copies[4 * tiles :]:
        copy.wait()
    for i, far, r in blocks:
        for c in range(tiles):
            for s in range(samples):
                v = n_to[c, s, pl.ds(r, levels, stride=rows)]
                put(i, far, s, c, v)
                data[i, far, s, c] = v
    edges = [
        both_edges(lambda g, side: data[i, True, g, side * (tiles - 1)], samples + 3, parts) for i in range(ITERS)
    ]
    head_ref[0], head_ref[1] = messages(edges, parts)


BATCH = 4


def replicate(values, seg):
    turned = [roll(v, SEG) for v in values]
    values = [jnp.where(seg == 1, t, v) for t, v in zip(turned, values)]
    turned = [roll(v, 2 * SEG) for v in values]
    return [jnp.where(seg >= 2, t, v) for t, v in zip(turned, values)]


def line_up(gets, samples, parts, low, high):
    _, seg, l32 = parts
    turned = [
        [(roll(get(s, low), SEG * s + 4), roll(get(s, high), SEG * s + 28)) for s in range(samples)] for get in gets
    ]
    lines = []
    for row in turned:
        line = None
        for s, (a, b) in enumerate(row):
            v = jnp.where(l32 < SEG // 2, a, b)
            line = v if line is None else jnp.where(seg == s, v, line)
        lines.append(line)
    return lines


def both_edges(get, groups, parts):
    return [jnp.where(parts[0] < LANES // 2, get(g, 0), get(g, 1)) for g in range(groups)]


def by_segment(values, seg, first):
    line = values[0]
    for i, v in enumerate(values[1:]):
        line = jnp.where(seg == first + 1 + i, v, line)
    return line


def messages(both, parts):
    _, seg, l32 = parts
    samples = len(both[0]) - 3
    slot = l32 // 4
    east = west = None
    for j, row in enumerate(both):
        line = by_segment([roll(row[s], SEG * s + 4 * j + 4) for s in range(samples)], seg, 0)
        turned = [roll(row[samples + k], SEG * k + 4 * j + 20) for k in range(3)]
        weights = by_segment(turned, seg, 0)
        east = line if east is None else jnp.where(slot == j, line, east)
        west = line if west is None else jnp.where(slot == j + 1, line, west)
        east = jnp.where(slot == 4 + j, weights, east)
        if j < BATCH - 1:
            west = jnp.where(slot == 5 + j, weights, west)
        else:
            west = jnp.where(slot == 0, by_segment(turned, seg, 1), west)
    return east, west


def unpack(tile, parts, from_east):
    _, seg, _ = parts
    turned = [roll(tile, SEG * q) for q in range(4)]
    every = [by_segment([turned[(q - k) % 4] for q in range(4)], seg, 0) for k in range(4 if from_east else 3)]
    rows = []
    for j in range(BATCH):
        if not from_east:
            rows.append([roll(tile, -4 * j)] + [roll(every[k], -16 - 4 * j) for k in range(3)])
        elif j < BATCH - 1:
            rows.append([roll(tile, 24 - 4 * j)] + [roll(every[k], 8 - 4 * j) for k in range(3)])
        else:
            rows.append([roll(tile, 24 - 4 * j)] + [roll(every[k + 1], 28) for k in range(3)])
    return rows


def strips(gets, samples, parts):
    _, seg, l32 = parts
    lines = line_up(gets, samples, parts, 0, 1)
    turned = [(roll(get(samples + k, 0), 4), roll(get(samples + k, 1), 28)) for get in gets for k in range(3)]
    weights = replicate([jnp.where(l32 < SEG // 2, a, b) for a, b in turned], seg)
    return lines, [weights[3 * i : 3 * i + 3] for i in range(len(gets))]


def own_row(refs, r, rows, levels):
    n_ref, a_ref, b_ref, s_ref, m_ref = refs
    at = pl.ds(row_order(rows)[0](r), levels, stride=rows)
    return [
        [n_ref[c, s, at] for s in range(n_ref.shape[1])]
        + list(cell_weights(a_ref[c, at], b_ref[c, at], s_ref[c, at], m_ref[c, at]))
        for c in range(n_ref.shape[0])
    ]


def own_gets(data):
    return [lambda g, side, row=row: row[-side][g] for row in data]


def message_kernel(n_ref, a_ref, b_ref, s_ref, m_ref, msg_ref, n_to, a_to, b_to, s_to, m_to):
    levels = msg_ref.shape[2]
    rows, samples, last = n_ref.shape[2] // levels, n_ref.shape[1], n_ref.shape[0] - 1
    parts = lane_parts((levels, LANES))
    left = lax.broadcasted_iota(jnp.int32, a_to.shape, 1) < LANES // 2
    for ref, to in ((a_ref, a_to), (b_ref, b_to), (s_ref, s_to), (m_ref, m_to)):
        to[...] = jnp.where(left, ref[0], ref[last])
    for s in range(samples):
        n_to[s] = jnp.where(left, n_ref[0, s], n_ref[last, s])
    row_at, _ = row_order(rows)
    for first in range(0, rows, BATCH):
        both = []
        for d in range(first, first + BATCH):
            at = pl.ds(row_at(d), levels, stride=rows)
            both.append([n_to[s, at] for s in range(samples)] + list(cell_weights(a_to[at], b_to[at], s_to[at], m_to[at])))
        msg_ref[0, first // BATCH], msg_ref[1, first // BATCH] = messages(both, parts)


def own_kernel(n_ref, a_ref, b_ref, s_ref, m_ref, y_ref, w_ref, sy_ref, sw_ref):
    rows, samples, levels, _ = y_ref.shape
    parts = lane_parts((levels, LANES))
    _, sign = row_order(rows)
    for first in range(0, rows, BATCH):
        batch = range(first, first + BATCH)
        data = [own_row((n_ref, a_ref, b_ref, s_ref, m_ref), r, rows, levels) for r in batch]
        lines, weights = strips(own_gets(data), samples, parts)
        for i, r in enumerate(batch):
            for c, values in enumerate(data[i]):
                lanes = pl.ds(c * LANES, LANES)
                for s in range(samples):
                    y_ref[r, s, :, lanes] = values[s]
                for k, v in enumerate(all_weights(values[samples:], sign)):
                    w_ref[r, k, :, lanes] = v
            sy_ref[r] = lines[i]
            for k in range(3):
                sw_ref[r, k] = weights[i][k]


def halo_gets(ref):
    last = ref.shape[3] - LANES
    return [lambda g, side, i=i: ref[i, g, :, pl.ds(side * last, LANES)] for i in range(ITERS)]


def join_kernel(own_ref, near_ref, head_ref, east_ref, west_ref):
    tiles = own_ref.shape[1]
    parts = lane_parts(own_ref.shape[2:])
    sent = messages([both_edges(get, near_ref.shape[1], parts) for get in halo_gets(near_ref)], parts)
    for d, ref in enumerate((east_ref, west_ref)):
        ref[0] = sent[d]
        ref[1 : 1 + tiles] = own_ref[d]
        ref[1 + tiles] = head_ref[d]


def near_kernel(y_ref, w_ref, near_ref, x_ref, keep_ref, hy_ref, hw_ref, wh_ref, p_ref, q_ref):
    rows, samples, levels, _ = y_ref.shape
    high = rows + ITERS
    _, sign = row_order(rows)
    lines, weights = strips(halo_gets(near_ref), samples, lane_parts((levels, LANES)))
    for i in range(ITERS):
        hy_ref[i] = lines[i]
        for k in range(3):
            hw_ref[i, k] = weights[i][k]
        for k, v in enumerate(all_weights([near_ref[i, samples + k] for k in range(3)], sign)):
            wh_ref[i, k] = v

    def get_w(r):
        ref, i = (wh_ref, r) if r < ITERS else (w_ref, r - ITERS)
        return [ref[i, k] for k in range(4)]

    def sample(s, carry):
        source = lambda r: near_ref[r, s] if r < ITERS else y_ref[r - ITERS, s]
        for step in range(ITERS):
            target = (p_ref, q_ref)[step % 2]

            def put(r, v, target=target, step=step):
                if step == ITERS - 1:
                    x_ref[r - ITERS, s] = v
                    return
                target[r, s] = v
                kept = r - (high - 3 - step)
                if kept >= 0:
                    keep_ref[step, kept, s] = v

            stencil(source, get_w, step + 1, high - 1 - step, put)
            source = functools.partial(lambda r, target: target[r, s], target=target)
        return carry

    lax.fori_loop(0, samples, sample, 0)


def far_kernel(y_ref, w_ref, keep_ref, head_ref, tail_ref, x_ref, hy_ref, hw_ref, wh_ref, yh_ref):
    rows, samples, levels, cols = y_ref.shape
    high = rows + ITERS
    tiles = cols // LANES
    _, sign = row_order(rows)

    def tile(i, g, c):
        return head_ref[2 + g * tiles + c] if i == 0 else tail_ref[i - 1, g, :, pl.ds(c * LANES, LANES)]

    for i in range(ITERS):
        for c in range(tiles):
            lanes = pl.ds(c * LANES, LANES)
            for k, v in enumerate(all_weights([tile(i, samples + k, c) for k in range(3)], sign)):
                wh_ref[i, k, :, lanes] = v
    for c in range(tiles):
        for s in range(samples):
            yh_ref[s, :, pl.ds(c * LANES, LANES)] = tile(0, s, c)
    gets = [lambda g, side, i=i: tile(i, g, side * (tiles - 1)) for i in range(ITERS)]
    lines, weights = strips(gets, samples, lane_parts((levels, LANES)))
    for i in range(ITERS):
        hy_ref[i] = lines[i]
        for k in range(3):
            hw_ref[i, k] = weights[i][k]

    def get_w(r):
        ref, i = (wh_ref, r - high) if r >= high else (w_ref, r - ITERS)
        return [ref[i, k] for k in range(4)]

    for s in range(samples):

        def source(r, s=s):
            if r < high:
                return y_ref[r - ITERS, s]
            return yh_ref[s] if r == high else tail_ref[r - high - 1, s]

        for step in range(ITERS):
            new = {}
            stencil(source, get_w, high - 1 - step, high - 1 - step + ITERS, new.__setitem__)
            if step < ITERS - 1:
                new[high - 3 - step], new[high - 2 - step] = keep_ref[step, 0, s], keep_ref[step, 1, s]
            source = new.__getitem__
        for r, v in new.items():
            x_ref[r - rows, s] = v


def finish_kernel(
    x_ref, xf_ref, w_ref, sy_ref, sw_ref, hy_ref, hw_ref, fy_ref, fw_ref, left_ref, right_ref, out_ref, var_ref, sum_ref
):
    rows, samples, levels, cols = x_ref.shape
    high = rows + 2 * ITERS
    parts = lane_parts((levels, LANES))
    lane, _, l32 = parts
    from_left, from_right = l32 < 4, l32 >= 28
    _, sign = row_order(rows)

    def strip_at(r):
        if r < ITERS:
            return hy_ref[r], [hw_ref[r, k] for k in range(3)]
        if r < ITERS + rows:
            return sy_ref[r - ITERS], [sw_ref[r - ITERS, k] for k in range(3)]
        return fy_ref[r - ITERS - rows], [fw_ref[r - ITERS - rows, k] for k in range(3)]

    lefts = [row for q in range(high // BATCH) for row in unpack(left_ref[q], parts, False)]
    rights = [row for q in range(high // BATCH) for row in unpack(right_ref[q], parts, True)]
    field, weights = {}, {}
    for r in range(high):
        y, w = strip_at(r)
        values = [
            jnp.where(from_left, a, jnp.where(from_right, b, v)) for a, b, v in zip(lefts[r], rights[r], [y, *w])
        ]
        field[r], weights[r] = values[0], all_weights(values[1:], sign)
    for step in range(ITERS):
        new = {}
        stencil(field.__getitem__, weights.__getitem__, step + 1, high - 1 - step, new.__setitem__)
        field = new

    total, count = None, None
    for r in range(rows):
        strip = field[ITERS + r]
        for c in range(0, cols, LANES):
            lanes = pl.ds(c, LANES)
            square = None
            for s in range(samples):
                v = x_ref[r, s, :, lanes] if r < rows - ITERS else xf_ref[r - rows + ITERS, s, :, lanes]
                if c == 0:
                    v = jnp.where(lane < 4, roll(strip, -(SEG * s + 4)), v)
                if c == cols - LANES:
                    v = jnp.where(lane >= LANES - 4, roll(strip, LANES - SEG * s - 28), v)
                out_ref[r, s, :, lanes] = v
                square = v * v if square is None else square + v * v
            var = square / samples
            var_ref[r, :, lanes] = var
            m = jnp.where(w_ref[r, 1, :, lanes] > 0, 1.0, 0.0)
            total = m * var if total is None else total + m * var
            count = m if count is None else count + m
    total, count = [jnp.sum(v, axis=0, keepdims=True) for v in (total, count)]
    low = lax.broadcasted_iota(jnp.int32, total.shape, 1) < LANES // 2
    sum_ref[...] = jnp.where(low, total + roll(total, LANES // 2), count + roll(count, LANES // 2))


def scale_kernel(x_ref, w_ref, var_ref, all_ref, out_ref, mean_ref, stage, mean_to, sem, mean_sem):
    rows, samples, levels, cols = x_ref.shape
    sums = jnp.sum(all_ref[...], axis=0)
    low = lax.broadcasted_iota(jnp.int32, sums.shape, 1) < LANES // 2
    total, count = [jnp.sum(jnp.where(m, sums, 0.0), axis=1, keepdims=True) for m in (low, ~low)]
    mean = total / count
    mean_to[...] = mean
    copies = [pltpu.make_async_copy(mean_to, mean_ref, mean_sem)]
    copies[0].start()
    row_at, _ = row_order(rows)
    for c in range(cols // LANES):
        lanes = pl.ds(c * LANES, LANES)
        factors = []
        for r in range(rows):
            wet = w_ref[r, 1, :, lanes] > 0
            safe = jnp.where(wet, var_ref[r, :, lanes], 1.0)
            factors.append(jnp.where(wet, jnp.sqrt(mean / (safe + 1e-06)), 0.0))
        for s in range(samples):
            for r in range(rows):
                stage[c, s, pl.ds(row_at(r), levels, stride=rows)] = x_ref[r, s, :, lanes] * factors[r]
            copies.append(pltpu.make_async_copy(stage.at[c, s], out_ref.at[s, :, lanes], sem.at[c, s]))
            copies[-1].start()
    for copy in copies:
        copy.wait()


def call(kernel, out, *args, scratch=(), flops=0, in_space=None, out_space=None):
    out = [o if isinstance(o, jax.ShapeDtypeStruct) else jax.ShapeDtypeStruct(o, F32) for o in out]
    scratch = [pltpu.VMEM(o, F32) if isinstance(o, tuple) else o for o in scratch]
    return pl.pallas_call(
        kernel,
        out_shape=out,
        in_specs=[pl.BlockSpec(memory_space=in_space or pltpu.VMEM)] * len(args),
        out_specs=[pl.BlockSpec(memory_space=m) for m in out_space or [pltpu.VMEM] * len(out)],
        scratch_shapes=scratch,
        cost_estimate=pl.CostEstimate(flops=flops, bytes_accessed=sum(a.size * 4 for a in args), transcendentals=0),
        compiler_params=pltpu.CompilerParams(vmem_limit_bytes=12 << 20),
    )(*args)


def shards(noise, diff_lat, diff_lon, shear, sea_mask):
    samples, levels, rows, cols = noise.shape
    high = rows + 2 * ITERS
    flat = [noise.reshape(samples, levels * rows, cols)] + [
        a.reshape(levels * rows, cols) for a in (diff_lat, diff_lon, shear, sea_mask)
    ]
    n_lat, n_lon = lax.axis_size("lat"), lax.axis_size("lon")
    pair = [(i, i ^ 1) for i in range(n_lat)]
    across = [(i, i - 1 if i % 2 == 0 else i + 1) for i in range(1, n_lat - 1)]
    east = [(i, (i + 1) % n_lon) for i in range(n_lon)]
    west = [(j, i) for i, j in east]

    halo = (ITERS, samples + 3, levels, cols)
    tiles = cols // LANES
    plane = (tiles, levels * rows, LANES)
    flat = [pltpu.with_memory_space_constraint(a, pltpu.HBM) for a in flat]
    head = (2 + (samples + 3) * tiles, levels, LANES)
    to_near, to_far, to_far_tail, *staged = call(
        edge_kernel,
        [halo, head, (ITERS - 1, *halo[1:]), (tiles, samples, levels * rows, LANES)] + [plane] * 3 + [jax.ShapeDtypeStruct(plane, sea_mask.dtype)],
        *flat,
        scratch=[pltpu.SemaphoreType.DMA((tiles, 5))],
        in_space=pltpu.HBM,
    )
    near = lax.ppermute(to_near, "lat", pair)
    far = lax.ppermute(to_far, "lat", across)
    far_tail = lax.ppermute(to_far_tail, "lat", across)
    flat_plane = plane[1:]
    (own_msg,) = call(
        message_kernel,
        [(2, rows // BATCH, levels, LANES)],
        *staged,
        scratch=[(samples, *flat_plane)] + [flat_plane] * 3 + [pltpu.VMEM(flat_plane, sea_mask.dtype)],
        flops=10**6,
    )
    message = (high // BATCH, levels, LANES)
    to_east, to_west = call(join_kernel, [message, message], own_msg, near, far)
    left = lax.ppermute(to_east, "lon", east)
    right = lax.ppermute(to_west, "lon", west)
    strip = (rows, levels, LANES)
    y, w, sy, sw = call(
        own_kernel,
        [(rows, samples, levels, cols), (rows, 4, levels, cols), strip, (rows, 3, levels, LANES)],
        *staged,
        flops=10**6,
    )
    buffer = (rows + ITERS, samples, levels, cols)
    side = [(ITERS, levels, LANES), (ITERS, 3, levels, LANES)]
    x, keep, hy, hw = call(
        near_kernel,
        [y.shape, (ITERS - 1, 2, samples, levels, cols), *side],
        y,
        w,
        near,
        scratch=[(ITERS, 4, levels, cols), buffer, buffer],
        flops=10**7,
    )
    x_far, fy, fw = call(
        far_kernel,
        [(ITERS, samples, levels, cols), *side],
        y,
        w,
        keep,
        far,
        far_tail,
        scratch=[(ITERS, 4, levels, cols), (samples, levels, cols)],
        flops=10**6,
    )
    x, var, part = call(
        finish_kernel,
        [y.shape, (rows, levels, cols), (1, LANES)],
        x,
        x_far,
        w,
        sy,
        sw,
        hy,
        hw,
        fy,
        fw,
        left,
        right,
    )
    spread = jnp.broadcast_to(part, (n_lat * n_lon, 1, LANES))
    every = lax.all_to_all(spread, ("lat", "lon"), 0, 0, tiled=True)
    out, mean = call(
        scale_kernel,
        [(samples, levels * rows, cols), (1, 1)],
        x,
        w,
        var,
        every,
        scratch=[
            (tiles, samples, levels * rows, LANES),
            (1, 1),
            pltpu.SemaphoreType.DMA((tiles, samples)),
            pltpu.SemaphoreType.DMA,
        ],
        out_space=[pl.ANY, pl.ANY],
    )
    return out.reshape(noise.shape), mean.reshape(())


def solution(mesh):
    grid = P(None, "lat", "lon")
    field = P(None, None, "lat", "lon")
    return jax.shard_map(
        shards,
        mesh=mesh,
        in_specs=(field, grid, grid, grid, grid),
        out_specs=(field, P()),
        check_vma=False,
    )
```

```python
import functools

import jax
import jax.numpy as jnp
from jax import lax
from jax.experimental import pallas as pl
from jax.experimental.pallas import tpu as pltpu
from jax.sharding import PartitionSpec as P

ITERS = 4
LANES = 128
SEG = 32
F32 = jnp.float32


def cell_weights(k11, k22, shear, mask):
    m = mask.astype(F32)
    return m * k11, m * k22, m * (0.5 * (shear * jnp.sqrt(k11 * k22)))


def centre_weight(wa, wb):
    return jnp.where(wa > 0, 1.0, 0.0) - 2.0 * (wa + wb)


def all_weights(w, sign):
    return centre_weight(w[0], w[1]), w[0], w[1], sign * w[2]


def roll(x, shift):
    n = x.shape[-1]
    shift = shift % n
    return x if shift == 0 else pltpu.roll(x, shift, x.ndim - 1)


def lane_parts(shape):
    lane = lax.broadcasted_iota(jnp.int32, shape, 1)
    return lane, lane // SEG, lane % SEG


def stencil(get_y, get_w, first, last, put):
    def products(r):
        y = get_y(r)
        w0, wa, wb, wc = get_w(r)
        return w0 * y, wa * y, wb * y, wc * y

    prev, here = products(first - 1), products(first)
    for r in range(first, last):
        after = products(r + 1)
        d, _, b, _ = here
        g = prev[3] - after[3]
        put(r, d + (prev[1] + after[1]) + roll(b + g, 1) + roll(b - g, -1))
        prev, here = here, after


def row_order(rows):
    odd = lax.rem(lax.axis_index("lat"), 2)
    step = 2 * odd - 1
    return lambda d: (1 - odd) * (rows - 1) + step * d, step.astype(F32)


def edge_kernel(n_ref, a_ref, b_ref, s_ref, m_ref, near_ref, head_ref, tail_ref, n_to, a_to, b_to, s_to, m_to, sem):
    samples, levels, tiles = n_ref.shape[0], near_ref.shape[2], n_to.shape[0]
    rows = n_ref.shape[1] // levels
    copies = []
    for c in range(tiles):
        lanes = pl.ds(c * LANES, LANES)
        for k, (ref, to) in enumerate(((a_ref, a_to), (b_ref, b_to), (s_ref, s_to), (m_ref, m_to))):
            copies.append(pltpu.make_async_copy(ref.at[:, lanes], to.at[c], sem.at[c, k]))
    for c in range(tiles):
        lanes = pl.ds(c * LANES, LANES)
        copies.append(pltpu.make_async_copy(n_ref.at[:, :, lanes], n_to.at[c], sem.at[c, 4]))
    for copy in copies:
        copy.start()
    row_at, _ = row_order(rows)
    parts = lane_parts((levels, LANES))

    def put(i, far, g, c, v):
        if not far:
            near_ref[i, g, :, pl.ds(c * LANES, LANES)] = v
        elif i == 0:
            head_ref[2 + g * tiles + c] = v
        else:
            tail_ref[i - 1, g, :, pl.ds(c * LANES, LANES)] = v

    blocks = [(i, far, row_at(rows - 1 - i if far else ITERS - 1 - i)) for i in range(ITERS) for far in (False, True)]
    data = {}
    for copy in copies[: 4 * tiles]:
        copy.wait()
    for i, far, r in blocks:
        at = pl.ds(r, levels, stride=rows)
        for c in range(tiles):
            for k, v in enumerate(cell_weights(a_to[c, at], b_to[c, at], s_to[c, at], m_to[c, at])):
                put(i, far, samples + k, c, v)
                data[i, far, samples + k, c] = v
    for copy in copies[4 * tiles :]:
        copy.wait()
    for i, far, r in blocks:
        for c in range(tiles):
            for s in range(samples):
                v = n_to[c, s, pl.ds(r, levels, stride=rows)]
                put(i, far, s, c, v)
                data[i, far, s, c] = v
    edges = [
        both_edges(lambda g, side: data[i, True, g, side * (tiles - 1)], samples + 3, parts) for i in range(ITERS)
    ]
    head_ref[0], head_ref[1] = messages(edges, parts)


BATCH = 4


def replicate(values, seg):
    turned = [roll(v, SEG) for v in values]
    values = [jnp.where(seg == 1, t, v) for t, v in zip(turned, values)]
    turned = [roll(v, 2 * SEG) for v in values]
    return [jnp.where(seg >= 2, t, v) for t, v in zip(turned, values)]


def line_up(gets, samples, parts, low, high):
    _, seg, l32 = parts
    turned = [
        [(roll(get(s, low), SEG * s + 4), roll(get(s, high), SEG * s + 28)) for s in range(samples)] for get in gets
    ]
    lines = []
    for row in turned:
        line = None
        for s, (a, b) in enumerate(row):
            v = jnp.where(l32 < SEG // 2, a, b)
            line = v if line is None else jnp.where(seg == s, v, line)
        lines.append(line)
    return lines


def both_edges(get, groups, parts):
    return [jnp.where(parts[0] < LANES // 2, get(g, 0), get(g, 1)) for g in range(groups)]


def by_segment(values, seg, first):
    line = values[0]
    for i, v in enumerate(values[1:]):
        line = jnp.where(seg == first + 1 + i, v, line)
    return line


def messages(both, parts):
    _, seg, l32 = parts
    samples = len(both[0]) - 3
    slot = l32 // 4
    east = west = None
    for j, row in enumerate(both):
        line = by_segment([roll(row[s], SEG * s + 4 * j + 4) for s in range(samples)], seg, 0)
        turned = [roll(row[samples + k], SEG * k + 4 * j + 20) for k in range(3)]
        weights = by_segment(turned, seg, 0)
        east = line if east is None else jnp.where(slot == j, line, east)
        west = line if west is None else jnp.where(slot == j + 1, line, west)
        east = jnp.where(slot == 4 + j, weights, east)
        if j < BATCH - 1:
            west = jnp.where(slot == 5 + j, weights, west)
        else:
            west = jnp.where(slot == 0, by_segment(turned, seg, 1), west)
    return east, west


def unpack(tile, parts, from_east):
    _, seg, _ = parts
    turned = [roll(tile, SEG * q) for q in range(4)]
    every = [by_segment([turned[(q - k) % 4] for q in range(4)], seg, 0) for k in range(4 if from_east else 3)]
    rows = []
    for j in range(BATCH):
        if not from_east:
            rows.append([roll(tile, -4 * j)] + [roll(every[k], -16 - 4 * j) for k in range(3)])
        elif j < BATCH - 1:
            rows.append([roll(tile, 24 - 4 * j)] + [roll(every[k], 8 - 4 * j) for k in range(3)])
        else:
            rows.append([roll(tile, 24 - 4 * j)] + [roll(every[k + 1], 28) for k in range(3)])
    return rows


def strips(gets, samples, parts):
    _, seg, l32 = parts
    lines = line_up(gets, samples, parts, 0, 1)
    turned = [(roll(get(samples + k, 0), 4), roll(get(samples + k, 1), 28)) for get in gets for k in range(3)]
    weights = replicate([jnp.where(l32 < SEG // 2, a, b) for a, b in turned], seg)
    return lines, [weights[3 * i : 3 * i + 3] for i in range(len(gets))]


def own_row(refs, r, rows, levels):
    n_ref, a_ref, b_ref, s_ref, m_ref = refs
    at = pl.ds(row_order(rows)[0](r), levels, stride=rows)
    return [
        [n_ref[c, s, at] for s in range(n_ref.shape[1])]
        + list(cell_weights(a_ref[c, at], b_ref[c, at], s_ref[c, at], m_ref[c, at]))
        for c in range(n_ref.shape[0])
    ]


def own_gets(data):
    return [lambda g, side, row=row: row[-side][g] for row in data]


def message_kernel(n_ref, a_ref, b_ref, s_ref, m_ref, msg_ref, n_to, a_to, b_to, s_to, m_to):
    levels = msg_ref.shape[2]
    rows, samples, last = n_ref.shape[2] // levels, n_ref.shape[1], n_ref.shape[0] - 1
    parts = lane_parts((levels, LANES))
    left = lax.broadcasted_iota(jnp.int32, a_to.shape, 1) < LANES // 2
    for ref, to in ((a_ref, a_to), (b_ref, b_to), (s_ref, s_to), (m_ref, m_to)):
        to[...] = jnp.where(left, ref[0], ref[last])
    for s in range(samples):
        n_to[s] = jnp.where(left, n_ref[0, s], n_ref[last, s])
    row_at, _ = row_order(rows)
    for first in range(0, rows, BATCH):
        both = []
        for d in range(first, first + BATCH):
            at = pl.ds(row_at(d), levels, stride=rows)
            both.append([n_to[s, at] for s in range(samples)] + list(cell_weights(a_to[at], b_to[at], s_to[at], m_to[at])))
        msg_ref[0, first // BATCH], msg_ref[1, first // BATCH] = messages(both, parts)


def own_kernel(n_ref, a_ref, b_ref, s_ref, m_ref, y_ref, w_ref, sy_ref, sw_ref):
    rows, samples, levels, _ = y_ref.shape
    parts = lane_parts((levels, LANES))
    _, sign = row_order(rows)
    for first in range(0, rows, BATCH):
        batch = range(first, first + BATCH)
        data = [own_row((n_ref, a_ref, b_ref, s_ref, m_ref), r, rows, levels) for r in batch]
        lines, weights = strips(own_gets(data), samples, parts)
        for i, r in enumerate(batch):
            for c, values in enumerate(data[i]):
                lanes = pl.ds(c * LANES, LANES)
                for s in range(samples):
                    y_ref[r, s, :, lanes] = values[s]
                for k, v in enumerate(all_weights(values[samples:], sign)):
                    w_ref[r, k, :, lanes] = v
            sy_ref[r] = lines[i]
            for k in range(3):
                sw_ref[r, k] = weights[i][k]


def halo_gets(ref):
    last = ref.shape[3] - LANES
    return [lambda g, side, i=i: ref[i, g, :, pl.ds(side * last, LANES)] for i in range(ITERS)]


def join_kernel(own_ref, near_ref, head_ref, east_ref, west_ref):
    tiles = own_ref.shape[1]
    parts = lane_parts(own_ref.shape[2:])
    sent = messages([both_edges(get, near_ref.shape[1], parts) for get in halo_gets(near_ref)], parts)
    for d, ref in enumerate((east_ref, west_ref)):
        ref[0] = sent[d]
        ref[1 : 1 + tiles] = own_ref[d]
        ref[1 + tiles] = head_ref[d]


def near_kernel(y_ref, w_ref, near_ref, x_ref, keep_ref, hy_ref, hw_ref, wh_ref, p_ref, q_ref):
    rows, samples, levels, _ = y_ref.shape
    high = rows + ITERS
    _, sign = row_order(rows)
    lines, weights = strips(halo_gets(near_ref), samples, lane_parts((levels, LANES)))
    for i in range(ITERS):
        hy_ref[i] = lines[i]
        for k in range(3):
            hw_ref[i, k] = weights[i][k]
        for k, v in enumerate(all_weights([near_ref[i, samples + k] for k in range(3)], sign)):
            wh_ref[i, k] = v

    def get_w(r):
        ref, i = (wh_ref, r) if r < ITERS else (w_ref, r - ITERS)
        return [ref[i, k] for k in range(4)]

    def sample(s, carry):
        source = lambda r: near_ref[r, s] if r < ITERS else y_ref[r - ITERS, s]
        for step in range(ITERS):
            target = (p_ref, q_ref)[step % 2]

            def put(r, v, target=target, step=step):
                if step == ITERS - 1:
                    x_ref[r - ITERS, s] = v
                    return
                target[r, s] = v
                kept = r - (high - 3 - step)
                if kept >= 0:
                    keep_ref[step, kept, s] = v

            stencil(source, get_w, step + 1, high - 1 - step, put)
            source = functools.partial(lambda r, target: target[r, s], target=target)
        return carry

    lax.fori_loop(0, samples, sample, 0)


def far_kernel(y_ref, w_ref, keep_ref, head_ref, tail_ref, x_ref, hy_ref, hw_ref, wh_ref, yh_ref):
    rows, samples, levels, cols = y_ref.shape
    high = rows + ITERS
    tiles = cols // LANES
    _, sign = row_order(rows)

    def tile(i, g, c):
        return head_ref[2 + g * tiles + c] if i == 0 else tail_ref[i - 1, g, :, pl.ds(c * LANES, LANES)]

    for i in range(ITERS):
        for c in range(tiles):
            lanes = pl.ds(c * LANES, LANES)
            for k, v in enumerate(all_weights([tile(i, samples + k, c) for k in range(3)], sign)):
                wh_ref[i, k, :, lanes] = v
    for c in range(tiles):
        for s in range(samples):
            yh_ref[s, :, pl.ds(c * LANES, LANES)] = tile(0, s, c)
    gets = [lambda g, side, i=i: tile(i, g, side * (tiles - 1)) for i in range(ITERS)]
    lines, weights = strips(gets, samples, lane_parts((levels, LANES)))
    for i in range(ITERS):
        hy_ref[i] = lines[i]
        for k in range(3):
            hw_ref[i, k] = weights[i][k]

    def get_w(r):
        ref, i = (wh_ref, r - high) if r >= high else (w_ref, r - ITERS)
        return [ref[i, k] for k in range(4)]

    for s in range(samples):

        def source(r, s=s):
            if r < high:
                return y_ref[r - ITERS, s]
            return yh_ref[s] if r == high else tail_ref[r - high - 1, s]

        for step in range(ITERS):
            new = {}
            stencil(source, get_w, high - 1 - step, high - 1 - step + ITERS, new.__setitem__)
            if step < ITERS - 1:
                new[high - 3 - step], new[high - 2 - step] = keep_ref[step, 0, s], keep_ref[step, 1, s]
            source = new.__getitem__
        for r, v in new.items():
            x_ref[r - rows, s] = v


def finish_kernel(
    x_ref, xf_ref, w_ref, sy_ref, sw_ref, hy_ref, hw_ref, fy_ref, fw_ref, left_ref, right_ref, out_ref, var_ref, sum_ref,
    line_ref,
):
    rows, samples, levels, cols = x_ref.shape
    high = rows + 2 * ITERS
    parts = lane_parts((levels, LANES))
    lane, _, l32 = parts
    from_left, from_right = l32 < 4, l32 >= 28
    _, sign = row_order(rows)

    def strip_at(r):
        if r < ITERS:
            return hy_ref[r], [hw_ref[r, k] for k in range(3)]
        if r < ITERS + rows:
            return sy_ref[r - ITERS], [sw_ref[r - ITERS, k] for k in range(3)]
        return fy_ref[r - ITERS - rows], [fw_ref[r - ITERS - rows, k] for k in range(3)]

    for q in range(high // BATCH):
        lefts, rights = unpack(left_ref[q], parts, False), unpack(right_ref[q], parts, True)
        for j in range(BATCH):
            y, w = strip_at(q * BATCH + j)
            values = [
                jnp.where(from_left, a, jnp.where(from_right, b, v)) for a, b, v in zip(lefts[j], rights[j], [y, *w])
            ]
            for k, v in enumerate([values[0], *all_weights(values[1:], sign)]):
                line_ref[q * BATCH + j, k] = v

    def get_w(r):
        return [line_ref[r, 1 + k] for k in range(4)]

    field = {r: line_ref[r, 0] for r in range(high)}
    for step in range(ITERS):
        new = {}
        stencil(field.__getitem__, get_w, step + 1, high - 1 - step, new.__setitem__)
        field = new

    total, count = None, None
    for r in range(rows):
        strip = field[ITERS + r]
        for c in range(0, cols, LANES):
            lanes = pl.ds(c, LANES)
            square = None
            for s in range(samples):
                v = x_ref[r, s, :, lanes] if r < rows - ITERS else xf_ref[r - rows + ITERS, s, :, lanes]
                if c == 0:
                    v = jnp.where(lane < 4, roll(strip, -(SEG * s + 4)), v)
                if c == cols - LANES:
                    v = jnp.where(lane >= LANES - 4, roll(strip, LANES - SEG * s - 28), v)
                out_ref[r, s, :, lanes] = v
                square = v * v if square is None else square + v * v
            var = square / samples
            var_ref[r, :, lanes] = var
            m = jnp.where(w_ref[r, 1, :, lanes] > 0, 1.0, 0.0)
            total = m * var if total is None else total + m * var
            count = m if count is None else count + m
    total, count = [jnp.sum(v, axis=0, keepdims=True) for v in (total, count)]
    low = lax.broadcasted_iota(jnp.int32, total.shape, 1) < LANES // 2
    sum_ref[...] = jnp.where(low, total + roll(total, LANES // 2), count + roll(count, LANES // 2))


def scale_kernel(x_ref, w_ref, var_ref, all_ref, out_ref, mean_ref, stage, mean_to, sem, mean_sem):
    rows, samples, levels, cols = x_ref.shape
    sums = jnp.sum(all_ref[...], axis=0)
    low = lax.broadcasted_iota(jnp.int32, sums.shape, 1) < LANES // 2
    total, count = [jnp.sum(jnp.where(m, sums, 0.0), axis=1, keepdims=True) for m in (low, ~low)]
    mean = total / count
    mean_to[...] = mean
    copies = [pltpu.make_async_copy(mean_to, mean_ref, mean_sem)]
    copies[0].start()
    row_at, _ = row_order(rows)
    for c in range(cols // LANES):
        lanes = pl.ds(c * LANES, LANES)
        factors = []
        for r in range(rows):
            wet = w_ref[r, 1, :, lanes] > 0
            safe = jnp.where(wet, var_ref[r, :, lanes], 1.0)
            factors.append(jnp.where(wet, jnp.sqrt(mean / (safe + 1e-06)), 0.0))
        for s in range(samples):
            for r in range(rows):
                stage[c, s, pl.ds(row_at(r), levels, stride=rows)] = x_ref[r, s, :, lanes] * factors[r]
            copies.append(pltpu.make_async_copy(stage.at[c, s], out_ref.at[s, :, lanes], sem.at[c, s]))
            copies[-1].start()
    for copy in copies:
        copy.wait()


def call(kernel, out, *args, scratch=(), flops=0, in_space=None, out_space=None):
    out = [o if isinstance(o, jax.ShapeDtypeStruct) else jax.ShapeDtypeStruct(o, F32) for o in out]
    scratch = [pltpu.VMEM(o, F32) if isinstance(o, tuple) else o for o in scratch]
    return pl.pallas_call(
        kernel,
        out_shape=out,
        in_specs=[pl.BlockSpec(memory_space=in_space or pltpu.VMEM)] * len(args),
        out_specs=[pl.BlockSpec(memory_space=m) for m in out_space or [pltpu.VMEM] * len(out)],
        scratch_shapes=scratch,
        cost_estimate=pl.CostEstimate(flops=flops, bytes_accessed=sum(a.size * 4 for a in args), transcendentals=0),
        compiler_params=pltpu.CompilerParams(vmem_limit_bytes=12 << 20),
    )(*args)


def shards(noise, diff_lat, diff_lon, shear, sea_mask):
    samples, levels, rows, cols = noise.shape
    high = rows + 2 * ITERS
    flat = [noise.reshape(samples, levels * rows, cols)] + [
        a.reshape(levels * rows, cols) for a in (diff_lat, diff_lon, shear, sea_mask)
    ]
    n_lat, n_lon = lax.axis_size("lat"), lax.axis_size("lon")
    pair = [(i, i ^ 1) for i in range(n_lat)]
    across = [(i, i - 1 if i % 2 == 0 else i + 1) for i in range(1, n_lat - 1)]
    east = [(i, (i + 1) % n_lon) for i in range(n_lon)]
    west = [(j, i) for i, j in east]

    halo = (ITERS, samples + 3, levels, cols)
    tiles = cols // LANES
    plane = (tiles, levels * rows, LANES)
    flat = [pltpu.with_memory_space_constraint(a, pltpu.HBM) for a in flat]
    head = (2 + (samples + 3) * tiles, levels, LANES)
    to_near, to_far, to_far_tail, *staged = call(
        edge_kernel,
        [halo, head, (ITERS - 1, *halo[1:]), (tiles, samples, levels * rows, LANES)] + [plane] * 3 + [jax.ShapeDtypeStruct(plane, sea_mask.dtype)],
        *flat,
        scratch=[pltpu.SemaphoreType.DMA((tiles, 5))],
        in_space=pltpu.HBM,
    )
    near = lax.ppermute(to_near, "lat", pair)
    far = lax.ppermute(to_far, "lat", across)
    far_tail = lax.ppermute(to_far_tail, "lat", across)
    flat_plane = plane[1:]
    (own_msg,) = call(
        message_kernel,
        [(2, rows // BATCH, levels, LANES)],
        *staged,
        scratch=[(samples, *flat_plane)] + [flat_plane] * 3 + [pltpu.VMEM(flat_plane, sea_mask.dtype)],
        flops=10**6,
    )
    message = (high // BATCH, levels, LANES)
    to_east, to_west = call(join_kernel, [message, message], own_msg, near, far)
    left = lax.ppermute(to_east, "lon", east)
    right = lax.ppermute(to_west, "lon", west)
    strip = (rows, levels, LANES)
    y, w, sy, sw = call(
        own_kernel,
        [(rows, samples, levels, cols), (rows, 4, levels, cols), strip, (rows, 3, levels, LANES)],
        *staged,
        flops=10**6,
    )
    buffer = (rows + ITERS, samples, levels, cols)
    side = [(ITERS, levels, LANES), (ITERS, 3, levels, LANES)]
    x, keep, hy, hw = call(
        near_kernel,
        [y.shape, (ITERS - 1, 2, samples, levels, cols), *side],
        y,
        w,
        near,
        scratch=[(ITERS, 4, levels, cols), buffer, buffer],
        flops=10**7,
    )
    x_far, fy, fw = call(
        far_kernel,
        [(ITERS, samples, levels, cols), *side],
        y,
        w,
        keep,
        far,
        far_tail,
        scratch=[(ITERS, 4, levels, cols), (samples, levels, cols)],
        flops=10**6,
    )
    x, var, part = call(
        finish_kernel,
        [y.shape, (rows, levels, cols), (1, LANES)],
        x,
        x_far,
        w,
        sy,
        sw,
        hy,
        hw,
        fy,
        fw,
        left,
        right,
        scratch=[(high, 5, levels, LANES)],
    )
    spread = jnp.broadcast_to(part, (n_lat * n_lon, 1, LANES))
    every = lax.all_to_all(spread, ("lat", "lon"), 0, 0, tiled=True)
    out, mean = call(
        scale_kernel,
        [(samples, levels * rows, cols), (1, 1)],
        x,
        w,
        var,
        every,
        scratch=[
            (tiles, samples, levels * rows, LANES),
            (1, 1),
            pltpu.SemaphoreType.DMA((tiles, samples)),
            pltpu.SemaphoreType.DMA,
        ],
        out_space=[pl.ANY, pl.ANY],
    )
    return out.reshape(noise.shape), mean.reshape(())


def solution(mesh):
    grid = P(None, "lat", "lon")
    field = P(None, None, "lat", "lon")
    return jax.shard_map(
        shards,
        mesh=mesh,
        in_specs=(field, grid, grid, grid, grid),
        out_specs=(field, P()),
        check_vma=False,
    )
```

```python
import functools

import jax
import jax.numpy as jnp
from jax import lax
from jax.experimental import pallas as pl
from jax.experimental.pallas import tpu as pltpu
from jax.sharding import PartitionSpec as P

ITERS = 4
LANES = 128
SEG = 32
F32 = jnp.float32


def cell_weights(k11, k22, shear, mask):
    m = mask.astype(F32)
    return m * k11, m * k22, m * (0.5 * (shear * jnp.sqrt(k11 * k22)))


def centre_weight(wa, wb):
    return jnp.where(wa > 0, 1.0, 0.0) - 2.0 * (wa + wb)


def all_weights(w, sign):
    return centre_weight(w[0], w[1]), w[0], w[1], sign * w[2]


def roll(x, shift):
    n = x.shape[-1]
    shift = shift % n
    return x if shift == 0 else pltpu.roll(x, shift, x.ndim - 1)


def lane_parts(shape):
    lane = lax.broadcasted_iota(jnp.int32, shape, 1)
    return lane, lane // SEG, lane % SEG


def stencil(get_y, get_w, first, last, put):
    def products(r):
        y = get_y(r)
        w0, wa, wb, wc = get_w(r)
        return w0 * y, wa * y, wb * y, wc * y

    prev, here = products(first - 1), products(first)
    for r in range(first, last):
        after = products(r + 1)
        d, _, b, _ = here
        g = prev[3] - after[3]
        put(r, d + (prev[1] + after[1]) + roll(b + g, 1) + roll(b - g, -1))
        prev, here = here, after


def row_order(rows):
    odd = lax.rem(lax.axis_index("lat"), 2)
    step = 2 * odd - 1
    return lambda d: (1 - odd) * (rows - 1) + step * d, step.astype(F32)


def edge_kernel(n_ref, a_ref, b_ref, s_ref, m_ref, near_ref, head_ref, tail_ref, n_to, a_to, b_to, s_to, m_to, sem):
    samples, levels, tiles = n_ref.shape[0], near_ref.shape[2], n_to.shape[0]
    rows = n_ref.shape[1] // levels
    copies = []
    for c in range(tiles):
        lanes = pl.ds(c * LANES, LANES)
        for k, (ref, to) in enumerate(((a_ref, a_to), (b_ref, b_to), (s_ref, s_to), (m_ref, m_to))):
            copies.append(pltpu.make_async_copy(ref.at[:, lanes], to.at[c], sem.at[c, k]))
    for c in range(tiles):
        lanes = pl.ds(c * LANES, LANES)
        copies.append(pltpu.make_async_copy(n_ref.at[:, :, lanes], n_to.at[c], sem.at[c, 4]))
    for copy in copies:
        copy.start()
    row_at, _ = row_order(rows)
    parts = lane_parts((levels, LANES))

    def put(i, far, g, c, v):
        if not far:
            near_ref[i, g, :, pl.ds(c * LANES, LANES)] = v
        elif i == 0:
            head_ref[2 + g * tiles + c] = v
        else:
            tail_ref[i - 1, g, :, pl.ds(c * LANES, LANES)] = v

    blocks = [(i, far, row_at(rows - 1 - i if far else ITERS - 1 - i)) for i in range(ITERS) for far in (False, True)]
    data = {}
    for copy in copies[: 4 * tiles]:
        copy.wait()
    for i, far, r in blocks:
        at = pl.ds(r, levels, stride=rows)
        for c in range(tiles):
            for k, v in enumerate(cell_weights(a_to[c, at], b_to[c, at], s_to[c, at], m_to[c, at])):
                put(i, far, samples + k, c, v)
                data[i, far, samples + k, c] = v
    for copy in copies[4 * tiles :]:
        copy.wait()
    for i, far, r in blocks:
        for c in range(tiles):
            for s in range(samples):
                v = n_to[c, s, pl.ds(r, levels, stride=rows)]
                put(i, far, s, c, v)
                data[i, far, s, c] = v
    edges = [
        both_edges(lambda g, side: data[i, True, g, side * (tiles - 1)], samples + 3, parts) for i in range(ITERS)
    ]
    head_ref[0], head_ref[1] = messages(edges, parts)


BATCH = 4


def replicate(values, seg):
    turned = [roll(v, SEG) for v in values]
    values = [jnp.where(seg == 1, t, v) for t, v in zip(turned, values)]
    turned = [roll(v, 2 * SEG) for v in values]
    return [jnp.where(seg >= 2, t, v) for t, v in zip(turned, values)]


def line_up(gets, samples, parts, low, high):
    _, seg, l32 = parts
    turned = [
        [(roll(get(s, low), SEG * s + 4), roll(get(s, high), SEG * s + 28)) for s in range(samples)] for get in gets
    ]
    lines = []
    for row in turned:
        line = None
        for s, (a, b) in enumerate(row):
            v = jnp.where(l32 < SEG // 2, a, b)
            line = v if line is None else jnp.where(seg == s, v, line)
        lines.append(line)
    return lines


def both_edges(get, groups, parts):
    return [jnp.where(parts[0] < LANES // 2, get(g, 0), get(g, 1)) for g in range(groups)]


def by_segment(values, seg, first):
    line = values[0]
    for i, v in enumerate(values[1:]):
        line = jnp.where(seg == first + 1 + i, v, line)
    return line


def messages(both, parts):
    _, seg, l32 = parts
    samples = len(both[0]) - 3
    slot = l32 // 4
    east = west = None
    for j, row in enumerate(both):
        line = by_segment([roll(row[s], SEG * s + 4 * j + 4) for s in range(samples)], seg, 0)
        turned = [roll(row[samples + k], SEG * k + 4 * j + 20) for k in range(3)]
        weights = by_segment(turned, seg, 0)
        east = line if east is None else jnp.where(slot == j, line, east)
        west = line if west is None else jnp.where(slot == j + 1, line, west)
        east = jnp.where(slot == 4 + j, weights, east)
        if j < BATCH - 1:
            west = jnp.where(slot == 5 + j, weights, west)
        else:
            west = jnp.where(slot == 0, by_segment(turned, seg, 1), west)
    return east, west


def turns(tile):
    return [roll(tile, SEG * q) for q in range(4)]


def unpack(turned, parts, from_east):
    _, seg, _ = parts
    tile = turned[0]
    every = [by_segment([turned[(q - k) % 4] for q in range(4)], seg, 0) for k in range(4 if from_east else 3)]
    rows = []
    for j in range(BATCH):
        if not from_east:
            rows.append([roll(tile, -4 * j)] + [roll(every[k], -16 - 4 * j) for k in range(3)])
        elif j < BATCH - 1:
            rows.append([roll(tile, 24 - 4 * j)] + [roll(every[k], 8 - 4 * j) for k in range(3)])
        else:
            rows.append([roll(tile, 24 - 4 * j)] + [roll(every[k + 1], 28) for k in range(3)])
    return rows


def strips(gets, samples, parts):
    _, seg, l32 = parts
    lines = line_up(gets, samples, parts, 0, 1)
    turned = [(roll(get(samples + k, 0), 4), roll(get(samples + k, 1), 28)) for get in gets for k in range(3)]
    weights = replicate([jnp.where(l32 < SEG // 2, a, b) for a, b in turned], seg)
    return lines, [weights[3 * i : 3 * i + 3] for i in range(len(gets))]


def own_row(refs, r, rows, levels):
    n_ref, a_ref, b_ref, s_ref, m_ref = refs
    at = pl.ds(row_order(rows)[0](r), levels, stride=rows)
    return [
        [n_ref[c, s, at] for s in range(n_ref.shape[1])]
        + list(cell_weights(a_ref[c, at], b_ref[c, at], s_ref[c, at], m_ref[c, at]))
        for c in range(n_ref.shape[0])
    ]


def own_gets(data):
    return [lambda g, side, row=row: row[-side][g] for row in data]


def message_kernel(n_ref, a_ref, b_ref, s_ref, m_ref, msg_ref, n_to, a_to, b_to, s_to, m_to):
    levels = msg_ref.shape[2]
    rows, samples, last = n_ref.shape[2] // levels, n_ref.shape[1], n_ref.shape[0] - 1
    parts = lane_parts((levels, LANES))
    left = lax.broadcasted_iota(jnp.int32, a_to.shape, 1) < LANES // 2
    for ref, to in ((a_ref, a_to), (b_ref, b_to), (s_ref, s_to), (m_ref, m_to)):
        to[...] = jnp.where(left, ref[0], ref[last])
    for s in range(samples):
        n_to[s] = jnp.where(left, n_ref[0, s], n_ref[last, s])
    row_at, _ = row_order(rows)
    for first in range(0, rows, BATCH):
        both = []
        for d in range(first, first + BATCH):
            at = pl.ds(row_at(d), levels, stride=rows)
            both.append([n_to[s, at] for s in range(samples)] + list(cell_weights(a_to[at], b_to[at], s_to[at], m_to[at])))
        msg_ref[0, first // BATCH], msg_ref[1, first // BATCH] = messages(both, parts)


def own_kernel(n_ref, a_ref, b_ref, s_ref, m_ref, y_ref, w_ref, sy_ref, sw_ref):
    rows, samples, levels, _ = y_ref.shape
    parts = lane_parts((levels, LANES))
    _, sign = row_order(rows)
    for first in range(0, rows, BATCH):
        batch = range(first, first + BATCH)
        data = [own_row((n_ref, a_ref, b_ref, s_ref, m_ref), r, rows, levels) for r in batch]
        lines, weights = strips(own_gets(data), samples, parts)
        for i, r in enumerate(batch):
            for c, values in enumerate(data[i]):
                lanes = pl.ds(c * LANES, LANES)
                for s in range(samples):
                    y_ref[r, s, :, lanes] = values[s]
                for k, v in enumerate(all_weights(values[samples:], sign)):
                    w_ref[r, k, :, lanes] = v
            sy_ref[r] = lines[i]
            for k in range(3):
                sw_ref[r, k] = weights[i][k]


def halo_gets(ref):
    last = ref.shape[3] - LANES
    return [lambda g, side, i=i: ref[i, g, :, pl.ds(side * last, LANES)] for i in range(ITERS)]


def join_kernel(own_ref, near_ref, head_ref, east_ref, west_ref):
    tiles = own_ref.shape[1]
    parts = lane_parts(own_ref.shape[2:])
    sent = messages([both_edges(get, near_ref.shape[1], parts) for get in halo_gets(near_ref)], parts)
    for d, ref in enumerate((east_ref, west_ref)):
        ref[0] = sent[d]
        ref[1 : 1 + tiles] = own_ref[d]
        ref[1 + tiles] = head_ref[d]


def near_kernel(y_ref, w_ref, near_ref, x_ref, keep_ref, hy_ref, hw_ref, wh_ref, p_ref, q_ref):
    rows, samples, levels, _ = y_ref.shape
    high = rows + ITERS
    _, sign = row_order(rows)
    lines, weights = strips(halo_gets(near_ref), samples, lane_parts((levels, LANES)))
    for i in range(ITERS):
        hy_ref[i] = lines[i]
        for k in range(3):
            hw_ref[i, k] = weights[i][k]
        for k, v in enumerate(all_weights([near_ref[i, samples + k] for k in range(3)], sign)):
            wh_ref[i, k] = v

    def get_w(r):
        ref, i = (wh_ref, r) if r < ITERS else (w_ref, r - ITERS)
        return [ref[i, k] for k in range(4)]

    def sample(s, carry):
        source = lambda r: near_ref[r, s] if r < ITERS else y_ref[r - ITERS, s]
        for step in range(ITERS):
            target = (p_ref, q_ref)[step % 2]

            def put(r, v, target=target, step=step):
                if step == ITERS - 1:
                    x_ref[r - ITERS, s] = v
                    return
                target[r, s] = v
                kept = r - (high - 3 - step)
                if kept >= 0:
                    keep_ref[step, kept, s] = v

            stencil(source, get_w, step + 1, high - 1 - step, put)
            source = functools.partial(lambda r, target: target[r, s], target=target)
        return carry

    lax.fori_loop(0, samples, sample, 0)


def far_kernel(y_ref, w_ref, keep_ref, head_ref, tail_ref, x_ref, hy_ref, hw_ref, wh_ref, yh_ref):
    rows, samples, levels, cols = y_ref.shape
    high = rows + ITERS
    tiles = cols // LANES
    _, sign = row_order(rows)

    def tile(i, g, c):
        return head_ref[2 + g * tiles + c] if i == 0 else tail_ref[i - 1, g, :, pl.ds(c * LANES, LANES)]

    for i in range(ITERS):
        for c in range(tiles):
            lanes = pl.ds(c * LANES, LANES)
            for k, v in enumerate(all_weights([tile(i, samples + k, c) for k in range(3)], sign)):
                wh_ref[i, k, :, lanes] = v
    for c in range(tiles):
        for s in range(samples):
            yh_ref[s, :, pl.ds(c * LANES, LANES)] = tile(0, s, c)
    gets = [lambda g, side, i=i: tile(i, g, side * (tiles - 1)) for i in range(ITERS)]
    lines, weights = strips(gets, samples, lane_parts((levels, LANES)))
    for i in range(ITERS):
        hy_ref[i] = lines[i]
        for k in range(3):
            hw_ref[i, k] = weights[i][k]

    def get_w(r):
        ref, i = (wh_ref, r - high) if r >= high else (w_ref, r - ITERS)
        return [ref[i, k] for k in range(4)]

    for s in range(samples):

        def source(r, s=s):
            if r < high:
                return y_ref[r - ITERS, s]
            return yh_ref[s] if r == high else tail_ref[r - high - 1, s]

        for step in range(ITERS):
            new = {}
            stencil(source, get_w, high - 1 - step, high - 1 - step + ITERS, new.__setitem__)
            if step < ITERS - 1:
                new[high - 3 - step], new[high - 2 - step] = keep_ref[step, 0, s], keep_ref[step, 1, s]
            source = new.__getitem__
        for r, v in new.items():
            x_ref[r - rows, s] = v


def finish_kernel(
    x_ref, xf_ref, w_ref, sy_ref, sw_ref, hy_ref, hw_ref, fy_ref, fw_ref, left_ref, right_ref, out_ref, var_ref, sum_ref,
    line_ref,
):
    rows, samples, levels, cols = x_ref.shape
    high = rows + 2 * ITERS
    parts = lane_parts((levels, LANES))
    lane, _, l32 = parts
    from_left, from_right = l32 < 4, l32 >= 28
    _, sign = row_order(rows)

    def strip_at(r):
        if r < ITERS:
            return hy_ref[r], [hw_ref[r, k] for k in range(3)]
        if r < ITERS + rows:
            return sy_ref[r - ITERS], [sw_ref[r - ITERS, k] for k in range(3)]
        return fy_ref[r - ITERS - rows], [fw_ref[r - ITERS - rows, k] for k in range(3)]

    tiles = high // BATCH
    group = 2 if tiles % 2 == 0 else 1

    def turn(first):
        return [(turns(left_ref[q]), turns(right_ref[q])) for q in range(first, min(first + group, tiles))]

    ahead = turn(0)
    for first in range(0, tiles, group):
        here, ahead = ahead, turn(first + group)
        sides = [(unpack(a, parts, False), unpack(b, parts, True)) for a, b in here]
        for i, (lefts, rights) in enumerate(sides):
            for j in range(BATCH):
                r = (first + i) * BATCH + j
                y, w = strip_at(r)
                values = [
                    jnp.where(from_left, a, jnp.where(from_right, b, v))
                    for a, b, v in zip(lefts[j], rights[j], [y, *w])
                ]
                for k, v in enumerate([values[0], *all_weights(values[1:], sign)]):
                    line_ref[r, k] = v

    def get_w(r):
        return [line_ref[r, 1 + k] for k in range(4)]

    field = {r: line_ref[r, 0] for r in range(high)}
    for step in range(ITERS):
        new = {}
        stencil(field.__getitem__, get_w, step + 1, high - 1 - step, new.__setitem__)
        field = new

    total, count = None, None
    for r in range(rows):
        strip = field[ITERS + r]
        for c in range(0, cols, LANES):
            lanes = pl.ds(c, LANES)
            square = None
            for s in range(samples):
                v = x_ref[r, s, :, lanes] if r < rows - ITERS else xf_ref[r - rows + ITERS, s, :, lanes]
                if c == 0:
                    v = jnp.where(lane < 4, roll(strip, -(SEG * s + 4)), v)
                if c == cols - LANES:
                    v = jnp.where(lane >= LANES - 4, roll(strip, LANES - SEG * s - 28), v)
                out_ref[r, s, :, lanes] = v
                square = v * v if square is None else square + v * v
            var = square / samples
            var_ref[r, :, lanes] = var
            m = jnp.where(w_ref[r, 1, :, lanes] > 0, 1.0, 0.0)
            total = m * var if total is None else total + m * var
            count = m if count is None else count + m
    total, count = [jnp.sum(v, axis=0, keepdims=True) for v in (total, count)]
    low = lax.broadcasted_iota(jnp.int32, total.shape, 1) < LANES // 2
    sum_ref[...] = jnp.where(low, total + roll(total, LANES // 2), count + roll(count, LANES // 2))


def scale_kernel(x_ref, w_ref, var_ref, all_ref, out_ref, mean_ref, stage, mean_to, sem, mean_sem):
    rows, samples, levels, cols = x_ref.shape
    sums = jnp.sum(all_ref[...], axis=0)
    low = lax.broadcasted_iota(jnp.int32, sums.shape, 1) < LANES // 2
    total, count = [jnp.sum(jnp.where(m, sums, 0.0), axis=1, keepdims=True) for m in (low, ~low)]
    mean = total / count
    mean_to[...] = mean
    copies = [pltpu.make_async_copy(mean_to, mean_ref, mean_sem)]
    copies[0].start()
    row_at, _ = row_order(rows)
    for c in range(cols // LANES):
        lanes = pl.ds(c * LANES, LANES)
        factors = []
        for r in range(rows):
            wet = w_ref[r, 1, :, lanes] > 0
            safe = jnp.where(wet, var_ref[r, :, lanes], 1.0)
            factors.append(jnp.where(wet, jnp.sqrt(mean / (safe + 1e-06)), 0.0))
        for s in range(samples):
            for r in range(rows):
                stage[c, s, pl.ds(row_at(r), levels, stride=rows)] = x_ref[r, s, :, lanes] * factors[r]
            copies.append(pltpu.make_async_copy(stage.at[c, s], out_ref.at[s, :, lanes], sem.at[c, s]))
            copies[-1].start()
    for copy in copies:
        copy.wait()


def call(kernel, out, *args, scratch=(), flops=0, in_space=None, out_space=None):
    out = [o if isinstance(o, jax.ShapeDtypeStruct) else jax.ShapeDtypeStruct(o, F32) for o in out]
    scratch = [pltpu.VMEM(o, F32) if isinstance(o, tuple) else o for o in scratch]
    return pl.pallas_call(
        kernel,
        out_shape=out,
        in_specs=[pl.BlockSpec(memory_space=in_space or pltpu.VMEM)] * len(args),
        out_specs=[pl.BlockSpec(memory_space=m) for m in out_space or [pltpu.VMEM] * len(out)],
        scratch_shapes=scratch,
        cost_estimate=pl.CostEstimate(flops=flops, bytes_accessed=sum(a.size * 4 for a in args), transcendentals=0),
        compiler_params=pltpu.CompilerParams(vmem_limit_bytes=12 << 20),
    )(*args)


def shards(noise, diff_lat, diff_lon, shear, sea_mask):
    samples, levels, rows, cols = noise.shape
    high = rows + 2 * ITERS
    flat = [noise.reshape(samples, levels * rows, cols)] + [
        a.reshape(levels * rows, cols) for a in (diff_lat, diff_lon, shear, sea_mask)
    ]
    n_lat, n_lon = lax.axis_size("lat"), lax.axis_size("lon")
    pair = [(i, i ^ 1) for i in range(n_lat)]
    across = [(i, i - 1 if i % 2 == 0 else i + 1) for i in range(1, n_lat - 1)]
    east = [(i, (i + 1) % n_lon) for i in range(n_lon)]
    west = [(j, i) for i, j in east]

    halo = (ITERS, samples + 3, levels, cols)
    tiles = cols // LANES
    plane = (tiles, levels * rows, LANES)
    flat = [pltpu.with_memory_space_constraint(a, pltpu.HBM) for a in flat]
    head = (2 + (samples + 3) * tiles, levels, LANES)
    to_near, to_far, to_far_tail, *staged = call(
        edge_kernel,
        [halo, head, (ITERS - 1, *halo[1:]), (tiles, samples, levels * rows, LANES)] + [plane] * 3 + [jax.ShapeDtypeStruct(plane, sea_mask.dtype)],
        *flat,
        scratch=[pltpu.SemaphoreType.DMA((tiles, 5))],
        in_space=pltpu.HBM,
    )
    near = lax.ppermute(to_near, "lat", pair)
    far = lax.ppermute(to_far, "lat", across)
    far_tail = lax.ppermute(to_far_tail, "lat", across)
    flat_plane = plane[1:]
    (own_msg,) = call(
        message_kernel,
        [(2, rows // BATCH, levels, LANES)],
        *staged,
        scratch=[(samples, *flat_plane)] + [flat_plane] * 3 + [pltpu.VMEM(flat_plane, sea_mask.dtype)],
        flops=10**6,
    )
    message = (high // BATCH, levels, LANES)
    to_east, to_west = call(join_kernel, [message, message], own_msg, near, far)
    left = lax.ppermute(to_east, "lon", east)
    right = lax.ppermute(to_west, "lon", west)
    strip = (rows, levels, LANES)
    y, w, sy, sw = call(
        own_kernel,
        [(rows, samples, levels, cols), (rows, 4, levels, cols), strip, (rows, 3, levels, LANES)],
        *staged,
        flops=10**6,
    )
    buffer = (rows + ITERS, samples, levels, cols)
    side = [(ITERS, levels, LANES), (ITERS, 3, levels, LANES)]
    x, keep, hy, hw = call(
        near_kernel,
        [y.shape, (ITERS - 1, 2, samples, levels, cols), *side],
        y,
        w,
        near,
        scratch=[(ITERS, 4, levels, cols), buffer, buffer],
        flops=10**7,
    )
    x_far, fy, fw = call(
        far_kernel,
        [(ITERS, samples, levels, cols), *side],
        y,
        w,
        keep,
        far,
        far_tail,
        scratch=[(ITERS, 4, levels, cols), (samples, levels, cols)],
        flops=10**6,
    )
    x, var, part = call(
        finish_kernel,
        [y.shape, (rows, levels, cols), (1, LANES)],
        x,
        x_far,
        w,
        sy,
        sw,
        hy,
        hw,
        fy,
        fw,
        left,
        right,
        scratch=[(high, 5, levels, LANES)],
    )
    spread = jnp.broadcast_to(part, (n_lat * n_lon, 1, LANES))
    every = lax.all_to_all(spread, ("lat", "lon"), 0, 0, tiled=True)
    out, mean = call(
        scale_kernel,
        [(samples, levels * rows, cols), (1, 1)],
        x,
        w,
        var,
        every,
        scratch=[
            (tiles, samples, levels * rows, LANES),
            (1, 1),
            pltpu.SemaphoreType.DMA((tiles, samples)),
            pltpu.SemaphoreType.DMA,
        ],
        out_space=[pl.ANY, pl.ANY],
    )
    return out.reshape(noise.shape), mean.reshape(())


def solution(mesh):
    grid = P(None, "lat", "lon")
    field = P(None, None, "lat", "lon")
    return jax.shard_map(
        shards,
        mesh=mesh,
        in_specs=(field, grid, grid, grid, grid),
        out_specs=(field, P()),
        check_vma=False,
    )
```

```python
import functools

import jax
import jax.numpy as jnp
from jax import lax
from jax.experimental import pallas as pl
from jax.experimental.pallas import tpu as pltpu
from jax.sharding import PartitionSpec as P

ITERS = 4
LANES = 128
SEG = 32
F32 = jnp.float32


def cell_weights(k11, k22, shear, mask):
    m = mask.astype(F32)
    return m * k11, m * k22, m * (0.5 * (shear * jnp.sqrt(k11 * k22)))


def centre_weight(wa, wb):
    return jnp.where(wa > 0, 1.0, 0.0) - 2.0 * (wa + wb)


def all_weights(w, sign):
    return centre_weight(w[0], w[1]), w[0], w[1], sign * w[2]


def roll(x, shift):
    n = x.shape[-1]
    shift = shift % n
    return x if shift == 0 else pltpu.roll(x, shift, x.ndim - 1)


def lane_parts(shape):
    lane = lax.broadcasted_iota(jnp.int32, shape, 1)
    return lane, lane // SEG, lane % SEG


def stencil(get_y, get_w, first, last, put):
    def products(r):
        y = get_y(r)
        w0, wa, wb, wc = get_w(r)
        return w0 * y, wa * y, wb * y, wc * y

    prev, here = products(first - 1), products(first)
    for r in range(first, last):
        after = products(r + 1)
        d, _, b, _ = here
        g = prev[3] - after[3]
        put(r, d + (prev[1] + after[1]) + roll(b + g, 1) + roll(b - g, -1))
        prev, here = here, after


def row_order(rows):
    odd = lax.rem(lax.axis_index("lat"), 2)
    step = 2 * odd - 1
    return lambda d: (1 - odd) * (rows - 1) + step * d, step.astype(F32)


def edge_kernel(n_ref, a_ref, b_ref, s_ref, m_ref, near_ref, head_ref, tail_ref, n_to, a_to, b_to, s_to, m_to, sem):
    samples, levels, tiles = n_ref.shape[0], near_ref.shape[2], n_to.shape[0]
    rows = n_ref.shape[1] // levels
    copies = []
    for c in range(tiles):
        lanes = pl.ds(c * LANES, LANES)
        for k, (ref, to) in enumerate(((a_ref, a_to), (b_ref, b_to), (s_ref, s_to), (m_ref, m_to))):
            copies.append(pltpu.make_async_copy(ref.at[:, lanes], to.at[c], sem.at[c, k]))
    for c in range(tiles):
        lanes = pl.ds(c * LANES, LANES)
        copies.append(pltpu.make_async_copy(n_ref.at[:, :, lanes], n_to.at[c], sem.at[c, 4]))
    for copy in copies:
        copy.start()
    row_at, _ = row_order(rows)
    parts = lane_parts((levels, LANES))

    def put(i, far, g, c, v):
        if not far:
            near_ref[i, g, :, pl.ds(c * LANES, LANES)] = v
        elif i == 0:
            head_ref[2 + g * tiles + c] = v
        else:
            tail_ref[i - 1, g, :, pl.ds(c * LANES, LANES)] = v

    blocks = [(i, far, row_at(rows - 1 - i if far else ITERS - 1 - i)) for i in range(ITERS) for far in (False, True)]
    data = {}
    for copy in copies[: 4 * tiles]:
        copy.wait()
    for i, far, r in blocks:
        at = pl.ds(r, levels, stride=rows)
        for c in range(tiles):
            for k, v in enumerate(cell_weights(a_to[c, at], b_to[c, at], s_to[c, at], m_to[c, at])):
                put(i, far, samples + k, c, v)
                data[i, far, samples + k, c] = v
    for copy in copies[4 * tiles :]:
        copy.wait()
    for i, far, r in blocks:
        for c in range(tiles):
            for s in range(samples):
                v = n_to[c, s, pl.ds(r, levels, stride=rows)]
                put(i, far, s, c, v)
                data[i, far, s, c] = v
    edges = [
        both_edges(lambda g, side: data[i, True, g, side * (tiles - 1)], samples + 3, parts) for i in range(ITERS)
    ]
    head_ref[0], head_ref[1] = messages(edges, parts)


BATCH = 4


def replicate(values, seg):
    turned = [roll(v, SEG) for v in values]
    values = [jnp.where(seg == 1, t, v) for t, v in zip(turned, values)]
    turned = [roll(v, 2 * SEG) for v in values]
    return [jnp.where(seg >= 2, t, v) for t, v in zip(turned, values)]


def line_up(gets, samples, parts, low, high):
    _, seg, l32 = parts
    turned = [
        [(roll(get(s, low), SEG * s + 4), roll(get(s, high), SEG * s + 28)) for s in range(samples)] for get in gets
    ]
    lines = []
    for row in turned:
        line = None
        for s, (a, b) in enumerate(row):
            v = jnp.where(l32 < SEG // 2, a, b)
            line = v if line is None else jnp.where(seg == s, v, line)
        lines.append(line)
    return lines


def both_edges(get, groups, parts):
    return [jnp.where(parts[0] < LANES // 2, get(g, 0), get(g, 1)) for g in range(groups)]


def by_segment(values, seg, first):
    line = values[0]
    for i, v in enumerate(values[1:]):
        line = jnp.where(seg == first + 1 + i, v, line)
    return line


def messages(both, parts):
    _, seg, l32 = parts
    samples = len(both[0]) - 3
    slot = l32 // 4
    east = west = None
    for j, row in enumerate(both):
        line = by_segment([roll(row[s], SEG * s + 4 * j + 4) for s in range(samples)], seg, 0)
        turned = [roll(row[samples + k], SEG * k + 4 * j + 20) for k in range(3)]
        weights = by_segment(turned, seg, 0)
        east = line if east is None else jnp.where(slot == j, line, east)
        west = line if west is None else jnp.where(slot == j + 1, line, west)
        east = jnp.where(slot == 4 + j, weights, east)
        if j < BATCH - 1:
            west = jnp.where(slot == 5 + j, weights, west)
        else:
            west = jnp.where(slot == 0, by_segment(turned, seg, 1), west)
    return east, west


def turns(tile):
    return [roll(tile, SEG * q) for q in range(4)]


def unpack(turned, parts, from_east):
    _, seg, _ = parts
    tile = turned[0]
    every = [by_segment([turned[(q - k) % 4] for q in range(4)], seg, 0) for k in range(4 if from_east else 3)]
    rows = []
    for j in range(BATCH):
        if not from_east:
            rows.append([roll(tile, -4 * j)] + [roll(every[k], -16 - 4 * j) for k in range(3)])
        elif j < BATCH - 1:
            rows.append([roll(tile, 24 - 4 * j)] + [roll(every[k], 8 - 4 * j) for k in range(3)])
        else:
            rows.append([roll(tile, 24 - 4 * j)] + [roll(every[k + 1], 28) for k in range(3)])
    return rows


def strips(gets, samples, parts):
    _, seg, l32 = parts
    lines = line_up(gets, samples, parts, 0, 1)
    turned = [(roll(get(samples + k, 0), 4), roll(get(samples + k, 1), 28)) for get in gets for k in range(3)]
    weights = replicate([jnp.where(l32 < SEG // 2, a, b) for a, b in turned], seg)
    return lines, [weights[3 * i : 3 * i + 3] for i in range(len(gets))]


def own_row(refs, r, rows, levels):
    n_ref, a_ref, b_ref, s_ref, m_ref = refs
    at = pl.ds(row_order(rows)[0](r), levels, stride=rows)
    return [
        [n_ref[c, s, at] for s in range(n_ref.shape[1])]
        + list(cell_weights(a_ref[c, at], b_ref[c, at], s_ref[c, at], m_ref[c, at]))
        for c in range(n_ref.shape[0])
    ]


def own_gets(data):
    return [lambda g, side, row=row: row[-side][g] for row in data]


def message_kernel(n_ref, a_ref, b_ref, s_ref, m_ref, msg_ref, n_to, a_to, b_to, s_to, m_to):
    levels = msg_ref.shape[2]
    rows, samples, last = n_ref.shape[2] // levels, n_ref.shape[1], n_ref.shape[0] - 1
    parts = lane_parts((levels, LANES))
    left = lax.broadcasted_iota(jnp.int32, a_to.shape, 1) < LANES // 2
    for ref, to in ((a_ref, a_to), (b_ref, b_to), (s_ref, s_to), (m_ref, m_to)):
        to[...] = jnp.where(left, ref[0], ref[last])
    for s in range(samples):
        n_to[s] = jnp.where(left, n_ref[0, s], n_ref[last, s])
    row_at, _ = row_order(rows)
    for first in range(0, rows, BATCH):
        both = []
        for d in range(first, first + BATCH):
            at = pl.ds(row_at(d), levels, stride=rows)
            both.append([n_to[s, at] for s in range(samples)] + list(cell_weights(a_to[at], b_to[at], s_to[at], m_to[at])))
        msg_ref[0, first // BATCH], msg_ref[1, first // BATCH] = messages(both, parts)


def own_kernel(n_ref, a_ref, b_ref, s_ref, m_ref, y_ref, w_ref, sy_ref, sw_ref):
    rows, samples, levels, _ = y_ref.shape
    parts = lane_parts((levels, LANES))
    _, sign = row_order(rows)
    for first in range(0, rows, BATCH):
        batch = range(first, first + BATCH)
        data = [own_row((n_ref, a_ref, b_ref, s_ref, m_ref), r, rows, levels) for r in batch]
        lines, weights = strips(own_gets(data), samples, parts)
        for i, r in enumerate(batch):
            for c, values in enumerate(data[i]):
                lanes = pl.ds(c * LANES, LANES)
                for s in range(samples):
                    y_ref[r, s, :, lanes] = values[s]
                for k, v in enumerate(all_weights(values[samples:], sign)):
                    w_ref[r, k, :, lanes] = v
            sy_ref[r] = lines[i]
            for k in range(3):
                sw_ref[r, k] = weights[i][k]


def halo_gets(ref):
    last = ref.shape[3] - LANES
    return [lambda g, side, i=i: ref[i, g, :, pl.ds(side * last, LANES)] for i in range(ITERS)]


def join_kernel(own_ref, near_ref, head_ref, east_ref, west_ref):
    tiles = own_ref.shape[1]
    parts = lane_parts(own_ref.shape[2:])
    sent = messages([both_edges(get, near_ref.shape[1], parts) for get in halo_gets(near_ref)], parts)
    for d, ref in enumerate((east_ref, west_ref)):
        ref[0] = sent[d]
        ref[1 : 1 + tiles] = own_ref[d]
        ref[1 + tiles] = head_ref[d]


def near_kernel(y_ref, w_ref, near_ref, x_ref, keep_ref, hy_ref, hw_ref, wh_ref, p_ref, q_ref):
    rows, samples, levels, _ = y_ref.shape
    high = rows + ITERS
    _, sign = row_order(rows)
    lines, weights = strips(halo_gets(near_ref), samples, lane_parts((levels, LANES)))
    for i in range(ITERS):
        hy_ref[i] = lines[i]
        for k in range(3):
            hw_ref[i, k] = weights[i][k]
        for k, v in enumerate(all_weights([near_ref[i, samples + k] for k in range(3)], sign)):
            wh_ref[i, k] = v

    def get_w(r):
        ref, i = (wh_ref, r) if r < ITERS else (w_ref, r - ITERS)
        return [ref[i, k] for k in range(4)]

    def sample(s, carry):
        source = lambda r: near_ref[r, s] if r < ITERS else y_ref[r - ITERS, s]
        for step in range(ITERS):
            target = (p_ref, q_ref)[step % 2]

            def put(r, v, target=target, step=step):
                if step == ITERS - 1:
                    x_ref[r - ITERS, s] = v
                    return
                target[r, s] = v
                kept = r - (high - 3 - step)
                if kept >= 0:
                    keep_ref[step, kept, s] = v

            stencil(source, get_w, step + 1, high - 1 - step, put)
            source = functools.partial(lambda r, target: target[r, s], target=target)
        return carry

    lax.fori_loop(0, samples, sample, 0)


def far_kernel(y_ref, w_ref, keep_ref, head_ref, tail_ref, x_ref, hy_ref, hw_ref, wh_ref, yh_ref):
    rows, samples, levels, cols = y_ref.shape
    high = rows + ITERS
    tiles = cols // LANES
    _, sign = row_order(rows)

    def tile(i, g, c):
        return head_ref[2 + g * tiles + c] if i == 0 else tail_ref[i - 1, g, :, pl.ds(c * LANES, LANES)]

    for i in range(ITERS):
        for c in range(tiles):
            lanes = pl.ds(c * LANES, LANES)
            for k, v in enumerate(all_weights([tile(i, samples + k, c) for k in range(3)], sign)):
                wh_ref[i, k, :, lanes] = v
    for c in range(tiles):
        for s in range(samples):
            yh_ref[s, :, pl.ds(c * LANES, LANES)] = tile(0, s, c)
    gets = [lambda g, side, i=i: tile(i, g, side * (tiles - 1)) for i in range(ITERS)]
    lines, weights = strips(gets, samples, lane_parts((levels, LANES)))
    for i in range(ITERS):
        hy_ref[i] = lines[i]
        for k in range(3):
            hw_ref[i, k] = weights[i][k]

    def get_w(r):
        ref, i = (wh_ref, r - high) if r >= high else (w_ref, r - ITERS)
        return [ref[i, k] for k in range(4)]

    def first(s):
        def source(r):
            if r < high:
                return y_ref[r - ITERS, s]
            return yh_ref[s] if r == high else tail_ref[r - high - 1, s]

        return source

    sources = [first(s) for s in range(samples)]
    for step in range(ITERS):
        for s in range(samples):
            new = {}
            stencil(sources[s], get_w, high - 1 - step, high - 1 - step + ITERS, new.__setitem__)
            if step < ITERS - 1:
                new[high - 3 - step], new[high - 2 - step] = keep_ref[step, 0, s], keep_ref[step, 1, s]
                sources[s] = new.__getitem__
            else:
                for r, v in new.items():
                    x_ref[r - rows, s] = v


def finish_kernel(
    x_ref, xf_ref, w_ref, sy_ref, sw_ref, hy_ref, hw_ref, fy_ref, fw_ref, left_ref, right_ref, out_ref, var_ref, sum_ref,
    line_ref,
):
    rows, samples, levels, cols = x_ref.shape
    high = rows + 2 * ITERS
    parts = lane_parts((levels, LANES))
    lane, _, l32 = parts
    from_left, from_right = l32 < 4, l32 >= 28
    _, sign = row_order(rows)

    def strip_at(r):
        if r < ITERS:
            return hy_ref[r], [hw_ref[r, k] for k in range(3)]
        if r < ITERS + rows:
            return sy_ref[r - ITERS], [sw_ref[r - ITERS, k] for k in range(3)]
        return fy_ref[r - ITERS - rows], [fw_ref[r - ITERS - rows, k] for k in range(3)]

    tiles = high // BATCH
    group = 3 if tiles % 3 == 0 else 1

    def turn(first):
        return [(turns(left_ref[q]), turns(right_ref[q])) for q in range(first, min(first + group, tiles))]

    ahead = turn(0)
    for first in range(0, tiles, group):
        here, ahead = ahead, turn(first + group)
        sides = [(unpack(a, parts, False), unpack(b, parts, True)) for a, b in here]
        for i, (lefts, rights) in enumerate(sides):
            for j in range(BATCH):
                r = (first + i) * BATCH + j
                y, w = strip_at(r)
                values = [
                    jnp.where(from_left, a, jnp.where(from_right, b, v))
                    for a, b, v in zip(lefts[j], rights[j], [y, *w])
                ]
                for k, v in enumerate([values[0], *all_weights(values[1:], sign)]):
                    line_ref[r, k] = v

    def get_w(r):
        return [line_ref[r, 1 + k] for k in range(4)]

    field = {r: line_ref[r, 0] for r in range(high)}
    for step in range(ITERS):
        new = {}
        stencil(field.__getitem__, get_w, step + 1, high - 1 - step, new.__setitem__)
        field = new

    total, count = None, None
    for r in range(rows):
        strip = field[ITERS + r]
        for c in range(0, cols, LANES):
            lanes = pl.ds(c, LANES)
            square = None
            for s in range(samples):
                v = x_ref[r, s, :, lanes] if r < rows - ITERS else xf_ref[r - rows + ITERS, s, :, lanes]
                if c == 0:
                    v = jnp.where(lane < 4, roll(strip, -(SEG * s + 4)), v)
                if c == cols - LANES:
                    v = jnp.where(lane >= LANES - 4, roll(strip, LANES - SEG * s - 28), v)
                out_ref[r, s, :, lanes] = v
                square = v * v if square is None else square + v * v
            var = square / samples
            var_ref[r, :, lanes] = var
            m = jnp.where(w_ref[r, 1, :, lanes] > 0, 1.0, 0.0)
            total = m * var if total is None else total + m * var
            count = m if count is None else count + m
    total, count = [jnp.sum(v, axis=0, keepdims=True) for v in (total, count)]
    low = lax.broadcasted_iota(jnp.int32, total.shape, 1) < LANES // 2
    sum_ref[...] = jnp.where(low, total + roll(total, LANES // 2), count + roll(count, LANES // 2))


def scale_kernel(x_ref, w_ref, var_ref, all_ref, out_ref, mean_ref, stage, mean_to, sem, mean_sem):
    rows, samples, levels, cols = x_ref.shape
    sums = jnp.sum(all_ref[...], axis=0)
    low = lax.broadcasted_iota(jnp.int32, sums.shape, 1) < LANES // 2
    total, count = [jnp.sum(jnp.where(m, sums, 0.0), axis=1, keepdims=True) for m in (low, ~low)]
    mean = total / count
    mean_to[...] = mean
    copies = [pltpu.make_async_copy(mean_to, mean_ref, mean_sem)]
    copies[0].start()
    row_at, _ = row_order(rows)
    for c in range(cols // LANES):
        lanes = pl.ds(c * LANES, LANES)
        factors = []
        for r in range(rows):
            wet = w_ref[r, 1, :, lanes] > 0
            safe = jnp.where(wet, var_ref[r, :, lanes], 1.0)
            factors.append(jnp.where(wet, jnp.sqrt(mean / (safe + 1e-06)), 0.0))
        for s in range(samples):
            for r in range(rows):
                stage[c, s, pl.ds(row_at(r), levels, stride=rows)] = x_ref[r, s, :, lanes] * factors[r]
            copies.append(pltpu.make_async_copy(stage.at[c, s], out_ref.at[s, :, lanes], sem.at[c, s]))
            copies[-1].start()
    for copy in copies:
        copy.wait()


def call(kernel, out, *args, scratch=(), flops=0, in_space=None, out_space=None):
    out = [o if isinstance(o, jax.ShapeDtypeStruct) else jax.ShapeDtypeStruct(o, F32) for o in out]
    scratch = [pltpu.VMEM(o, F32) if isinstance(o, tuple) else o for o in scratch]
    return pl.pallas_call(
        kernel,
        out_shape=out,
        in_specs=[pl.BlockSpec(memory_space=in_space or pltpu.VMEM)] * len(args),
        out_specs=[pl.BlockSpec(memory_space=m) for m in out_space or [pltpu.VMEM] * len(out)],
        scratch_shapes=scratch,
        cost_estimate=pl.CostEstimate(flops=flops, bytes_accessed=sum(a.size * 4 for a in args), transcendentals=0),
        compiler_params=pltpu.CompilerParams(vmem_limit_bytes=12 << 20),
    )(*args)


def shards(noise, diff_lat, diff_lon, shear, sea_mask):
    samples, levels, rows, cols = noise.shape
    high = rows + 2 * ITERS
    flat = [noise.reshape(samples, levels * rows, cols)] + [
        a.reshape(levels * rows, cols) for a in (diff_lat, diff_lon, shear, sea_mask)
    ]
    n_lat, n_lon = lax.axis_size("lat"), lax.axis_size("lon")
    pair = [(i, i ^ 1) for i in range(n_lat)]
    across = [(i, i - 1 if i % 2 == 0 else i + 1) for i in range(1, n_lat - 1)]
    east = [(i, (i + 1) % n_lon) for i in range(n_lon)]
    west = [(j, i) for i, j in east]

    halo = (ITERS, samples + 3, levels, cols)
    tiles = cols // LANES
    plane = (tiles, levels * rows, LANES)
    flat = [pltpu.with_memory_space_constraint(a, pltpu.HBM) for a in flat]
    head = (2 + (samples + 3) * tiles, levels, LANES)
    to_near, to_far, to_far_tail, *staged = call(
        edge_kernel,
        [halo, head, (ITERS - 1, *halo[1:]), (tiles, samples, levels * rows, LANES)] + [plane] * 3 + [jax.ShapeDtypeStruct(plane, sea_mask.dtype)],
        *flat,
        scratch=[pltpu.SemaphoreType.DMA((tiles, 5))],
        in_space=pltpu.HBM,
    )
    near = lax.ppermute(to_near, "lat", pair)
    far = lax.ppermute(to_far, "lat", across)
    far_tail = lax.ppermute(to_far_tail, "lat", across)
    flat_plane = plane[1:]
    (own_msg,) = call(
        message_kernel,
        [(2, rows // BATCH, levels, LANES)],
        *staged,
        scratch=[(samples, *flat_plane)] + [flat_plane] * 3 + [pltpu.VMEM(flat_plane, sea_mask.dtype)],
        flops=10**6,
    )
    message = (high // BATCH, levels, LANES)
    to_east, to_west = call(join_kernel, [message, message], own_msg, near, far)
    left = lax.ppermute(to_east, "lon", east)
    right = lax.ppermute(to_west, "lon", west)
    strip = (rows, levels, LANES)
    y, w, sy, sw = call(
        own_kernel,
        [(rows, samples, levels, cols), (rows, 4, levels, cols), strip, (rows, 3, levels, LANES)],
        *staged,
        flops=10**6,
    )
    buffer = (rows + ITERS, samples, levels, cols)
    side = [(ITERS, levels, LANES), (ITERS, 3, levels, LANES)]
    x, keep, hy, hw = call(
        near_kernel,
        [y.shape, (ITERS - 1, 2, samples, levels, cols), *side],
        y,
        w,
        near,
        scratch=[(ITERS, 4, levels, cols), buffer, buffer],
        flops=10**7,
    )
    x_far, fy, fw = call(
        far_kernel,
        [(ITERS, samples, levels, cols), *side],
        y,
        w,
        keep,
        far,
        far_tail,
        scratch=[(ITERS, 4, levels, cols), (samples, levels, cols)],
        flops=10**6,
    )
    x, var, part = call(
        finish_kernel,
        [y.shape, (rows, levels, cols), (1, LANES)],
        x,
        x_far,
        w,
        sy,
        sw,
        hy,
        hw,
        fy,
        fw,
        left,
        right,
        scratch=[(high, 5, levels, LANES)],
    )
    spread = jnp.broadcast_to(part, (n_lat * n_lon, 1, LANES))
    every = lax.all_to_all(spread, ("lat", "lon"), 0, 0, tiled=True)
    out, mean = call(
        scale_kernel,
        [(samples, levels * rows, cols), (1, 1)],
        x,
        w,
        var,
        every,
        scratch=[
            (tiles, samples, levels * rows, LANES),
            (1, 1),
            pltpu.SemaphoreType.DMA((tiles, samples)),
            pltpu.SemaphoreType.DMA,
        ],
        out_space=[pl.ANY, pl.ANY],
    )
    return out.reshape(noise.shape), mean.reshape(())


def solution(mesh):
    grid = P(None, "lat", "lon")
    field = P(None, None, "lat", "lon")
    return jax.shard_map(
        shards,
        mesh=mesh,
        in_specs=(field, grid, grid, grid, grid),
        out_specs=(field, P()),
        check_vma=False,
    )
```
